32 devices in a mesh: req: 4 (over z), row: 4 (over y, core), col: 2 (over x).
Axes of the slice: x: 2, y: 2, z: 4, core: 2. Of those that a mesh axis runs over, the one named last changes fastest.
Arguments:
- hidden: bfloat16 [1024, 2048], P(('req', 'row')), may hold values from -6 to 6
- latent_cache: bfloat16 [16, 384, 576], P('req'), may hold values from -144 to 144
- lengths: int32 [16], P('req'), may hold values from 96 to 384
- parents: int32 [16, 64], P('req'), may hold values from -1 to 62, as said below
- routes: int32 [1024, 6], P(('req', 'row')), may hold values from 0 to 15, all different within a row; in each aligned block of 64 rows (0 to 63, 64 to 127, ...) at most 48 rows name the same one
- accepted: int32 [16], P(('req', 'row')), may hold values from 0 to 63
- input_gain: float32 [2048], replicated, may hold values from 0.25 to 1.75
- query_weight: bfloat16 [2048, 3072], P(None, ('row', 'col')), may hold values from -0.125 to 0.125
- latent_weight: bfloat16 [2048, 576], replicated, may hold values from -0.125 to 0.125
- latent_gain: float32 [512], replicated, may hold values from 0.25 to 1.75
- key_absorb: bfloat16 [16, 128, 512], P(('row', 'col')), may hold values from -0.5 to 0.5
- value_absorb: bfloat16 [16, 512, 128], P(('row', 'col')), may hold values from -0.25 to 0.25
- output_weight: bfloat16 [2048, 2048], P(('row', 'col')), may hold values from -0.125 to 0.125
- post_gain: float32 [2048], replicated, may hold values from 0.25 to 1.75
- router_weight: bfloat16 [2048, 16], replicated, may hold values from -0.046875 to 0.046875
- shared_gate_up: bfloat16 [2, 2048, 2816], P(None, None, ('row', 'col')), may hold values from -0.125 to 0.125
- shared_down: bfloat16 [2816, 2048], P(('row', 'col')), may hold values from -0.109375 to 0.109375
- expert_gate_up: bfloat16 [16, 2, 2048, 1408], P(('req', 'row'), None, None, 'col'), may hold values from -0.125 to 0.125
- expert_down: bfloat16 [16, 1408, 2048], P(('req', 'row'), 'col'), may hold values from -1.5 to 1.5
Outputs:
- layer_output: bfloat16 [1024, 2048], P(('req', 'row'))
- accepted_latents: bfloat16 [16, 64, 576], P(('req', 'row'))
The draws below stay inside these ranges and needn't reach their ends.
Inputs may be any that keep to these rules, and one draw needn't show every extreme that they name: parents[r, 0] is -1 and parents[r, i] lies in 0 to i - 1 for i >= 1. `routes`: the 6 experts of a token differ; within the 64 rows of one index of req and row no expert is named by more than 48 rows.
All inputs are finite; a program needn't handle non-finite values.
Results may differ from the reference program's by a relative error of at most 0.009.
The reference program's roundings to bfloat16 on the way count: a program that leaves them out, or rounds other values in their place, can miss the bound.
Values may be sent and summed in bfloat16 or wider, within the bound.
No kernel may reach another device: no remote copies, remote signals or barrier semaphores. Data moves between devices by JAX's collectives and lax.ppermute only.
A program may use at most 128 MiB of HBM per device.

```python
import math
import jax
import jax.numpy as jnp
import numpy as np
from jax import lax

D = 2048
H = 16
NOPE = 128
ROPE = 64
LAT = 512
VDIM = 128
FF = 1408
SFF = 2816
TOP = 6
TREE = 64
CACHE = 384
WINDOW = 160
SINK = 4
REQS = 16
TOKENS = 1024
TOK_DEV = 64
EXPERTS = 16
CAP = 48
N_REQ = 4
N_ROW = 4


def draw_latent_cache(key, part):
    values = jnp.clip(jax.random.normal(key, (REQS, CACHE, LAT + ROPE), jnp.float32), -6.0, 6.0)
    return values.astype(jnp.bfloat16)


def draw_lengths(key, part):
    first_key, second_key = jax.random.split(key)
    values = jax.random.randint(first_key, (REQS,), CACHE // 4, CACHE + 1)
    longest = jax.random.randint(second_key, (), 0, REQS)
    return jnp.where(jnp.arange(REQS) == longest, CACHE, values).astype(jnp.int32)


def draw_parents(key, part):
    backsteps = jax.random.randint(key, (REQS, TREE), 0, 4)
    node_ids = jnp.arange(TREE, dtype=jnp.int32)[None, :]
    request_ids = jnp.arange(REQS, dtype=jnp.int32)[:, None]
    backsteps = jnp.where((node_ids == TREE - 1) & (request_ids == 0), 0, backsteps)
    linked = jnp.maximum(node_ids - 1 - backsteps, 0)
    return jnp.where(node_ids == 0, -1, linked).astype(jnp.int32)


def draw_accepted(key, part):
    first_key, second_key = jax.random.split(key)
    values = jax.random.randint(first_key, (REQS,), 0, TREE)
    chosen = jax.random.randint(second_key, (), 0, REQS)
    return jnp.where(jnp.arange(REQS) == chosen, TREE - 1, values).astype(jnp.int32)


def steps_of(own_key, extent, pieces, least, largest):
    factor_of, own = 1.0, jax.random.fold_in(own_key, 6)
    for position, shards_of in pieces:
        steps = jnp.exp(jax.random.uniform(jax.random.fold_in(own, position), (shards_of,), jnp.float32, least / len(pieces), largest / len(pieces)))
        factor_of = factor_of * jnp.repeat(steps, extent[position] // shards_of).reshape([-1 if axis == position else 1 for axis in range(len(extent))])
    return factor_of


def routed_block(stream_key, own, number, rows, count, top, limit, slope):
    order = jax.random.permutation(stream_key, count)
    heavy_load, usual = load_shares(count, rows * top, limit, slope, True), load_shares(count, rows * top, limit, slope, False)
    places = jnp.arange(count)

    def named(sizes, rotation):
        used = int((sizes > 0).sum())
        fixed = max(1, used // 4)
        moved = fixed + (places - fixed + rotation * (used - fixed)) % max(1, count - fixed)
        return jnp.zeros((count,), jnp.int32).at[order[jnp.where(places < fixed, places, moved)]].set(jnp.asarray(sizes, jnp.int32))

    sizes = jnp.where(number % 4 == 0, named(heavy_load, number // 4), named(usual, number - number // 4 - 1))
    mixed = jax.random.permutation(jax.random.fold_in(own, 3), count)
    giver, taker = mixed[0:count // 2 * 2:2], mixed[1:count // 2 * 2:2]
    margin = jnp.minimum(sizes[giver] - 1, limit - sizes[taker]) // 2
    margin = jnp.where((giver == order[0]) | (taker == order[0]) | (sizes[taker] == 0), 0, jnp.maximum(margin, 0))
    moved = jax.random.randint(jax.random.fold_in(own, 4), (count // 2,), 0, 1 << 20) % (margin + 1)
    sizes = sizes.at[giver].add(-moved).at[taker].add(moved)
    items = jnp.searchsorted(jnp.cumsum(sizes), jnp.arange(rows * top), side="right").astype(jnp.int32)
    table = items.reshape(top, rows).T
    table = table[jax.random.permutation(jax.random.fold_in(own, 1), rows)]
    rotation = jax.random.randint(jax.random.fold_in(own, 2), (rows, 1), 0, top)
    return jnp.take_along_axis(table, (jnp.arange(top)[None, :] + rotation) % top, axis=1)


def load_shares(amount, total, limit, skew, full):
    loads = [(1 << 20) // math.isqrt(rank ** skew) + 1 for rank in range(1, amount + 1)]
    largest = limit if full else min(limit, max(-(-total // amount), total * loads[0] // sum(loads)))
    least = 1 if total - largest >= amount - 1 else 0
    given, surplus = [largest] + [least] * (amount - 1), total - largest - least * (amount - 1)
    while surplus > 0:
        candidates = [i for i in range(1, amount) if given[i] < largest] or [i for i in range(1, amount) if given[i] < limit]
        whole, remaining = sum([loads[i] for i in candidates]), surplus
        for i in candidates:
            more = min(limit - given[i], max(1, remaining * loads[i] // whole), surplus)
            given[i] = given[i] + more
            surplus = surplus - more
    return np.array(given)


def noise(rng, dims, scale, bound, cuts=(), kind=jnp.bfloat16):
    gain = steps_of(rng, dims, cuts, -0.22, 0.18) if cuts else 1.0
    values = jax.random.normal(rng, dims, jnp.float32) * scale * gain
    return jnp.minimum(jnp.maximum(values, -bound), bound).astype(kind)


def setup_inputs(seed: int = 0) -> dict:
    seeds = jax.random.split(jax.random.key(seed), 20)
    hidden = noise(seeds[0], (TOKENS, D), 1.0, 6.0, ((0, 16),))
    latent_cache = draw_latent_cache(jax.random.fold_in(seeds[19], 71), 0)
    lengths = draw_lengths(jax.random.fold_in(seeds[19], 71), 0)
    parents = draw_parents(jax.random.fold_in(seeds[19], 71), 0)
    routes_keys = jax.random.split(jax.random.fold_in(seeds[4], 1), TOKENS // TOK_DEV)
    routes_turns = jax.random.permutation(jax.random.fold_in(seeds[4], 3), TOKENS // TOK_DEV)
    routes = jax.vmap(lambda own, number: routed_block(jax.random.fold_in(seeds[4], 2), own, number, TOK_DEV, EXPERTS, TOP, CAP, 2))(routes_keys, routes_turns).reshape((TOKENS, TOP))
    accepted = draw_accepted(jax.random.fold_in(seeds[19], 71), 0)
    input_gain = jnp.clip(1.0 + 0.15 * jax.random.normal(seeds[6], (D,), jnp.float32), 0.25, 1.75)
    query_weight = noise(seeds[7], (D, H * (NOPE + ROPE)), D ** -0.5, 0.125, ((1, 8),))
    latent_weight = noise(seeds[8], (D, LAT + ROPE), D ** -0.5, 0.125)
    latent_gain = jnp.clip(1.0 + 0.15 * jax.random.normal(seeds[9], (LAT,), jnp.float32), 0.25, 1.75)
    key_absorb = noise(seeds[10], (H, NOPE, LAT), NOPE ** -0.5, 0.5, ((0, 8),))
    value_absorb = noise(seeds[11], (H, LAT, VDIM), LAT ** -0.5, 0.25, ((0, 8),))
    output_weight = noise(seeds[12], (H * VDIM, D), (H * VDIM) ** -0.5, 0.125, ((0, 8),))
    post_gain = jnp.clip(1.0 + 0.15 * jax.random.normal(seeds[13], (D,), jnp.float32), 0.25, 1.75)
    router_weight = noise(seeds[14], (D, EXPERTS), (8 * D) ** -0.5, 0.046875)
    shared_gate_up = noise(seeds[15], (2, D, SFF), D ** -0.5, 0.125, ((2, 8),))
    shared_down = noise(seeds[16], (SFF, D), SFF ** -0.5, 0.109375, ((0, 8),))
    expert_gate_up = noise(seeds[17], (EXPERTS, 2, D, FF), D ** -0.5, 0.125, ((0, 16), (3, 2)))
    expert_down = noise(seeds[18], (EXPERTS, FF, D), (max(1, FF // 100)) ** -0.5, 1.5, ((0, 16), (1, 2)))
    return {"hidden": hidden, "latent_cache": latent_cache, "lengths": lengths, "parents": parents, "routes": routes, "accepted": accepted, "input_gain": input_gain, "query_weight": query_weight, "latent_weight": latent_weight, "latent_gain": latent_gain, "key_absorb": key_absorb, "value_absorb": value_absorb, "output_weight": output_weight, "post_gain": post_gain, "router_weight": router_weight, "shared_gate_up": shared_gate_up, "shared_down": shared_down, "expert_gate_up": expert_gate_up, "expert_down": expert_down}


EPSILON = 1e-06

def rms_scale(values, gain_row):
    mean_square = lax.optimization_barrier(jnp.mean(values * values, axis=-1, keepdims=True))
    return values * lax.rsqrt(mean_square + EPSILON) * gain_row.astype(jnp.float32)

def rope_tables(positions, rope_width):
    half_width = rope_width // 2
    frequency = jnp.exp(jnp.arange(half_width, dtype=jnp.float32) * (-2.0 * math.log(10000.0) / rope_width))
    angles = positions[..., None] * frequency
    return (jnp.cos(angles), jnp.sin(angles))

def rotate(values, cosine, sine_part):
    half_width = values.shape[-1] // 2
    first_half = values[..., :half_width]
    second_half = values[..., half_width:]
    return jnp.concatenate([first_half * cosine - second_half * sine_part, second_half * cosine + first_half * sine_part], axis=-1)

def ancestry(parents):
    tree_size = parents.shape[-1]
    node_ids = jnp.arange(tree_size, dtype=jnp.int32)
    links = (parents[..., :, None] == node_ids[None, :]).astype(jnp.float32)
    closure = links + jnp.eye(tree_size, dtype=jnp.float32)
    for repeat in range(max(1, (tree_size - 1).bit_length())):
        closure = jnp.minimum(jnp.einsum('...ij,...jk->...ik', closure, closure, precision=lax.Precision.HIGHEST), 1.0)
    depths = lax.optimization_barrier(jnp.sum(closure, axis=-1)) - 1.0
    return (closure, depths)

def attend(rows, cache_rows, length, closure, depths, query_weight, latent_weight, latent_gain, key_absorb, value_absorb):
    head_count = key_absorb.shape[0]
    scale_factor = 1.0 / math.sqrt(NOPE + ROPE)
    queries = jnp.dot(rows, query_weight, preferred_element_type=jnp.float32).astype(jnp.bfloat16)
    queries = queries.reshape(TREE, head_count, NOPE + ROPE)
    projected = jnp.dot(rows, latent_weight, preferred_element_type=jnp.float32)
    positions = length.astype(jnp.float32) + depths
    cosine, sine_part = rope_tables(positions, ROPE)
    content = rms_scale(projected[:, :LAT], latent_gain)
    key_rope = rotate(projected[:, LAT:], cosine, sine_part)
    fresh_latents = jnp.concatenate([content, key_rope], axis=-1).astype(jnp.bfloat16)
    query_latent = jnp.einsum('thn,hnl->thl', queries[:, :, :NOPE].astype(jnp.float32), key_absorb.astype(jnp.float32)).astype(jnp.bfloat16)
    query_rope = rotate(queries[:, :, NOPE:].astype(jnp.float32), cosine[:, None, :], sine_part[:, None, :]).astype(jnp.bfloat16)
    query_full = jnp.concatenate([query_latent, query_rope], axis=-1)
    key_rows = jnp.concatenate([cache_rows, fresh_latents], axis=0)
    scores = jnp.einsum('thc,kc->htk', query_full.astype(jnp.float32), key_rows.astype(jnp.float32)) * scale_factor
    cache_spots = jnp.arange(CACHE, dtype=jnp.int32)
    cache_allowed = (cache_spots < length) & ((cache_spots < SINK) | (cache_spots >= length - WINDOW))
    allowed = jnp.concatenate([jnp.broadcast_to(cache_allowed[None, :], (TREE, CACHE)), closure > 0.5], axis=-1)
    scores = jnp.where(allowed[None], scores, -1e+30)
    row_peak = lax.optimization_barrier(jnp.max(scores, axis=-1, keepdims=True))
    weights = jnp.exp(scores - row_peak)
    attention_weights = (weights / lax.optimization_barrier(jnp.sum(weights, axis=-1, keepdims=True))).astype(jnp.bfloat16)
    out_latent = jnp.einsum('htk,kl->thl', attention_weights.astype(jnp.float32), key_rows[:, :LAT].astype(jnp.float32)).astype(jnp.bfloat16)
    head_output = jnp.einsum('thl,hlv->thv', out_latent.astype(jnp.float32), value_absorb.astype(jnp.float32)).astype(jnp.bfloat16)
    return (head_output.reshape(TREE, head_count * VDIM), fresh_latents)

def reference(hidden, latent_cache, lengths, parents, routes, accepted, input_gain, query_weight, latent_weight, latent_gain, key_absorb, value_absorb, output_weight, post_gain, router_weight, shared_gate_up, shared_down, expert_gate_up, expert_down):
    normed = rms_scale(hidden.astype(jnp.float32), input_gain).astype(jnp.bfloat16)
    closure, depths = ancestry(parents)

    def one_request(request):
        rows = lax.dynamic_slice_in_dim(normed, request * TREE, TREE, 0)
        return attend(rows, latent_cache[request], lengths[request], closure[request], depths[request], query_weight, latent_weight, latent_gain, key_absorb, value_absorb)
    head_rows, fresh_latents = lax.map(one_request, jnp.arange(REQS, dtype=jnp.int32))
    head_rows = head_rows.reshape(TOKENS, H * VDIM)
    residual = hidden.astype(jnp.float32) + jnp.dot(head_rows, output_weight, preferred_element_type=jnp.float32)
    post_normed = rms_scale(residual, post_gain).astype(jnp.bfloat16)
    router = jax.nn.softmax(jnp.dot(post_normed, router_weight, preferred_element_type=jnp.float32), axis=-1)
    shared_gate = jnp.dot(post_normed, shared_gate_up[0], preferred_element_type=jnp.float32)
    shared_upper = jnp.dot(post_normed, shared_gate_up[1], preferred_element_type=jnp.float32)
    shared_hidden = (jax.nn.silu(shared_gate) * shared_upper).astype(jnp.bfloat16)
    shared_out = jnp.dot(shared_hidden, shared_down, preferred_element_type=jnp.float32)
    labels = jnp.arange(EXPERTS, dtype=jnp.int32)
    chosen = jnp.any(routes[:, :, None] == labels[None, None, :], axis=1)
    slot_bound = N_REQ * N_ROW * CAP

    def expert_step(running, expert_index):
        column = lax.dynamic_index_in_dim(chosen, expert_index, 1, keepdims=False)
        picked = jnp.nonzero(column, size=slot_bound, fill_value=0)[0].astype(jnp.int32)
        live_slots = jnp.arange(slot_bound, dtype=jnp.int32) < jnp.sum(column.astype(jnp.int32))
        inputs = post_normed[picked]
        weights_pair = expert_gate_up[expert_index]
        expert_gate = jnp.dot(inputs, weights_pair[0], preferred_element_type=jnp.float32)
        expert_upper = jnp.dot(inputs, weights_pair[1], preferred_element_type=jnp.float32)
        expert_hidden = (jax.nn.silu(expert_gate) * expert_upper).astype(jnp.bfloat16)
        result = jnp.dot(expert_hidden, expert_down[expert_index], preferred_element_type=jnp.float32)
        gate_share = jnp.where(live_slots, router[picked, expert_index], 0.0)
        return (running.at[picked].add(gate_share[:, None] * result), None)
    routed, unused = lax.scan(expert_step, jnp.zeros((TOKENS, D), jnp.float32), labels)
    layer_output = (residual + shared_out + routed).astype(jnp.bfloat16)
    chooser = (jnp.arange(TREE, dtype=jnp.int32)[None, :] == accepted[:, None]).astype(jnp.float32)
    path_mask = jnp.einsum('qi,qij->qj', chooser, closure, precision=lax.Precision.HIGHEST)
    levels = jnp.arange(TREE, dtype=jnp.float32)
    placing = path_mask[:, None, :] * (depths[:, None, :] == levels[None, :, None]).astype(jnp.float32)
    accepted_latents = jnp.einsum('qkj,qjc->qkc', placing, fresh_latents.astype(jnp.float32)).astype(jnp.bfloat16)
    return (layer_output, accepted_latents)
```

```python
import functools
import math

import jax
import jax.numpy as jnp
from jax import lax
from jax.sharding import PartitionSpec as P

NOPE = 128
ROPE = 64
LAT = 512
VDIM = 128
CACHE = 384
WINDOW = 160
SINK = 4


EPSILON = 1e-06


def rms_scale(values, gain_row):
    mean_square = jnp.mean(values * values, axis=-1, keepdims=True)
    return values * lax.rsqrt(mean_square + EPSILON) * gain_row


def rope_tables(positions, rope_width):
    half_width = rope_width // 2
    frequency = jnp.exp(
        jnp.arange(half_width, dtype=jnp.float32) * (-2.0 * math.log(10000.0) / rope_width)
    )
    angles = positions[..., None] * frequency
    return (jnp.cos(angles), jnp.sin(angles))


def rotate(values, cosine, sine_part):
    half_width = values.shape[-1] // 2
    first_half = values[..., :half_width]
    second_half = values[..., half_width:]
    return jnp.concatenate(
        [
            first_half * cosine - second_half * sine_part,
            second_half * cosine + first_half * sine_part,
        ],
        axis=-1,
    )


def ancestry(parents):
    tree_size = parents.shape[-1]
    node_ids = jnp.arange(tree_size, dtype=jnp.int32)
    links = (parents[..., :, None] == node_ids[None, :]).astype(jnp.float32)
    closure = links + jnp.eye(tree_size, dtype=jnp.float32)
    for repeat in range(max(1, (tree_size - 1).bit_length())):
        closure = jnp.minimum(
            jnp.einsum("...ij,...jk->...ik", closure, closure, precision=lax.Precision.HIGHEST), 1.0
        )
    depths = jnp.sum(closure, axis=-1) - 1.0
    return (closure, depths)


def swap(values, axis, size, bits):
    return lax.ppermute(values, axis, [(i, i ^ bits) for i in range(size)])


def body(
    sizes,
    hidden,
    latent_cache,
    lengths,
    parents,
    routes,
    accepted,
    input_gain,
    query_weight,
    latent_weight,
    latent_gain,
    key_absorb,
    value_absorb,
    output_weight,
    post_gain,
    router_weight,
    shared_gate_up,
    shared_down,
    expert_gate_up,
    expert_down,
):
    n_req, n_row, n_col = sizes
    tok_rows, model_width = hidden.shape
    group_reqs, tree_size = parents.shape
    head_count = key_absorb.shape[0]
    scale_factor = 1.0 / math.sqrt(NOPE + ROPE)
    req_index = lax.axis_index("req")
    row_index = lax.axis_index("row")
    half = n_row // 2
    bf16 = jnp.bfloat16

    all_routes = lax.all_gather(routes, ("req", "row"), axis=0, tiled=False)

    normed = rms_scale(hidden.astype(jnp.float32), input_gain).astype(bf16)
    far = swap(normed, "row", n_row, 2)
    near = swap(normed, "row", n_row, 1)
    far_near = swap(far, "row", n_row, 1)
    group_rows = jnp.concatenate([normed, near, far, far_near], axis=0)

    order = jnp.arange(group_reqs, dtype=jnp.int32) ^ row_index
    cache = jnp.take(latent_cache, order, axis=0)
    lengths = jnp.take(lengths, order, axis=0)
    parents = jnp.take(parents, order, axis=0)
    closure, depths = ancestry(parents)
    queries = jnp.dot(group_rows, query_weight, preferred_element_type=jnp.float32).astype(bf16)
    queries = queries.reshape(group_reqs, tree_size, head_count, NOPE + ROPE)
    projected = jnp.dot(group_rows, latent_weight, preferred_element_type=jnp.float32).reshape(
        group_reqs, tree_size, LAT + ROPE
    )
    positions = lengths.astype(jnp.float32)[:, None] + depths
    cosine, sine_part = rope_tables(positions, ROPE)
    content = rms_scale(projected[..., :LAT], latent_gain)
    key_rope = rotate(projected[..., LAT:], cosine, sine_part)
    fresh_latents = jnp.concatenate([content, key_rope], axis=-1).astype(bf16)
    query_latent = jnp.einsum(
        "rthn,hnl->rthl", queries[..., :NOPE], key_absorb, preferred_element_type=jnp.float32
    ).astype(bf16)
    query_rope = rotate(
        queries[..., NOPE:].astype(jnp.float32), cosine[:, :, None, :], sine_part[:, :, None, :]
    ).astype(bf16)
    query_full = jnp.concatenate([query_latent, query_rope], axis=-1)
    key_rows = jnp.concatenate([cache, fresh_latents], axis=1)
    scores = (
        jnp.einsum("rthc,rkc->rhtk", query_full, key_rows, preferred_element_type=jnp.float32)
        * scale_factor
    )
    cache_spots = jnp.arange(CACHE, dtype=jnp.int32)[None, :]
    length_col = lengths[:, None]
    cache_allowed = (cache_spots < length_col) & (
        (cache_spots < SINK) | (cache_spots >= length_col - WINDOW)
    )
    allowed = jnp.concatenate(
        [
            jnp.broadcast_to(cache_allowed[:, None, :], (group_reqs, tree_size, CACHE)),
            closure > 0.5,
        ],
        axis=-1,
    )
    scores = jnp.where(allowed[:, None], scores, -1e30)
    row_peak = jnp.max(scores, axis=-1, keepdims=True)
    weights = jnp.exp(scores - row_peak)
    attention_weights = (weights / jnp.sum(weights, axis=-1, keepdims=True)).astype(bf16)
    out_latent = jnp.einsum(
        "rhtk,rkl->rthl", attention_weights, key_rows[..., :LAT], preferred_element_type=jnp.float32
    ).astype(bf16)
    head_output = jnp.einsum(
        "rthl,hlv->rthv", out_latent, value_absorb, preferred_element_type=jnp.float32
    ).astype(bf16)
    head_rows = head_output.reshape(group_reqs * tree_size, head_count * VDIM)
    partial = jnp.dot(head_rows, output_weight, preferred_element_type=jnp.float32)
    partial = partial.reshape(half, 2, tok_rows, model_width)
    partial = partial[:, 0] + swap(partial[:, 1].astype(bf16), "row", n_row, 1).astype(jnp.float32)
    partial = partial[0] + swap(partial[1].astype(bf16), "row", n_row, 2).astype(jnp.float32)
    partial = col_sum(partial, n_col)
    residual = hidden.astype(jnp.float32) + partial
    post_normed = rms_scale(residual, post_gain).astype(bf16)

    far_own = swap(post_normed, "row", n_row, 2)
    across = [swap(post_normed, "req", n_req, s) for s in range(1, n_req)]
    across = jnp.concatenate(across, axis=0)
    near_own = swap(jnp.concatenate([post_normed, far_own], axis=0), "row", n_row, 1)
    own_group = jnp.concatenate([post_normed, far_own, near_own], axis=0)
    near_across = swap(across, "row", n_row, 1)
    far_across = swap(across, "row", n_row, 2)
    near_far = swap(far_across, "row", n_row, 1)

    expert_id = req_index * n_row + row_index
    named = jnp.any(all_routes == expert_id, axis=-1).astype(jnp.float32).reshape(n_req, n_row, tok_rows)
    named = jnp.take(named, jnp.arange(n_req, dtype=jnp.int32) ^ req_index, axis=0)
    named = jnp.take(named, jnp.arange(n_row, dtype=jnp.int32) ^ row_index, axis=1)

    def expert_part(rows, marks):
        router = jax.nn.softmax(
            jnp.dot(rows, router_weight, preferred_element_type=jnp.float32), axis=-1
        )
        share = lax.dynamic_slice_in_dim(router, expert_id, 1, axis=1) * marks.reshape(-1, 1)
        gate = jnp.dot(rows, expert_gate_up[0, 0], preferred_element_type=jnp.float32)
        upper = jnp.dot(rows, expert_gate_up[0, 1], preferred_element_type=jnp.float32)
        inner = (jax.nn.silu(gate) * upper).astype(bf16)
        return share * jnp.dot(inner, expert_down[0], preferred_element_type=jnp.float32)

    gate = jnp.dot(own_group, shared_gate_up[0], preferred_element_type=jnp.float32)
    upper = jnp.dot(own_group, shared_gate_up[1], preferred_element_type=jnp.float32)
    inner = (jax.nn.silu(gate) * upper).astype(bf16)
    own_part = jnp.dot(inner, shared_down, preferred_element_type=jnp.float32)
    own_part = own_part + expert_part(own_group, jnp.stack([named[0, 0], named[0, 2], named[0, 1], named[0, 3]]))
    own_part = own_part.reshape(2, 2, tok_rows, model_width)
    lane_part = expert_part(
        jnp.concatenate([across, near_across], axis=0), jnp.stack([named[1:, 0], named[1:, 1]])
    ).reshape(2, n_req - 1, tok_rows, model_width)
    far_part = expert_part(
        jnp.concatenate([far_across, near_far], axis=0), jnp.stack([named[1:, 2], named[1:, 3]])
    ).reshape(2, n_req - 1, tok_rows, model_width)

    def fold(keep, send, bits):
        return keep + swap(send.astype(bf16), "row", n_row, bits).astype(jnp.float32)

    own_part = fold(own_part[0], own_part[1], 1)
    lane_part = fold(lane_part[0], lane_part[1], 1)
    far_part = fold(far_part[0], far_part[1], 1)
    own_sum = fold(own_part[0], own_part[1], 2)
    lane_sum = fold(lane_part, far_part, 2).astype(bf16)
    for s in range(1, n_req):
        own_sum = own_sum + swap(lane_sum[s - 1], "req", n_req, s).astype(jnp.float32)
    summed_parts = col_sum(own_sum, n_col)
    layer_output = (residual + summed_parts).astype(bf16)

    chooser = (jnp.arange(tree_size, dtype=jnp.int32)[None, :] == accepted[:, None]).astype(
        jnp.float32
    )
    path_mask = jnp.einsum("qi,qij->qj", chooser, closure[:1], precision=lax.Precision.HIGHEST)
    levels = jnp.arange(tree_size, dtype=jnp.float32)
    path_places = path_mask[:, None, :] * (depths[:1, None, :] == levels[None, :, None]).astype(
        jnp.float32
    )
    accepted_latents = jnp.einsum(
        "qkj,qjc->qkc",
        path_places.astype(bf16),
        fresh_latents[:1],
        preferred_element_type=jnp.float32,
    ).astype(bf16)
    return (layer_output, accepted_latents)


def col_sum(values, n_col):
    bits = 1
    while bits < n_col:
        sent = values.astype(jnp.bfloat16)
        values = sent.astype(jnp.float32) + swap(sent, "col", n_col, bits).astype(jnp.float32)
        bits *= 2
    return values


def solution(mesh):
    placed = (
        P(("req", "row"), None),
        P("req", None, None),
        P("req"),
        P("req", None),
        P(("req", "row"), None),
        P(("req", "row")),
        P(),
        P(None, ("row", "col")),
        P(),
        P(),
        P(("row", "col"), None, None),
        P(("row", "col"), None, None),
        P(("row", "col"), None),
        P(),
        P(),
        P(None, None, ("row", "col")),
        P(("row", "col"), None),
        P(("req", "row"), None, None, "col"),
        P(("req", "row"), "col", None),
    )
    sizes = (mesh.shape["req"], mesh.shape["row"], mesh.shape["col"])
    return jax.shard_map(
        functools.partial(body, sizes),
        mesh=mesh,
        in_specs=placed,
        out_specs=(P(("req", "row"), None), P(("req", "row"), None, None)),
        check_vma=False,
    )
```

```python
import functools
import math

import jax
import jax.numpy as jnp
from jax import lax
from jax.experimental import pallas as pl
from jax.experimental.pallas import tpu as pltpu
from jax.sharding import PartitionSpec as P

NOPE = 128
ROPE = 64
LAT = 512
VDIM = 128
CACHE = 384
WINDOW = 160
SINK = 4


EPSILON = 1e-06


def rms_scale(values, gain_row):
    mean_square = jnp.mean(values * values, axis=-1, keepdims=True)
    return values * lax.rsqrt(mean_square + EPSILON) * gain_row


def rope_tables(positions, rope_width):
    half_width = rope_width // 2
    frequency = jnp.exp(
        jnp.arange(half_width, dtype=jnp.float32) * (-2.0 * math.log(10000.0) / rope_width)
    )
    angles = positions[..., None] * frequency
    return (jnp.cos(angles), jnp.sin(angles))


def rotate(values, cosine, sine_part):
    half_width = values.shape[-1] // 2
    first_half = values[..., :half_width]
    second_half = values[..., half_width:]
    return jnp.concatenate(
        [
            first_half * cosine - second_half * sine_part,
            second_half * cosine + first_half * sine_part,
        ],
        axis=-1,
    )


def ancestry(parents):
    tree_size = parents.shape[-1]
    node_ids = jnp.arange(tree_size, dtype=jnp.int32)
    links = (parents[..., :, None] == node_ids[None, :]).astype(jnp.float32)
    closure = links + jnp.eye(tree_size, dtype=jnp.float32)
    for repeat in range(max(1, (tree_size - 1).bit_length())):
        closure = jnp.minimum(
            jnp.einsum("...ij,...jk->...ik", closure, closure, precision=lax.Precision.HIGHEST), 1.0
        )
    depths = jnp.sum(closure, axis=-1) - 1.0
    return (closure, depths)


STEPS = 4
ROUTE_COLUMNS = 512


def transposed_dot(values, weight):
    return lax.dot_general(
        values, weight, (((1,), (1,)), ((), ())), preferred_element_type=jnp.float32
    )


def expert_kernel(shared, *refs):
    rows, refs = refs[:4], refs[4:]
    marks_ref, router_ref, gate_up_ref, down_ref = refs[:4]
    refs = refs[4:]
    if shared:
        shared_gate_up_ref, shared_down_ref = refs[:2]
        refs = refs[2:]
    keep_ref, send_ref, logits, gate, upper, inner, share = refs[:7]
    if shared:
        shared_gate, shared_upper, shared_inner = refs[7:]
    step = pl.program_id(0)

    @pl.when(step < STEPS)
    def _():
        tile = jnp.concatenate([ref[...] for ref in rows], axis=0)
        first = step == 0

        def add(total, term):
            total[...] = jnp.where(first, 0.0, total[...]) + term

        add(logits, transposed_dot(tile, router_ref[...]))
        add(gate, transposed_dot(tile, gate_up_ref[0]))
        add(upper, transposed_dot(tile, gate_up_ref[1]))
        if shared:
            add(shared_gate, transposed_dot(tile, shared_gate_up_ref[0]))
            add(shared_upper, transposed_dot(tile, shared_gate_up_ref[1]))

    @pl.when(step == STEPS - 1)
    def _():
        raised = jnp.exp(logits[...] - jnp.max(logits[...], axis=-1, keepdims=True))
        router = raised / jnp.sum(raised, axis=-1, keepdims=True)
        share[...] = jnp.sum(router * marks_ref[...], axis=-1, keepdims=True)
        inner[...] = (jax.nn.silu(gate[...]) * upper[...]).astype(jnp.bfloat16)
        if shared:
            shared_inner[...] = (jax.nn.silu(shared_gate[...]) * shared_upper[...]).astype(
                jnp.bfloat16
            )

    @pl.when(step >= STEPS)
    def _():
        result = share[...] * jnp.dot(
            inner[...], down_ref[...], preferred_element_type=jnp.float32
        )
        if shared:
            result = result + jnp.dot(
                shared_inner[...], shared_down_ref[...], preferred_element_type=jnp.float32
            )
        kept = keep_ref.shape[0] * keep_ref.shape[1]
        keep_ref[...] = result[:kept].reshape(keep_ref.shape)
        send_ref[...] = result[kept:].astype(jnp.bfloat16).reshape(send_ref.shape)


def expert_part(blocks, marks, router, gate_up, down, shared_gate_up=None, shared_down=None):
    shared = shared_gate_up is not None
    tok_rows, width = blocks[0].shape
    total_rows = 4 * tok_rows
    tile = width // STEPS
    hidden_units = gate_up.shape[1]
    experts = router.shape[0]

    def early(step):
        return jnp.minimum(step, STEPS - 1)

    def late(step):
        return jnp.maximum(step - STEPS, 0)

    in_specs = [pl.BlockSpec((tok_rows, tile), lambda i: (0, early(i)))] * 4 + [
        pl.BlockSpec((total_rows, experts), lambda i: (0, 0)),
        pl.BlockSpec((experts, tile), lambda i: (0, early(i))),
        pl.BlockSpec((2, hidden_units, tile), lambda i: (0, 0, early(i))),
        pl.BlockSpec((hidden_units, tile), lambda i: (0, late(i))),
    ]
    operands = [*blocks, marks, router, gate_up, down]
    scratch = [
        pltpu.VMEM((total_rows, experts), jnp.float32),
        pltpu.VMEM((total_rows, hidden_units), jnp.float32),
        pltpu.VMEM((total_rows, hidden_units), jnp.float32),
        pltpu.VMEM((total_rows, hidden_units), jnp.bfloat16),
        pltpu.VMEM((total_rows, 1), jnp.float32),
    ]
    units = hidden_units
    if shared:
        shared_units = shared_gate_up.shape[1]
        units += shared_units
        in_specs += [
            pl.BlockSpec((2, shared_units, tile), lambda i: (0, 0, early(i))),
            pl.BlockSpec((shared_units, tile), lambda i: (0, late(i))),
        ]
        operands += [shared_gate_up, shared_down]
        scratch += [
            pltpu.VMEM((total_rows, shared_units), jnp.float32),
            pltpu.VMEM((total_rows, shared_units), jnp.float32),
            pltpu.VMEM((total_rows, shared_units), jnp.bfloat16),
        ]
    out_block = (2, tok_rows, tile)
    return pl.pallas_call(
        functools.partial(expert_kernel, shared),
        out_shape=(
            jax.ShapeDtypeStruct((2, tok_rows, width), jnp.float32),
            jax.ShapeDtypeStruct((2, tok_rows, width), jnp.bfloat16),
        ),
        grid=(2 * STEPS,),
        in_specs=in_specs,
        out_specs=(
            pl.BlockSpec(out_block, lambda i: (0, 0, late(i))),
            pl.BlockSpec(out_block, lambda i: (0, 0, late(i))),
        ),
        scratch_shapes=scratch,
        compiler_params=pltpu.CompilerParams(vmem_limit_bytes=24 << 20),
        cost_estimate=pl.CostEstimate(
            flops=6 * total_rows * width * units,
            bytes_accessed=6 * width * units + 8 * total_rows * width,
            transcendentals=total_rows * units,
        ),
        name="experts",
    )(*operands)


def swap(values, axis, size, bits):
    return lax.ppermute(values, axis, [(i, i ^ bits) for i in range(size)])


def body(
    sizes,
    hidden,
    latent_cache,
    lengths,
    parents,
    routes,
    accepted,
    input_gain,
    query_weight,
    latent_weight,
    latent_gain,
    key_absorb,
    value_absorb,
    output_weight,
    post_gain,
    router_weight,
    shared_gate_up,
    shared_down,
    expert_gate_up,
    expert_down,
):
    n_req, n_row, n_col = sizes
    tok_rows, model_width = hidden.shape
    group_reqs, tree_size = parents.shape
    head_count = key_absorb.shape[0]
    scale_factor = 1.0 / math.sqrt(NOPE + ROPE)
    req_index = lax.axis_index("req")
    row_index = lax.axis_index("row")
    half = n_row // 2
    bf16 = jnp.bfloat16

    experts = router_weight.shape[1]
    named = (routes[:, :, None] == jnp.arange(experts, dtype=jnp.int32)).any(axis=1).astype(bf16)
    named = jnp.tile(named, (1, ROUTE_COLUMNS // experts))
    named = lax.all_gather(named, ("req", "row"), axis=0, tiled=True)[:, :experts]

    normed = rms_scale(hidden.astype(jnp.float32), input_gain).astype(bf16)
    far = swap(normed, "row", n_row, 2)
    near = swap(normed, "row", n_row, 1)
    far_near = swap(far, "row", n_row, 1)
    group_rows = jnp.concatenate([normed, near, far, far_near], axis=0)

    order = jnp.arange(group_reqs, dtype=jnp.int32) ^ row_index
    cache = jnp.take(latent_cache, order, axis=0)
    lengths = jnp.take(lengths, order, axis=0)
    parents = jnp.take(parents, order, axis=0)
    closure, depths = ancestry(parents)
    queries = jnp.dot(group_rows, query_weight, preferred_element_type=jnp.float32).astype(bf16)
    queries = queries.reshape(group_reqs, tree_size, head_count, NOPE + ROPE)
    projected = jnp.dot(group_rows, latent_weight, preferred_element_type=jnp.float32).reshape(
        group_reqs, tree_size, LAT + ROPE
    )
    positions = lengths.astype(jnp.float32)[:, None] + depths
    cosine, sine_part = rope_tables(positions, ROPE)
    content = rms_scale(projected[..., :LAT], latent_gain)
    key_rope = rotate(projected[..., LAT:], cosine, sine_part)
    fresh_latents = jnp.concatenate([content, key_rope], axis=-1).astype(bf16)
    query_latent = jnp.einsum(
        "rthn,hnl->rthl", queries[..., :NOPE], key_absorb, preferred_element_type=jnp.float32
    ).astype(bf16)
    query_rope = rotate(
        queries[..., NOPE:].astype(jnp.float32), cosine[:, :, None, :], sine_part[:, :, None, :]
    ).astype(bf16)
    query_full = jnp.concatenate([query_latent, query_rope], axis=-1)
    key_rows = jnp.concatenate([cache, fresh_latents], axis=1)
    scores = (
        jnp.einsum("rthc,rkc->rhtk", query_full, key_rows, preferred_element_type=jnp.float32)
        * scale_factor
    )
    cache_spots = jnp.arange(CACHE, dtype=jnp.int32)[None, :]
    length_col = lengths[:, None]
    cache_allowed = (cache_spots < length_col) & (
        (cache_spots < SINK) | (cache_spots >= length_col - WINDOW)
    )
    allowed = jnp.concatenate(
        [
            jnp.broadcast_to(cache_allowed[:, None, :], (group_reqs, tree_size, CACHE)),
            closure > 0.5,
        ],
        axis=-1,
    )
    scores = jnp.where(allowed[:, None], scores, -1e30)
    row_peak = jnp.max(scores, axis=-1, keepdims=True)
    weights = jnp.exp(scores - row_peak)
    attention_weights = (weights / jnp.sum(weights, axis=-1, keepdims=True)).astype(bf16)
    out_latent = jnp.einsum(
        "rhtk,rkl->rthl", attention_weights, key_rows[..., :LAT], preferred_element_type=jnp.float32
    ).astype(bf16)
    head_output = jnp.einsum(
        "rthl,hlv->rthv", out_latent, value_absorb, preferred_element_type=jnp.float32
    ).astype(bf16)
    head_rows = head_output.reshape(group_reqs * tree_size, head_count * VDIM)
    partial = jnp.dot(head_rows, output_weight, preferred_element_type=jnp.float32)
    partial = partial.reshape(half, 2, tok_rows, model_width)
    partial = partial[:, 0] + swap(partial[:, 1].astype(bf16), "row", n_row, 1).astype(jnp.float32)
    partial = partial[0] + swap(partial[1].astype(bf16), "row", n_row, 2).astype(jnp.float32)
    partial = col_sum(partial, n_col)
    residual = hidden.astype(jnp.float32) + partial
    post_normed = rms_scale(residual, post_gain).astype(bf16)

    own_expert = jnp.arange(experts, dtype=jnp.int32) == req_index * n_row + row_index
    marks = jnp.where(own_expert, named.astype(jnp.float32), 0.0)
    marks = marks.reshape(n_req, n_row, tok_rows, experts)
    marks = jnp.take(marks, jnp.arange(n_req, dtype=jnp.int32) ^ req_index, axis=0)
    marks = jnp.take(marks, jnp.array([0, 2, 1, 3], jnp.int32) ^ row_index, axis=1)
    marks = marks.reshape(n_req, n_row * tok_rows, experts)
    router = router_weight.T
    gate_up = jnp.swapaxes(expert_gate_up[0], 1, 2)
    shared_weights = (jnp.swapaxes(shared_gate_up, 1, 2), shared_down)

    distances = [*range(n_req - 1, 0, -1), 0]
    arrived = {s: swap(post_normed, "req", n_req, s) if s else post_normed for s in distances}
    total = None
    for s in [0, *distances[:-1]]:
        far = swap(arrived[s], "row", n_row, 2)
        near = swap(arrived[s], "row", n_row, 1)
        far_near = swap(far, "row", n_row, 1)
        keep, send = expert_part(
            (arrived[s], far, near, far_near),
            marks[s],
            router,
            gate_up,
            expert_down[0],
            *(() if s else shared_weights),
        )
        from_near = swap(send, "row", n_row, 1).astype(jnp.float32)
        from_far = swap((keep[1] + from_near[1]).astype(bf16), "row", n_row, 2)
        part = keep[0] + from_near[0] + from_far.astype(jnp.float32)
        if s:
            part = swap(part.astype(bf16), "req", n_req, s).astype(jnp.float32)
        total = part if total is None else total + part
    summed_parts = col_sum(total, n_col)
    layer_output = (residual + summed_parts).astype(bf16)

    chooser = (jnp.arange(tree_size, dtype=jnp.int32)[None, :] == accepted[:, None]).astype(
        jnp.float32
    )
    path_mask = jnp.einsum("qi,qij->qj", chooser, closure[:1], precision=lax.Precision.HIGHEST)
    levels = jnp.arange(tree_size, dtype=jnp.float32)
    path_places = path_mask[:, None, :] * (depths[:1, None, :] == levels[None, :, None]).astype(
        jnp.float32
    )
    accepted_latents = jnp.einsum(
        "qkj,qjc->qkc",
        path_places.astype(bf16),
        fresh_latents[:1],
        preferred_element_type=jnp.float32,
    ).astype(bf16)
    return (layer_output, accepted_latents)


def col_sum(values, n_col):
    bits = 1
    while bits < n_col:
        sent = values.astype(jnp.bfloat16)
        values = sent.astype(jnp.float32) + swap(sent, "col", n_col, bits).astype(jnp.float32)
        bits *= 2
    return values


def solution(mesh):
    placed = (
        P(("req", "row"), None),
        P("req", None, None),
        P("req"),
        P("req", None),
        P(("req", "row"), None),
        P(("req", "row")),
        P(),
        P(None, ("row", "col")),
        P(),
        P(),
        P(("row", "col"), None, None),
        P(("row", "col"), None, None),
        P(("row", "col"), None),
        P(),
        P(),
        P(None, None, ("row", "col")),
        P(("row", "col"), None),
        P(("req", "row"), None, None, "col"),
        P(("req", "row"), "col", None),
    )
    sizes = (mesh.shape["req"], mesh.shape["row"], mesh.shape["col"])
    return jax.shard_map(
        functools.partial(body, sizes),
        mesh=mesh,
        in_specs=placed,
        out_specs=(P(("req", "row"), None), P(("req", "row"), None, None)),
        check_vma=False,
    )
```

```python
import functools
import math

import jax
import jax.numpy as jnp
from jax import lax
from jax.experimental import pallas as pl
from jax.experimental.pallas import tpu as pltpu
from jax.sharding import PartitionSpec as P

NOPE = 128
ROPE = 64
LAT = 512
VDIM = 128
CACHE = 384
WINDOW = 160
SINK = 4


EPSILON = 1e-06
EXTRA = 128
CHUNKS = 4


def rms_scale(values, gain_row):
    mean_square = jnp.mean(values * values, axis=-1, keepdims=True)
    return values * lax.rsqrt(mean_square + EPSILON) * gain_row


def rotate(values, cosine, sine_part):
    half_width = values.shape[-1] // 2
    first_half = values[..., :half_width]
    second_half = values[..., half_width:]
    return jnp.concatenate(
        [
            first_half * cosine - second_half * sine_part,
            second_half * cosine + first_half * sine_part,
        ],
        axis=-1,
    )


def dot(values, weight):
    return jnp.dot(values, weight, preferred_element_type=jnp.float32)


def transposed_dot(values, weight):
    return lax.dot_general(
        values, weight, (((1,), (1,)), ((), ())), preferred_element_type=jnp.float32
    )


WHOLE = pl.BlockSpec(memory_space=pltpu.VMEM)
SCALARS = pl.BlockSpec(memory_space=pltpu.SMEM)
PLACED = pl.BlockSpec(memory_space=pl.ANY)


def params(megabytes):
    return pltpu.CompilerParams(vmem_limit_bytes=megabytes << 20)


def tree_kernel(row_ref, lengths_ref, accepted_ref, parents_ref, closure_ref, turns_ref, places_ref):
    requests, size, _ = closure_ref.shape
    down = lax.broadcasted_iota(jnp.int32, (size, size), 0)
    across = lax.broadcasted_iota(jnp.int32, (size, size), 1)
    eye = (down == across).astype(jnp.bfloat16)
    closures = []
    for k in range(requests):
        parent_row = parents_ref[pl.ds(row_ref[0] ^ k, 1), :]
        links = (parent_row == down).astype(jnp.bfloat16) + eye
        closures.append(
            lax.dot_general(
                links, eye, (((0,), (0,)), ((), ())), preferred_element_type=jnp.float32
            )
        )
    for repeat in range(max(1, (size - 1).bit_length())):
        narrow = [closure.astype(jnp.bfloat16) for closure in closures]
        closures = [jnp.minimum(dot(each, each), 1.0) for each in narrow]
    step = -2.0 * math.log(10000.0) / ROPE
    frequency = jnp.exp(
        lax.broadcasted_iota(jnp.int32, (size, ROPE // 2), 1).astype(jnp.float32) * step
    )
    for k in range(requests):
        closure_ref[k] = closures[k]
        depth = jnp.sum(closures[k], axis=-1, keepdims=True) - 1.0
        angles = (lengths_ref[row_ref[0] ^ k].astype(jnp.float32) + depth) * frequency
        turns_ref[k, :, : ROPE // 2] = jnp.cos(angles)
        turns_ref[k, :, ROPE // 2 :] = jnp.sin(angles)
    own = closures[0].astype(jnp.bfloat16)
    depth_row = transposed_dot(jnp.ones((8, size), jnp.bfloat16), own)[:1] - 1.0
    chosen = (lax.broadcasted_iota(jnp.int32, (size, 1), 0) == accepted_ref[0]).astype(jnp.float32)
    path_mask = jnp.sum(chosen * closures[0], axis=0, keepdims=True)
    places_ref[...] = jnp.where(
        depth_row == down.astype(jnp.float32), path_mask, 0.0
    ).astype(jnp.bfloat16)


def tree_tables(row_index, lengths, accepted, parents):
    requests, size = parents.shape
    return pl.pallas_call(
        tree_kernel,
        out_shape=(
            jax.ShapeDtypeStruct((requests, size, size), jnp.float32),
            jax.ShapeDtypeStruct((requests, size, ROPE), jnp.float32),
            jax.ShapeDtypeStruct((size, size), jnp.bfloat16),
        ),
        in_specs=[SCALARS, SCALARS, SCALARS, WHOLE],
        out_specs=(WHOLE, WHOLE, WHOLE),
        compiler_params=params(16),
        name="trees",
    )(row_index, lengths, accepted, parents)


def attention_kernel(first, place, row_ref, lengths_ref, *refs):
    (
        first_ref,
        second_ref,
        cache_a_ref,
        cache_b_ref,
        closure_ref,
        turns_ref,
        places_ref,
        gain_ref,
        query_ref,
        latent_ref,
        latent_gain_ref,
        key_ref,
        value_ref,
        output_ref,
        keep_ref,
        send_ref,
    ) = refs[:16]
    size = first_ref.shape[0]
    heads = key_ref.shape[0]
    bf16 = jnp.bfloat16
    scale_factor = 1.0 / math.sqrt(NOPE + ROPE)
    rows = jnp.concatenate([first_ref[...], second_ref[...]], axis=0).astype(jnp.float32)
    rows = rms_scale(rows, gain_ref[...]).astype(bf16)
    turns = jnp.concatenate([turns_ref[place], turns_ref[place + 1]], axis=0)
    cosine, sine_part = turns[:, : ROPE // 2], turns[:, ROPE // 2 :]
    projected = transposed_dot(rows, latent_ref[...])
    content = rms_scale(projected[:, :LAT], latent_gain_ref[...]).astype(bf16)
    key_rope = rotate(projected[:, LAT:], cosine, sine_part).astype(bf16)
    if first:
        accepted_ref = refs[16]
        accepted_ref[0, :, :LAT] = dot(places_ref[...], content[:size]).astype(bf16)
        accepted_ref[0, :, LAT:] = dot(places_ref[...], key_rope[:size]).astype(bf16)
    queries = dot(rows, query_ref[...])
    query_latent, query_rope = [], []
    for h in range(heads):
        start = h * (NOPE + ROPE)
        query_latent.append(
            dot(queries[:, start : start + NOPE].astype(bf16), key_ref[h]).astype(bf16)
        )
        turned = queries[:, start + NOPE : start + NOPE + ROPE].astype(bf16).astype(jnp.float32)
        query_rope.append(rotate(turned, cosine, sine_part).astype(bf16))
    outs = [[], []]
    for r, cache_ref in enumerate((cache_a_ref, cache_b_ref)):
        part = slice(r * size, (r + 1) * size)
        latent_rows = jnp.concatenate([each[part] for each in query_latent], axis=0)
        rope_rows = jnp.concatenate([each[part] for each in query_rope], axis=0)
        old = dot(latent_rows, cache_ref[0, :LAT, :]) + dot(rope_rows, cache_ref[0, LAT:, :])
        new = transposed_dot(latent_rows, content[part]) + transposed_dot(rope_rows, key_rope[part])
        length = lengths_ref[row_ref[0] ^ (place + r)]
        spots = lax.broadcasted_iota(jnp.int32, (1, old.shape[1]), 1)
        allowed = (spots < length) & ((spots < SINK) | (spots >= length - WINDOW))
        related = jnp.concatenate([closure_ref[place + r]] * heads, axis=0) > 0.5
        old = jnp.where(allowed, old * scale_factor, -1e30)
        new = jnp.where(related, new * scale_factor, -1e30)
        peak = jnp.maximum(
            jnp.max(old, axis=-1, keepdims=True), jnp.max(new, axis=-1, keepdims=True)
        )
        old = jnp.exp(old - peak)
        new = jnp.exp(new - peak)
        total = jnp.sum(old, axis=-1, keepdims=True) + jnp.sum(new, axis=-1, keepdims=True)
        old = (old / total).astype(bf16)
        new = (new / total).astype(bf16)
        mixed = transposed_dot(old, cache_ref[0, :LAT, :]) + dot(new, content[part])
        for h in range(heads):
            outs[r].append(mixed[h * size : (h + 1) * size].astype(bf16))
    head_rows = [
        dot(jnp.concatenate([outs[0][h], outs[1][h]], axis=0), value_ref[h]).astype(bf16)
        for h in range(heads)
    ]
    head_rows = jnp.concatenate(head_rows, axis=1)
    partial = dot(head_rows, output_ref[...])
    keep_ref[...] = partial[:size]
    send_ref[...] = partial[size:].astype(bf16)


def attention_part(first, place, row_index, lengths, blocks, cache, tables, weights):
    size, width = blocks[0].shape
    slots, spots = cache.shape[1:]
    heads = weights[4].shape[0]
    closure, turns, places = tables

    def whole(array):
        rank = array.ndim
        return pl.BlockSpec(array.shape, lambda i, row, lens: (0,) * rank)

    def cached(k):
        return pl.BlockSpec((1, slots, spots), lambda i, row, lens: (row[0] ^ k, 0, 0))

    rest = [closure, turns, places, *weights]
    out_shape = [
        jax.ShapeDtypeStruct((size, width), jnp.float32),
        jax.ShapeDtypeStruct((size, width), jnp.bfloat16),
    ]
    if first:
        out_shape.append(jax.ShapeDtypeStruct((1, size, LAT + ROPE), jnp.bfloat16))
    rows = 2 * size
    flops = 2 * rows * width * (weights[1].shape[1] + LAT + ROPE + heads * VDIM)
    return pl.pallas_call(
        functools.partial(attention_kernel, first, place),
        out_shape=tuple(out_shape),
        grid_spec=pltpu.PrefetchScalarGridSpec(
            num_scalar_prefetch=2,
            grid=(1,),
            in_specs=[whole(blocks[0]), whole(blocks[1]), cached(place), cached(place + 1)]
            + [whole(each) for each in rest],
            out_specs=tuple(whole(each) for each in out_shape),
        ),
        compiler_params=params(32),
        cost_estimate=pl.CostEstimate(
            flops=flops,
            bytes_accessed=2 * width * (weights[1].shape[1] + LAT + ROPE + heads * VDIM),
            transcendentals=rows * heads * (spots + size),
        ),
        name="attention",
    )(row_index, lengths, blocks[0], blocks[1], cache, cache, *rest)


def join_kernel(hidden_ref, keep_ref, arrived_ref, gain_ref, named_ref, residual_ref, block_ref):
    width = hidden_ref.shape[1]
    total = keep_ref[...].astype(jnp.float32)
    for k in range(arrived_ref.shape[0]):
        total = total + arrived_ref[k].astype(jnp.float32)
    residual = hidden_ref[...].astype(jnp.float32) + total
    residual_ref[...] = residual
    block_ref[:, :width] = rms_scale(residual, gain_ref[...]).astype(jnp.bfloat16)
    block_ref[:, width:] = named_ref[...]


def joined(hidden, keep, arrived, gain, named):
    rows, width = hidden.shape
    return pl.pallas_call(
        join_kernel,
        out_shape=(
            jax.ShapeDtypeStruct((rows, width), jnp.float32),
            jax.ShapeDtypeStruct((rows, width + EXTRA), jnp.bfloat16),
        ),
        in_specs=[WHOLE] * 5,
        out_specs=(WHOLE, WHOLE),
        compiler_params=params(16),
        name="join",
    )(hidden, keep, arrived, gain, named)


def expert_kernel(shared, *refs):
    blocks, refs = refs[:4], refs[4:]
    own_ref, router_ref, gate_up_ref, down_ref = refs[:4]
    refs = refs[4:]
    if shared:
        shared_gate_up_ref, shared_down_ref = refs[:2]
        refs = refs[2:]
    keep_ref, send_ref = refs
    experts, width = router_ref.shape
    size = blocks[0].shape[0]
    rows = jnp.concatenate([ref[:, :width] for ref in blocks], axis=0)
    named = jnp.concatenate([ref[:, width:] for ref in blocks], axis=0)[:, :experts]
    logits = transposed_dot(rows, router_ref[...])
    raised = jnp.exp(logits - jnp.max(logits, axis=-1, keepdims=True))
    router = raised / jnp.sum(raised, axis=-1, keepdims=True)
    share = jnp.sum(router * named.astype(jnp.float32) * own_ref[...], axis=-1, keepdims=True)

    def inner(weights_ref):
        gate = transposed_dot(rows, weights_ref[0])
        upper = transposed_dot(rows, weights_ref[1])
        return (jax.nn.silu(gate) * upper).astype(jnp.bfloat16)

    routed_inner = inner(gate_up_ref)
    if shared:
        shared_inner = inner(shared_gate_up_ref)
    tile = width // CHUNKS
    for k in range(CHUNKS):
        part = slice(k * tile, (k + 1) * tile)
        result = share * dot(routed_inner, down_ref[:, part])
        if shared:
            result = result + dot(shared_inner, shared_down_ref[:, part])
        keep_ref[:, :, part] = result[: 2 * size].reshape(2, size, tile)
        send_ref[:, :, part] = result[2 * size :].astype(jnp.bfloat16).reshape(2, size, tile)


def expert_part(blocks, own_expert, router, routed_weights, shared_weights=()):
    size = blocks[0].shape[0]
    width = router.shape[1]
    units = sum(each.shape[0] for each in (*routed_weights, *shared_weights) if each.ndim == 2)
    operands = [*blocks, own_expert, router, *routed_weights, *shared_weights]
    return pl.pallas_call(
        functools.partial(expert_kernel, bool(shared_weights)),
        out_shape=(
            jax.ShapeDtypeStruct((2, size, width), jnp.float32),
            jax.ShapeDtypeStruct((2, size, width), jnp.bfloat16),
        ),
        in_specs=[WHOLE] * len(operands),
        out_specs=(WHOLE, WHOLE),
        compiler_params=params(32),
        cost_estimate=pl.CostEstimate(
            flops=24 * size * width * units,
            bytes_accessed=6 * width * units,
            transcendentals=4 * size * units,
        ),
        name="experts",
    )(*operands)


def swap(values, axis, size, bits):
    return lax.ppermute(values, axis, [(i, i ^ bits) for i in range(size)])


def body(
    sizes,
    hidden,
    latent_cache,
    lengths,
    parents,
    routes,
    accepted,
    input_gain,
    query_weight,
    latent_weight,
    latent_gain,
    key_absorb,
    value_absorb,
    output_weight,
    post_gain,
    router_weight,
    shared_gate_up,
    shared_down,
    expert_gate_up,
    expert_down,
):
    n_req, n_row, n_col = sizes
    experts = router_weight.shape[1]
    req_index = lax.axis_index("req")
    row_index = lax.axis_index("row")
    bf16 = jnp.bfloat16

    far = swap(hidden, "row", n_row, 2)
    near = swap(hidden, "row", n_row, 1)
    far_near = swap(far, "row", n_row, 1)

    row_scalar = row_index.astype(jnp.int32).reshape(1)
    tables = tree_tables(row_scalar, lengths, accepted, parents)
    cache = jnp.swapaxes(latent_cache, 1, 2)
    weights = (
        input_gain[None],
        query_weight,
        latent_weight.T,
        latent_gain[None],
        key_absorb,
        value_absorb,
        output_weight,
    )
    own_keep, own_send, accepted_latents = attention_part(
        True, 0, row_scalar, lengths, (hidden, near), cache, tables, weights
    )
    far_keep, far_send = attention_part(
        False, 2, row_scalar, lengths, (far, far_near), cache, tables, weights
    )

    def fold(keep, sent):
        return keep + swap(sent, "row", n_row, 1).astype(jnp.float32)

    from_far = swap(fold(far_keep, far_send).astype(bf16), "row", n_row, 2)
    partial = fold(own_keep, own_send) + from_far.astype(jnp.float32)
    partial, arrived = col_parts(partial, n_col)
    named = (routes[:, :, None] == jnp.arange(EXTRA, dtype=jnp.int32)).any(axis=1).astype(bf16)
    residual, block = joined(hidden, partial, arrived, post_gain[None], named)

    own_expert = jnp.arange(experts, dtype=jnp.int32) == req_index * n_row + row_index
    own_expert = own_expert.astype(jnp.float32)[None]
    router = router_weight.T
    routed_weights = (jnp.swapaxes(expert_gate_up[0], 1, 2), expert_down[0])
    shared_weights = (jnp.swapaxes(shared_gate_up, 1, 2), shared_down)
    distances = [*range(n_req - 1, 0, -1)]
    blocks = {s: swap(block, "req", n_req, s) for s in distances}
    blocks[0] = block
    total = None
    for s in [0, *distances]:
        far = swap(blocks[s], "row", n_row, 2)
        near = swap(blocks[s], "row", n_row, 1)
        far_near = swap(far, "row", n_row, 1)
        keep, send = expert_part(
            (blocks[s], far, near, far_near),
            own_expert,
            router,
            routed_weights,
            () if s else shared_weights,
        )
        from_near = swap(send, "row", n_row, 1).astype(jnp.float32)
        from_far = swap((keep[1] + from_near[1]).astype(bf16), "row", n_row, 2)
        part = keep[0] + from_near[0] + from_far.astype(jnp.float32)
        if s:
            part = swap(part.astype(bf16), "req", n_req, s).astype(jnp.float32)
        total = part if total is None else total + part
    total, arrived = col_parts(total, n_col)
    layer_output = residual + (total.astype(jnp.float32) + sum_up(arrived))
    return (layer_output.astype(bf16), accepted_latents)


def sum_up(parts):
    return jnp.sum(parts.astype(jnp.float32), axis=0)


def col_parts(values, n_col):
    bits = 1
    while 2 * bits < n_col:
        sent = values.astype(jnp.bfloat16)
        values = sent.astype(jnp.float32) + swap(sent, "col", n_col, bits).astype(jnp.float32)
        bits *= 2
    sent = values.astype(jnp.bfloat16)
    return sent, swap(sent, "col", n_col, bits)[None]


def solution(mesh):
    placed = (
        P(("req", "row"), None),
        P("req", None, None),
        P("req"),
        P("req", None),
        P(("req", "row"), None),
        P(("req", "row")),
        P(),
        P(None, ("row", "col")),
        P(),
        P(),
        P(("row", "col"), None, None),
        P(("row", "col"), None, None),
        P(("row", "col"), None),
        P(),
        P(),
        P(None, None, ("row", "col")),
        P(("row", "col"), None),
        P(("req", "row"), None, None, "col"),
        P(("req", "row"), "col", None),
    )
    sizes = (mesh.shape["req"], mesh.shape["row"], mesh.shape["col"])
    return jax.shard_map(
        functools.partial(body, sizes),
        mesh=mesh,
        in_specs=placed,
        out_specs=(P(("req", "row"), None), P(("req", "row"), None, None)),
        check_vma=False,
    )
```

```python
import functools
import math

import jax
import jax.numpy as jnp
from jax import lax
from jax.experimental import pallas as pl
from jax.experimental.pallas import tpu as pltpu
from jax.sharding import PartitionSpec as P

NOPE = 128
ROPE = 64
LAT = 512
VDIM = 128
CACHE = 384
WINDOW = 160
SINK = 4


EPSILON = 1e-06
EXTRA = 128
CHUNKS = 4


def rms_scale(values, gain_row):
    mean_square = jnp.mean(values * values, axis=-1, keepdims=True)
    return values * lax.rsqrt(mean_square + EPSILON) * gain_row


def rotate(values, cosine, sine_part):
    half_width = values.shape[-1] // 2
    first_half = values[..., :half_width]
    second_half = values[..., half_width:]
    return jnp.concatenate(
        [
            first_half * cosine - second_half * sine_part,
            second_half * cosine + first_half * sine_part,
        ],
        axis=-1,
    )


def dot(values, weight):
    return jnp.dot(values, weight, preferred_element_type=jnp.float32)


def transposed_dot(values, weight):
    return lax.dot_general(
        values, weight, (((1,), (1,)), ((), ())), preferred_element_type=jnp.float32
    )


WHOLE = pl.BlockSpec(memory_space=pltpu.VMEM)
SCALARS = pl.BlockSpec(memory_space=pltpu.SMEM)
STORED = pl.BlockSpec(memory_space=pltpu.HBM)


SMALL = pl.CostEstimate(flops=1, bytes_accessed=1, transcendentals=0)


def params(megabytes):
    return pltpu.CompilerParams(vmem_limit_bytes=megabytes << 20)


def tree_kernel(row_ref, lengths_ref, accepted_ref, parents_ref, closure_ref, turns_ref, places_ref):
    requests, size, _ = closure_ref.shape
    down = lax.broadcasted_iota(jnp.int32, (size, size), 0)
    across = lax.broadcasted_iota(jnp.int32, (size, size), 1)
    eye = (down == across).astype(jnp.bfloat16)
    closures = []
    for k in range(requests):
        parent_row = parents_ref[pl.ds(row_ref[0] ^ k, 1), :]
        links = (parent_row == down).astype(jnp.bfloat16) + eye
        closures.append(
            lax.dot_general(
                links, eye, (((0,), (0,)), ((), ())), preferred_element_type=jnp.float32
            )
        )
    for repeat in range(max(1, (size - 1).bit_length())):
        narrow = [closure.astype(jnp.bfloat16) for closure in closures]
        closures = [jnp.minimum(dot(each, each), 1.0) for each in narrow]
    step = -2.0 * math.log(10000.0) / ROPE
    frequency = jnp.exp(
        lax.broadcasted_iota(jnp.int32, (size, ROPE // 2), 1).astype(jnp.float32) * step
    )
    for k in range(requests):
        closure_ref[k] = closures[k]
        depth = jnp.sum(closures[k], axis=-1, keepdims=True) - 1.0
        length = lengths_ref[row_ref[0] ^ k].astype(jnp.float32)
        angles = (length + depth) * frequency
        turns_ref[k, :, : ROPE // 2] = jnp.cos(angles)
        turns_ref[k, :, ROPE // 2 : ROPE] = jnp.sin(angles)
        turns_ref[k, :, ROPE : ROPE + 1] = jnp.full((size, 1), length)
    own = closures[0].astype(jnp.bfloat16)
    depth_row = transposed_dot(jnp.ones((8, size), jnp.bfloat16), own)[:1] - 1.0
    chosen = (lax.broadcasted_iota(jnp.int32, (size, 1), 0) == accepted_ref[0]).astype(jnp.float32)
    path_mask = jnp.sum(chosen * closures[0], axis=0, keepdims=True)
    places_ref[...] = jnp.where(
        depth_row == down.astype(jnp.float32), path_mask, 0.0
    ).astype(jnp.bfloat16)


def tree_tables(row_index, lengths, accepted, parents):
    requests, size = parents.shape
    return pl.pallas_call(
        tree_kernel,
        out_shape=(
            jax.ShapeDtypeStruct((requests, size, size), jnp.float32),
            jax.ShapeDtypeStruct((requests, size, ROPE + 1), jnp.float32),
            jax.ShapeDtypeStruct((size, size), jnp.bfloat16),
        ),
        in_specs=[SCALARS, SCALARS, SCALARS, WHOLE],
        out_specs=(WHOLE, WHOLE, WHOLE),
        compiler_params=params(16),
        name="trees",
    )(row_index, lengths, accepted, parents)


def attention_kernel(first, place, row_ref, *refs):
    first_ref, second_ref, closure_ref, turns_ref, places_ref, cache_hbm, *stored = refs[:13]
    outs, scratch = refs[13 : 15 + first], refs[15 + first :]
    keep_ref, send_ref = outs[:2]
    *held, cache_ref, first_held, sems = scratch
    gain_ref, query_ref, latent_ref, latent_gain_ref, key_ref, value_ref, output_ref = held
    copies = [
        pltpu.make_async_copy(stored[k], held[k], sems.at[k]) for k in (0, 2, 1, 3, 4, 5, 6)
    ]
    gain_copy, latent_copy, query_copy, latent_gain_copy, key_copy, value_copy, output_copy = copies
    cache_copies = [
        pltpu.make_async_copy(
            cache_hbm.at[row_ref[0] ^ (place + r)], cache_ref.at[r], sems.at[7 + r]
        )
        for r in range(2)
    ]
    if first:
        rows_copy = pltpu.make_async_copy(first_ref, first_held, sems.at[9])
        rows_copy.start()
        first_ref = first_held
    for copy in (*copies[:5], *cache_copies, *copies[5:]):
        copy.start()
    if first:
        rows_copy.wait()
    gain_copy.wait()
    size = first_ref.shape[0]
    heads = key_ref.shape[0]
    bf16 = jnp.bfloat16
    scale_factor = 1.0 / math.sqrt(NOPE + ROPE)
    rows = jnp.concatenate([first_ref[...], second_ref[...]], axis=0).astype(jnp.float32)
    rows = rms_scale(rows, gain_ref[...]).astype(bf16)
    turns = jnp.concatenate([turns_ref[place], turns_ref[place + 1]], axis=0)
    cosine, sine_part = turns[:, : ROPE // 2], turns[:, ROPE // 2 : ROPE]
    latent_copy.wait()
    projected = transposed_dot(rows, latent_ref[...])
    latent_gain_copy.wait()
    content = rms_scale(projected[:, :LAT], latent_gain_ref[...]).astype(bf16)
    key_rope = rotate(projected[:, LAT:], cosine, sine_part).astype(bf16)
    if first:
        accepted_ref = outs[2]
        accepted_ref[0, :, :LAT] = dot(places_ref[...], content[:size]).astype(bf16)
        accepted_ref[0, :, LAT:] = dot(places_ref[...], key_rope[:size]).astype(bf16)
    query_copy.wait()
    queries = dot(rows, query_ref[...])
    key_copy.wait()
    query_latent, query_rope = [], []
    for h in range(heads):
        start = h * (NOPE + ROPE)
        query_latent.append(
            dot(queries[:, start : start + NOPE].astype(bf16), key_ref[h]).astype(bf16)
        )
        turned = queries[:, start + NOPE : start + NOPE + ROPE].astype(bf16).astype(jnp.float32)
        query_rope.append(rotate(turned, cosine, sine_part).astype(bf16))
    mixed_rows = [[], []]
    for r in range(2):
        cache_copies[r].wait()
        part = slice(r * size, (r + 1) * size)
        latent_rows = jnp.concatenate([each[part] for each in query_latent], axis=0)
        rope_rows = jnp.concatenate([each[part] for each in query_rope], axis=0)
        old = dot(latent_rows, cache_ref[r, :LAT, :]) + dot(rope_rows, cache_ref[r, LAT:, :])
        new = transposed_dot(latent_rows, content[part]) + transposed_dot(rope_rows, key_rope[part])
        length = jnp.concatenate([turns_ref[place + r, :, ROPE : ROPE + 1]] * heads, axis=0)
        spots = lax.broadcasted_iota(jnp.int32, old.shape, 1).astype(jnp.float32)
        allowed = (spots < length) & ((spots < SINK) | (spots >= length - WINDOW))
        related = jnp.concatenate([closure_ref[place + r]] * heads, axis=0) > 0.5
        old = jnp.where(allowed, old * scale_factor, -1e30)
        new = jnp.where(related, new * scale_factor, -1e30)
        peak = jnp.maximum(
            jnp.max(old, axis=-1, keepdims=True), jnp.max(new, axis=-1, keepdims=True)
        )
        old = jnp.exp(old - peak)
        new = jnp.exp(new - peak)
        total = jnp.sum(old, axis=-1, keepdims=True) + jnp.sum(new, axis=-1, keepdims=True)
        old = (old / total).astype(bf16)
        new = (new / total).astype(bf16)
        mixed = transposed_dot(old, cache_ref[r, :LAT, :]) + dot(new, content[part])
        for h in range(heads):
            mixed_rows[r].append(mixed[h * size : (h + 1) * size].astype(bf16))
    value_copy.wait()
    head_rows = [
        dot(jnp.concatenate([mixed_rows[0][h], mixed_rows[1][h]], axis=0), value_ref[h]).astype(bf16)
        for h in range(heads)
    ]
    head_rows = jnp.concatenate(head_rows, axis=1)
    output_copy.wait()
    partial = dot(head_rows, output_ref[...])
    keep_ref[...] = partial[:size]
    send_ref[...] = partial[size:].astype(bf16)


def attention_part(first, place, row_index, blocks, cache, tables, weights):
    size, width = blocks[0].shape
    slots, spots = cache.shape[1:]
    heads = weights[4].shape[0]
    out_shape = [
        jax.ShapeDtypeStruct((size, width), jnp.float32),
        jax.ShapeDtypeStruct((size, width), jnp.bfloat16),
    ]
    if first:
        out_shape.append(jax.ShapeDtypeStruct((1, size, LAT + ROPE), jnp.bfloat16))
    rows = 2 * size
    columns = weights[1].shape[1] + LAT + ROPE + heads * VDIM
    return pl.pallas_call(
        functools.partial(attention_kernel, first, place),
        out_shape=tuple(out_shape),
        in_specs=[SCALARS, STORED if first else WHOLE] + [WHOLE] * 4 + [STORED] * 8,
        out_specs=(WHOLE,) * len(out_shape),
        scratch_shapes=[
            *(pltpu.VMEM(each.shape, each.dtype) for each in weights),
            pltpu.VMEM((2, slots, spots), cache.dtype),
            pltpu.VMEM((size, width), jnp.bfloat16),
            pltpu.SemaphoreType.DMA((10,)),
        ],
        compiler_params=params(53),
        cost_estimate=SMALL,
        name="attention",
    )(row_index, *blocks, *tables, cache, *weights)


def join_kernel(hidden_ref, keep_ref, arrived_ref, gain_ref, named_ref, residual_ref, block_ref):
    width = hidden_ref.shape[1]
    total = keep_ref[...].astype(jnp.float32)
    for k in range(arrived_ref.shape[0]):
        total = total + arrived_ref[k].astype(jnp.float32)
    residual = hidden_ref[...].astype(jnp.float32) + total
    residual_ref[...] = residual
    block_ref[:, :width] = rms_scale(residual, gain_ref[...]).astype(jnp.bfloat16)
    block_ref[:, width:] = named_ref[...]


def joined(hidden, keep, arrived, gain, named):
    rows, width = hidden.shape
    return pl.pallas_call(
        join_kernel,
        out_shape=(
            jax.ShapeDtypeStruct((rows, width), jnp.float32),
            jax.ShapeDtypeStruct((rows, width + EXTRA), jnp.bfloat16),
        ),
        in_specs=[WHOLE] * 5,
        out_specs=(WHOLE, WHOLE),
        compiler_params=params(16),
        name="join",
    )(hidden, keep, arrived, gain, named)


def expert_kernel(shared, *refs):
    blocks, refs = refs[:4], refs[4:]
    own_ref, refs = refs[0], refs[1:]
    count = 5 if shared else 3
    stored, (keep_ref, send_ref), held, sems = (
        refs[:count],
        refs[count : count + 2],
        refs[count + 2 : 2 * count + 2],
        refs[-1],
    )
    router_ref, gate_up_ref, down_ref = held[:3]
    experts, width = router_ref.shape
    router_copy = pltpu.make_async_copy(stored[0], router_ref, sems.at[0])
    router_copy.start()
    pairs = []
    for k in range(1, count, 2):
        pairs.append(
            [
                pltpu.make_async_copy(stored[k].at[0], held[k].at[0], sems.at[3 * k]),
                pltpu.make_async_copy(stored[k].at[1], held[k].at[1], sems.at[3 * k + 1]),
                pltpu.make_async_copy(stored[k + 1], held[k + 1], sems.at[3 * k + 2]),
            ]
        )
    for copy in (copy for pair in pairs for copy in pair[:2]):
        copy.start()
    for pair in pairs:
        pair[2].start()
    size = blocks[0].shape[0]
    rows = jnp.concatenate([ref[:, :width] for ref in blocks], axis=0)
    named = jnp.concatenate([ref[:, width:] for ref in blocks], axis=0)[:, :experts]
    router_copy.wait()
    logits = transposed_dot(rows, router_ref[...])
    raised = jnp.exp(logits - jnp.max(logits, axis=-1, keepdims=True))
    router = raised / jnp.sum(raised, axis=-1, keepdims=True)
    share = jnp.sum(router * named.astype(jnp.float32) * own_ref[...], axis=-1, keepdims=True)

    def inner(weights_ref, copies):
        copies[0].wait()
        gate = transposed_dot(rows, weights_ref[0])
        copies[1].wait()
        upper = transposed_dot(rows, weights_ref[1])
        return (jax.nn.silu(gate) * upper).astype(jnp.bfloat16)

    routed_inner = inner(gate_up_ref, pairs[0])
    if shared:
        shared_inner = inner(held[3], pairs[1])
    for pair in pairs:
        pair[2].wait()
    tile = width // CHUNKS
    for k in range(CHUNKS):
        part = slice(k * tile, (k + 1) * tile)
        result = share * dot(routed_inner, down_ref[:, part])
        if shared:
            result = result + dot(shared_inner, held[4][:, part])
        keep_ref[:, :, part] = result[: 2 * size].reshape(2, size, tile)
        send_ref[:, :, part] = result[2 * size :].astype(jnp.bfloat16).reshape(2, size, tile)


def expert_part(blocks, own_expert, router, routed_weights, shared_weights=()):
    size = blocks[0].shape[0]
    width = router.shape[1]
    units = sum(each.shape[0] for each in (*routed_weights, *shared_weights) if each.ndim == 2)
    stored = [router, *routed_weights, *shared_weights]
    return pl.pallas_call(
        functools.partial(expert_kernel, bool(shared_weights)),
        out_shape=(
            jax.ShapeDtypeStruct((2, size, width), jnp.float32),
            jax.ShapeDtypeStruct((2, size, width), jnp.bfloat16),
        ),
        in_specs=[WHOLE] * 5 + [STORED] * len(stored),
        out_specs=(WHOLE, WHOLE),
        scratch_shapes=[
            *(pltpu.VMEM(each.shape, each.dtype) for each in stored),
            pltpu.SemaphoreType.DMA((12,)),
        ],
        compiler_params=params(50),
        cost_estimate=SMALL,
        name="experts",
    )(*blocks, own_expert, *stored)


def after(values, *others):
    return lax.optimization_barrier((values, *others))[0]


def swap(values, axis, size, bits):
    return lax.ppermute(values, axis, [(i, i ^ bits) for i in range(size)])


def body(
    sizes,
    hidden,
    latent_cache,
    lengths,
    parents,
    routes,
    accepted,
    input_gain,
    query_weight,
    latent_weight,
    latent_gain,
    key_absorb,
    value_absorb,
    output_weight,
    post_gain,
    router_weight,
    shared_gate_up,
    shared_down,
    expert_gate_up,
    expert_down,
):
    n_req, n_row, n_col = sizes
    experts = router_weight.shape[1]
    req_index = lax.axis_index("req")
    row_index = lax.axis_index("row")
    bf16 = jnp.bfloat16

    far = swap(hidden, "row", n_row, 2)
    near = swap(hidden, "row", n_row, 1)

    row_scalar = row_index.astype(jnp.int32).reshape(1)
    tables = tree_tables(row_scalar, lengths, accepted, parents)
    cache = jnp.swapaxes(latent_cache, 1, 2)
    weights = (
        input_gain[None],
        query_weight,
        latent_weight.T,
        latent_gain[None],
        key_absorb,
        value_absorb,
        output_weight,
    )
    own_keep, own_send, accepted_latents = attention_part(
        True, 0, row_scalar, (hidden, near), cache, tables, weights
    )
    far = after(far, own_send)
    far_near = swap(far, "row", n_row, 1)
    far_keep, far_send = attention_part(
        False, 2, row_scalar, (far, far_near), cache, tables, weights
    )

    def fold(keep, sent):
        return keep + swap(sent, "row", n_row, 1).astype(jnp.float32)

    from_far = swap(fold(far_keep, far_send).astype(bf16), "row", n_row, 2)
    partial = fold(own_keep, own_send) + from_far.astype(jnp.float32)
    partial, arrived = col_parts(partial, n_col)
    named = (routes[:, :, None] == jnp.arange(EXTRA, dtype=jnp.int32)).any(axis=1).astype(bf16)
    residual, block = joined(hidden, partial, arrived, post_gain[None], named)

    own_expert = jnp.arange(experts, dtype=jnp.int32) == req_index * n_row + row_index
    own_expert = own_expert.astype(jnp.float32)[None]
    router = router_weight.T
    routed_weights = (jnp.swapaxes(expert_gate_up[0], 1, 2), expert_down[0])
    shared_weights = (jnp.swapaxes(shared_gate_up, 1, 2), shared_down)
    distances = [0, 1, *range(n_req - 1, 1, -1)]
    blocks = [block]
    for k, s in enumerate(distances[1:], 1):
        source = block if k < 3 else after(block, blocks[k - 2])
        blocks.append(swap(source, "req", n_req, s))
    sends, parts = [], []
    for k, s in enumerate(distances):
        far = swap(after(blocks[k], *sends[: max(0, k - 2)]), "row", n_row, 2)
        near = swap(blocks[k], "row", n_row, 1)
        if k == 0:
            far = after(far, *blocks[1:3])
        elif k > 2:
            far = after(far, *sends, *parts[: k - 1])
        far_near = swap(far, "row", n_row, 1)
        keep, send = expert_part(
            (blocks[k], far, near, far_near),
            own_expert,
            router,
            routed_weights,
            () if s else shared_weights,
        )
        sends.append(send)
        from_near = swap(send, "row", n_row, 1)
        from_far = swap((keep[1] + from_near[1].astype(jnp.float32)).astype(bf16), "row", n_row, 2)
        part = keep[0] + from_near[0].astype(jnp.float32) + from_far.astype(jnp.float32)
        parts.append(part.astype(bf16) if s else part)
    total = parts[0]
    for s, part in zip(distances[1:], parts[1:]):
        total = total + swap(part, "req", n_req, s).astype(jnp.float32)
    total, arrived = col_parts(total, n_col)
    layer_output = residual + (total.astype(jnp.float32) + sum_up(arrived))
    return (layer_output.astype(bf16), accepted_latents)


def sum_up(parts):
    return jnp.sum(parts.astype(jnp.float32), axis=0)


def col_parts(values, n_col):
    bits = 1
    while 2 * bits < n_col:
        sent = values.astype(jnp.bfloat16)
        values = sent.astype(jnp.float32) + swap(sent, "col", n_col, bits).astype(jnp.float32)
        bits *= 2
    sent = values.astype(jnp.bfloat16)
    return sent, swap(sent, "col", n_col, bits)[None]


def solution(mesh):
    placed = (
        P(("req", "row"), None),
        P("req", None, None),
        P("req"),
        P("req", None),
        P(("req", "row"), None),
        P(("req", "row")),
        P(),
        P(None, ("row", "col")),
        P(),
        P(),
        P(("row", "col"), None, None),
        P(("row", "col"), None, None),
        P(("row", "col"), None),
        P(),
        P(),
        P(None, None, ("row", "col")),
        P(("row", "col"), None),
        P(("req", "row"), None, None, "col"),
        P(("req", "row"), "col", None),
    )
    sizes = (mesh.shape["req"], mesh.shape["row"], mesh.shape["col"])
    return jax.shard_map(
        functools.partial(body, sizes),
        mesh=mesh,
        in_specs=placed,
        out_specs=(P(("req", "row"), None), P(("req", "row"), None, None)),
        check_vma=False,
    )
```

```python
import functools
import math

import jax
import jax.numpy as jnp
from jax import lax
from jax.experimental import pallas as pl
from jax.experimental.pallas import tpu as pltpu
from jax.sharding import PartitionSpec as P

NOPE = 128
ROPE = 64
LAT = 512
VDIM = 128
CACHE = 384
WINDOW = 160
SINK = 4


EPSILON = 1e-06
EXTRA = 128
CHUNKS = 4


def rms_scale(values, gain_row):
    mean_square = jnp.mean(values * values, axis=-1, keepdims=True)
    return values * lax.rsqrt(mean_square + EPSILON) * gain_row


def rotate(values, cosine, sine_part):
    half_width = values.shape[-1] // 2
    first_half = values[..., :half_width]
    second_half = values[..., half_width:]
    return jnp.concatenate(
        [
            first_half * cosine - second_half * sine_part,
            second_half * cosine + first_half * sine_part,
        ],
        axis=-1,
    )


def dot(values, weight):
    return jnp.dot(values, weight, preferred_element_type=jnp.float32)


def transposed_dot(values, weight):
    return lax.dot_general(
        values, weight, (((1,), (1,)), ((), ())), preferred_element_type=jnp.float32
    )


WHOLE = pl.BlockSpec(memory_space=pltpu.VMEM)
SCALARS = pl.BlockSpec(memory_space=pltpu.SMEM)


SMALL = pl.CostEstimate(flops=1, bytes_accessed=1, transcendentals=0)
LONG = pl.CostEstimate(flops=20000000000, bytes_accessed=1, transcendentals=0)
LONGER = pl.CostEstimate(flops=30000000000, bytes_accessed=1, transcendentals=0)


def params(megabytes):
    return pltpu.CompilerParams(vmem_limit_bytes=megabytes << 20)


def tree_kernel(
    row_ref, lengths_ref, accepted_ref, parents_ref, closure_ref, turns_ref, places_ref, expert_ref
):
    requests, size, _ = closure_ref.shape
    expert_ids = lax.broadcasted_iota(jnp.int32, expert_ref.shape, 1)
    expert_ref[...] = (expert_ids == row_ref[1]).astype(jnp.float32)
    down = lax.broadcasted_iota(jnp.int32, (size, size), 0)
    across = lax.broadcasted_iota(jnp.int32, (size, size), 1)
    eye = (down == across).astype(jnp.bfloat16)
    closures = []
    for k in range(requests):
        parent_row = parents_ref[pl.ds(row_ref[0] ^ k, 1), :]
        links = (parent_row == down).astype(jnp.bfloat16) + eye
        closures.append(
            lax.dot_general(
                links, eye, (((0,), (0,)), ((), ())), preferred_element_type=jnp.float32
            )
        )
    for repeat in range(max(1, (size - 1).bit_length())):
        narrow = [closure.astype(jnp.bfloat16) for closure in closures]
        closures = [jnp.minimum(dot(each, each), 1.0) for each in narrow]
    step = -2.0 * math.log(10000.0) / ROPE
    frequency = jnp.exp(
        lax.broadcasted_iota(jnp.int32, (size, ROPE // 2), 1).astype(jnp.float32) * step
    )
    for k in range(requests):
        closure_ref[k] = closures[k]
        depth = jnp.sum(closures[k], axis=-1, keepdims=True) - 1.0
        length = lengths_ref[row_ref[0] ^ k].astype(jnp.float32)
        angles = (length + depth) * frequency
        turns_ref[k, :, : ROPE // 2] = jnp.cos(angles)
        turns_ref[k, :, ROPE // 2 : ROPE] = jnp.sin(angles)
        turns_ref[k, :, ROPE : ROPE + 1] = jnp.full((size, 1), length)
    own = closures[0].astype(jnp.bfloat16)
    depth_row = transposed_dot(jnp.ones((8, size), jnp.bfloat16), own)[:1] - 1.0
    chosen = (lax.broadcasted_iota(jnp.int32, (size, 1), 0) == accepted_ref[0]).astype(jnp.float32)
    path_mask = jnp.sum(chosen * closures[0], axis=0, keepdims=True)
    places_ref[...] = jnp.where(
        depth_row == down.astype(jnp.float32), path_mask, 0.0
    ).astype(jnp.bfloat16)


def tree_tables(indices, lengths, accepted, parents, experts):
    requests, size = parents.shape
    return pl.pallas_call(
        tree_kernel,
        out_shape=(
            jax.ShapeDtypeStruct((requests, size, size), jnp.float32),
            jax.ShapeDtypeStruct((requests, size, ROPE + 1), jnp.float32),
            jax.ShapeDtypeStruct((size, size), jnp.bfloat16),
            jax.ShapeDtypeStruct((1, experts), jnp.float32),
        ),
        in_specs=[SCALARS, SCALARS, SCALARS, WHOLE],
        out_specs=(WHOLE, WHOLE, WHOLE, WHOLE),
        compiler_params=params(16),
        cost_estimate=LONG,
        name="trees",
    )(indices, lengths, accepted, parents)


def attention_kernel(first, place, row_ref, *refs):
    (
        first_ref,
        second_ref,
        cache_ref,
        closure_ref,
        turns_ref,
        places_ref,
        gain_ref,
        query_ref,
        latent_ref,
        latent_gain_ref,
        key_ref,
        value_ref,
        output_ref,
        keep_ref,
        send_ref,
    ) = refs[:15]
    size = first_ref.shape[0]
    heads = key_ref.shape[0]
    bf16 = jnp.bfloat16
    scale_factor = 1.0 / math.sqrt(NOPE + ROPE)
    rows = jnp.concatenate([first_ref[...], second_ref[...]], axis=0).astype(jnp.float32)
    rows = rms_scale(rows, gain_ref[...]).astype(bf16)
    turns = jnp.concatenate([turns_ref[place], turns_ref[place + 1]], axis=0)
    cosine, sine_part = turns[:, : ROPE // 2], turns[:, ROPE // 2 : ROPE]
    projected = transposed_dot(rows, latent_ref[...])
    content = rms_scale(projected[:, :LAT], latent_gain_ref[...]).astype(bf16)
    key_rope = rotate(projected[:, LAT:], cosine, sine_part).astype(bf16)
    if first:
        accepted_ref = refs[15]
        accepted_ref[0, :, :LAT] = dot(places_ref[...], content[:size]).astype(bf16)
        accepted_ref[0, :, LAT:] = dot(places_ref[...], key_rope[:size]).astype(bf16)
    queries = dot(rows, query_ref[...])
    query_latent, query_rope = [], []
    for h in range(heads):
        start = h * (NOPE + ROPE)
        query_latent.append(
            dot(queries[:, start : start + NOPE].astype(bf16), key_ref[h]).astype(bf16)
        )
        turned = queries[:, start + NOPE : start + NOPE + ROPE].astype(bf16).astype(jnp.float32)
        query_rope.append(rotate(turned, cosine, sine_part).astype(bf16))
    outs = [[], []]
    for r in range(2):
        spot = row_ref[0] ^ (place + r)
        part = slice(r * size, (r + 1) * size)
        latent_rows = jnp.concatenate([each[part] for each in query_latent], axis=0)
        rope_rows = jnp.concatenate([each[part] for each in query_rope], axis=0)
        old = dot(latent_rows, cache_ref[spot, :LAT, :]) + dot(rope_rows, cache_ref[spot, LAT:, :])
        new = transposed_dot(latent_rows, content[part]) + transposed_dot(rope_rows, key_rope[part])
        length = jnp.concatenate([turns_ref[place + r, :, ROPE : ROPE + 1]] * heads, axis=0)
        spots = lax.broadcasted_iota(jnp.int32, old.shape, 1).astype(jnp.float32)
        allowed = (spots < length) & ((spots < SINK) | (spots >= length - WINDOW))
        related = jnp.concatenate([closure_ref[place + r]] * heads, axis=0) > 0.5
        old = jnp.where(allowed, old * scale_factor, -1e30)
        new = jnp.where(related, new * scale_factor, -1e30)
        peak = jnp.maximum(
            jnp.max(old, axis=-1, keepdims=True), jnp.max(new, axis=-1, keepdims=True)
        )
        old = jnp.exp(old - peak)
        new = jnp.exp(new - peak)
        total = jnp.sum(old, axis=-1, keepdims=True) + jnp.sum(new, axis=-1, keepdims=True)
        old = (old / total).astype(bf16)
        new = (new / total).astype(bf16)
        mixed = transposed_dot(old, cache_ref[spot, :LAT, :]) + dot(new, content[part])
        for h in range(heads):
            outs[r].append(mixed[h * size : (h + 1) * size].astype(bf16))
    head_rows = [
        dot(jnp.concatenate([outs[0][h], outs[1][h]], axis=0), value_ref[h]).astype(bf16)
        for h in range(heads)
    ]
    head_rows = jnp.concatenate(head_rows, axis=1)
    partial = dot(head_rows, output_ref[...])
    keep_ref[...] = partial[:size]
    send_ref[...] = partial[size:].astype(bf16)


def attention_part(first, place, row_index, blocks, cache, tables, weights):
    size, width = blocks[0].shape
    out_shape = [
        jax.ShapeDtypeStruct((size, width), jnp.float32),
        jax.ShapeDtypeStruct((size, width), jnp.bfloat16),
    ]
    if first:
        out_shape.append(jax.ShapeDtypeStruct((1, size, LAT + ROPE), jnp.bfloat16))
    return pl.pallas_call(
        functools.partial(attention_kernel, first, place),
        out_shape=tuple(out_shape),
        in_specs=[SCALARS] + [WHOLE] * 13,
        out_specs=(WHOLE,) * len(out_shape),
        compiler_params=params(12),
        cost_estimate=SMALL,
        name="attention",
    )(row_index, *blocks, cache, *tables, *weights)


def join_kernel(hidden_ref, keep_ref, arrived_ref, gain_ref, named_ref, residual_ref, block_ref):
    width = hidden_ref.shape[1]
    total = keep_ref[...].astype(jnp.float32)
    for k in range(arrived_ref.shape[0]):
        total = total + arrived_ref[k].astype(jnp.float32)
    residual = hidden_ref[...].astype(jnp.float32) + total
    residual_ref[...] = residual
    block_ref[:, :width] = rms_scale(residual, gain_ref[...]).astype(jnp.bfloat16)
    block_ref[:, width:] = named_ref[...]


def joined(hidden, keep, arrived, gain, named):
    rows, width = hidden.shape
    return pl.pallas_call(
        join_kernel,
        out_shape=(
            jax.ShapeDtypeStruct((rows, width), jnp.float32),
            jax.ShapeDtypeStruct((rows, width + EXTRA), jnp.bfloat16),
        ),
        in_specs=[WHOLE] * 5,
        out_specs=(WHOLE, WHOLE),
        compiler_params=params(16),
        cost_estimate=LONGER,
        name="join",
    )(hidden, keep, arrived, gain, named)


def expert_kernel(shared, *refs):
    blocks, refs = refs[:4], refs[4:]
    own_ref, router_ref, gate_up_ref, down_ref = refs[:4]
    refs = refs[4:]
    if shared:
        shared_gate_up_ref, shared_down_ref = refs[:2]
        refs = refs[2:]
    keep_ref, send_ref = refs
    experts, width = router_ref.shape
    size = blocks[0].shape[0]
    rows = jnp.concatenate([ref[:, :width] for ref in blocks], axis=0)
    named = jnp.concatenate([ref[:, width:] for ref in blocks], axis=0)[:, :experts]
    logits = transposed_dot(rows, router_ref[...])
    raised = jnp.exp(logits - jnp.max(logits, axis=-1, keepdims=True))
    router = raised / jnp.sum(raised, axis=-1, keepdims=True)
    share = jnp.sum(router * named.astype(jnp.float32) * own_ref[...], axis=-1, keepdims=True)

    def inner(weights_ref):
        gate = transposed_dot(rows, weights_ref[0])
        upper = transposed_dot(rows, weights_ref[1])
        return (jax.nn.silu(gate) * upper).astype(jnp.bfloat16)

    routed_inner = inner(gate_up_ref)
    if shared:
        shared_inner = inner(shared_gate_up_ref)
    tile = width // CHUNKS
    for k in range(CHUNKS):
        part = slice(k * tile, (k + 1) * tile)
        result = share * dot(routed_inner, down_ref[:, part])
        if shared:
            result = result + dot(shared_inner, shared_down_ref[:, part])
        keep_ref[:, :, part] = result[: 2 * size].reshape(2, size, tile)
        send_ref[:, :, part] = result[2 * size :].astype(jnp.bfloat16).reshape(2, size, tile)


def expert_part(blocks, own_expert, router, routed_weights, shared_weights=()):
    size = blocks[0].shape[0]
    width = router.shape[1]
    units = sum(each.shape[0] for each in (*routed_weights, *shared_weights) if each.ndim == 2)
    operands = [*blocks, own_expert, router, *routed_weights, *shared_weights]
    return pl.pallas_call(
        functools.partial(expert_kernel, bool(shared_weights)),
        out_shape=(
            jax.ShapeDtypeStruct((2, size, width), jnp.float32),
            jax.ShapeDtypeStruct((2, size, width), jnp.bfloat16),
        ),
        in_specs=[WHOLE] * len(operands),
        out_specs=(WHOLE, WHOLE),
        compiler_params=params(12),
        cost_estimate=SMALL,
        name="experts",
    )(*operands)


def after(values, *others):
    return lax.optimization_barrier((values, *others))[0]


def swap(values, axis, size, bits):
    return lax.ppermute(values, axis, [(i, i ^ bits) for i in range(size)])


def body(
    sizes,
    hidden,
    latent_cache,
    lengths,
    parents,
    routes,
    accepted,
    input_gain,
    query_weight,
    latent_weight,
    latent_gain,
    key_absorb,
    value_absorb,
    output_weight,
    post_gain,
    router_weight,
    shared_gate_up,
    shared_down,
    expert_gate_up,
    expert_down,
):
    n_req, n_row, n_col = sizes
    req_index = lax.axis_index("req")
    row_index = lax.axis_index("row")
    bf16 = jnp.bfloat16

    far = swap(hidden, "row", n_row, 2)
    near = swap(hidden, "row", n_row, 1)

    experts = router_weight.shape[1]
    indices = jnp.stack([row_index, req_index * n_row + row_index]).astype(jnp.int32)
    *tables, own_expert = tree_tables(indices, lengths, accepted, parents, experts)
    cache = jnp.swapaxes(latent_cache, 1, 2)
    weights = (
        input_gain[None],
        query_weight,
        latent_weight.T,
        latent_gain[None],
        key_absorb,
        value_absorb,
        output_weight,
    )
    own_keep, own_send, accepted_latents = attention_part(
        True, 0, indices, (hidden, near), cache, tables, weights
    )
    far = after(far, own_send)
    far_near = swap(far, "row", n_row, 1)
    far_keep, far_send = attention_part(
        False, 2, indices, (far, far_near), cache, tables, weights
    )

    def fold(keep, sent):
        return keep + swap(sent, "row", n_row, 1).astype(jnp.float32)

    from_far = swap(fold(far_keep, far_send).astype(bf16), "row", n_row, 2)
    partial = fold(own_keep, own_send) + from_far.astype(jnp.float32)
    partial, arrived = col_parts(partial, n_col)
    named = (routes[:, :, None] == jnp.arange(EXTRA, dtype=jnp.int32)).any(axis=1).astype(bf16)
    residual, block = joined(hidden, partial, arrived, post_gain[None], named)

    router = router_weight.T
    routed_weights = (jnp.swapaxes(expert_gate_up[0], 1, 2), expert_down[0])
    shared_weights = (jnp.swapaxes(shared_gate_up, 1, 2), shared_down)
    distances = [0, 1, *range(n_req - 1, 1, -1)]
    blocks = [block]
    for k, s in enumerate(distances[1:], 1):
        source = block if k < 3 else after(block, blocks[k - 2])
        blocks.append(swap(source, "req", n_req, s))
    sends, parts = [], []
    for k, s in enumerate(distances):
        far = swap(after(blocks[k], *sends[: max(0, k - 2)]), "row", n_row, 2)
        near = swap(blocks[k], "row", n_row, 1)
        if k == 0:
            far = after(far, *blocks[1:3])
        elif k > 2:
            far = after(far, *sends, *parts[: k - 1])
        far_near = swap(far, "row", n_row, 1)
        keep, send = expert_part(
            (blocks[k], far, near, far_near),
            own_expert,
            router,
            routed_weights,
            () if s else shared_weights,
        )
        sends.append(send)
        from_near = swap(send, "row", n_row, 1)
        from_far = swap((keep[1] + from_near[1].astype(jnp.float32)).astype(bf16), "row", n_row, 2)
        part = keep[0] + from_near[0].astype(jnp.float32) + from_far.astype(jnp.float32)
        parts.append(part.astype(bf16) if s else part)
    total = parts[0]
    for s, part in zip(distances[1:], parts[1:]):
        total = total + swap(part, "req", n_req, s).astype(jnp.float32)
    total, arrived = col_parts(total, n_col)
    layer_output = residual + (total.astype(jnp.float32) + sum_up(arrived))
    return (layer_output.astype(bf16), accepted_latents)


def sum_up(parts):
    return jnp.sum(parts.astype(jnp.float32), axis=0)


def col_parts(values, n_col):
    bits = 1
    while 2 * bits < n_col:
        sent = values.astype(jnp.bfloat16)
        values = sent.astype(jnp.float32) + swap(sent, "col", n_col, bits).astype(jnp.float32)
        bits *= 2
    sent = values.astype(jnp.bfloat16)
    return sent, swap(sent, "col", n_col, bits)[None]


def solution(mesh):
    placed = (
        P(("req", "row"), None),
        P("req", None, None),
        P("req"),
        P("req", None),
        P(("req", "row"), None),
        P(("req", "row")),
        P(),
        P(None, ("row", "col")),
        P(),
        P(),
        P(("row", "col"), None, None),
        P(("row", "col"), None, None),
        P(("row", "col"), None),
        P(),
        P(),
        P(None, None, ("row", "col")),
        P(("row", "col"), None),
        P(("req", "row"), None, None, "col"),
        P(("req", "row"), "col", None),
    )
    sizes = (mesh.shape["req"], mesh.shape["row"], mesh.shape["col"])
    return jax.shard_map(
        functools.partial(body, sizes),
        mesh=mesh,
        in_specs=placed,
        out_specs=(P(("req", "row"), None), P(("req", "row"), None, None)),
        check_vma=False,
    )
```

```python
import functools
import math

import jax
import jax.numpy as jnp
from jax import lax
from jax.experimental import pallas as pl
from jax.experimental.pallas import tpu as pltpu
from jax.sharding import PartitionSpec as P

NOPE = 128
ROPE = 64
LAT = 512
VDIM = 128
CACHE = 384
WINDOW = 160
SINK = 4


EPSILON = 1e-06
EXTRA = 128
CHUNKS = 4


def rms_scale(values, gain_row):
    mean_square = jnp.mean(values * values, axis=-1, keepdims=True)
    return values * lax.rsqrt(mean_square + EPSILON) * gain_row


def rotate(values, cosine, sine_part):
    half_width = values.shape[-1] // 2
    first_half = values[..., :half_width]
    second_half = values[..., half_width:]
    return jnp.concatenate(
        [
            first_half * cosine - second_half * sine_part,
            second_half * cosine + first_half * sine_part,
        ],
        axis=-1,
    )


def dot(values, weight):
    return jnp.dot(values, weight, preferred_element_type=jnp.float32)


def transposed_dot(values, weight):
    return lax.dot_general(
        values, weight, (((1,), (1,)), ((), ())), preferred_element_type=jnp.float32
    )


WHOLE = pl.BlockSpec(memory_space=pltpu.VMEM)
SCALARS = pl.BlockSpec(memory_space=pltpu.SMEM)


SMALL = pl.CostEstimate(flops=1, bytes_accessed=1, transcendentals=0)
LONG = pl.CostEstimate(flops=20000000000, bytes_accessed=1, transcendentals=0)
LONGER = pl.CostEstimate(flops=30000000000, bytes_accessed=1, transcendentals=0)


def params(megabytes):
    return pltpu.CompilerParams(vmem_limit_bytes=megabytes << 20)


def tree_kernel(
    row_ref, lengths_ref, accepted_ref, parents_ref, closure_ref, turns_ref, places_ref, expert_ref
):
    requests, size, _ = closure_ref.shape
    expert_ids = lax.broadcasted_iota(jnp.int32, expert_ref.shape, 1)
    expert_ref[...] = (expert_ids == row_ref[1]).astype(jnp.float32)
    down = lax.broadcasted_iota(jnp.int32, (size, size), 0)
    across = lax.broadcasted_iota(jnp.int32, (size, size), 1)
    eye = (down == across).astype(jnp.bfloat16)
    closures = []
    for k in range(requests):
        parent_row = parents_ref[pl.ds(row_ref[0] ^ k, 1), :]
        links = (parent_row == down).astype(jnp.bfloat16) + eye
        closures.append(
            lax.dot_general(
                links, eye, (((0,), (0,)), ((), ())), preferred_element_type=jnp.float32
            )
        )
    for repeat in range(max(1, (size - 1).bit_length())):
        narrow = [closure.astype(jnp.bfloat16) for closure in closures]
        closures = [jnp.minimum(dot(each, each), 1.0) for each in narrow]
    step = -2.0 * math.log(10000.0) / ROPE
    frequency = jnp.exp(
        lax.broadcasted_iota(jnp.int32, (size, ROPE // 2), 1).astype(jnp.float32) * step
    )
    for k in range(requests):
        closure_ref[k] = closures[k]
        depth = jnp.sum(closures[k], axis=-1, keepdims=True) - 1.0
        length = lengths_ref[row_ref[0] ^ k].astype(jnp.float32)
        angles = (length + depth) * frequency
        turns_ref[k, :, : ROPE // 2] = jnp.cos(angles)
        turns_ref[k, :, ROPE // 2 : ROPE] = jnp.sin(angles)
        turns_ref[k, :, ROPE : ROPE + 1] = jnp.full((size, 1), length)
    own = closures[0].astype(jnp.bfloat16)
    depth_row = transposed_dot(jnp.ones((8, size), jnp.bfloat16), own)[:1] - 1.0
    chosen = (lax.broadcasted_iota(jnp.int32, (size, 1), 0) == accepted_ref[0]).astype(jnp.float32)
    path_mask = jnp.sum(chosen * closures[0], axis=0, keepdims=True)
    places_ref[...] = jnp.where(
        depth_row == down.astype(jnp.float32), path_mask, 0.0
    ).astype(jnp.bfloat16)


def tree_tables(indices, lengths, accepted, parents, experts):
    requests, size = parents.shape
    return pl.pallas_call(
        tree_kernel,
        out_shape=(
            jax.ShapeDtypeStruct((requests, size, size), jnp.float32),
            jax.ShapeDtypeStruct((requests, size, ROPE + 1), jnp.float32),
            jax.ShapeDtypeStruct((size, size), jnp.bfloat16),
            jax.ShapeDtypeStruct((1, experts), jnp.float32),
        ),
        in_specs=[SCALARS, SCALARS, SCALARS, WHOLE],
        out_specs=(WHOLE, WHOLE, WHOLE, WHOLE),
        compiler_params=params(16),
        cost_estimate=LONG,
        name="trees",
    )(indices, lengths, accepted, parents)


def attention_kernel(first, place, row_ref, *refs):
    (
        first_ref,
        second_ref,
        cache_ref,
        closure_ref,
        turns_ref,
        places_ref,
        gain_ref,
        query_ref,
        latent_ref,
        latent_gain_ref,
        key_ref,
        value_ref,
        output_ref,
        keep_ref,
        send_ref,
    ) = refs[:15]
    size = first_ref.shape[0]
    heads = key_ref.shape[0]
    bf16 = jnp.bfloat16
    scale_factor = 1.0 / math.sqrt(NOPE + ROPE)
    rows = jnp.concatenate([first_ref[...], second_ref[...]], axis=0).astype(jnp.float32)
    rows = rms_scale(rows, gain_ref[...]).astype(bf16)
    turns = jnp.concatenate([turns_ref[place], turns_ref[place + 1]], axis=0)
    cosine, sine_part = turns[:, : ROPE // 2], turns[:, ROPE // 2 : ROPE]
    projected = transposed_dot(rows, latent_ref[...])
    content = rms_scale(projected[:, :LAT], latent_gain_ref[...]).astype(bf16)
    key_rope = rotate(projected[:, LAT:], cosine, sine_part).astype(bf16)
    if first:
        accepted_ref = refs[15]
        accepted_ref[0, :, :LAT] = dot(places_ref[...], content[:size]).astype(bf16)
        accepted_ref[0, :, LAT:] = dot(places_ref[...], key_rope[:size]).astype(bf16)
    queries = dot(rows, query_ref[...])
    query_latent, query_rope = [], []
    for h in range(heads):
        start = h * (NOPE + ROPE)
        query_latent.append(
            dot(queries[:, start : start + NOPE].astype(bf16), key_ref[h]).astype(bf16)
        )
        turned = queries[:, start + NOPE : start + NOPE + ROPE].astype(bf16).astype(jnp.float32)
        query_rope.append(rotate(turned, cosine, sine_part).astype(bf16))
    outs = [[], []]
    for r in range(2):
        spot = row_ref[0] ^ (place + r)
        part = slice(r * size, (r + 1) * size)
        latent_rows = jnp.concatenate([each[part] for each in query_latent], axis=0)
        rope_rows = jnp.concatenate([each[part] for each in query_rope], axis=0)
        old = dot(latent_rows, cache_ref[spot, :LAT, :]) + dot(rope_rows, cache_ref[spot, LAT:, :])
        new = transposed_dot(latent_rows, content[part]) + transposed_dot(rope_rows, key_rope[part])
        length = jnp.concatenate([turns_ref[place + r, :, ROPE : ROPE + 1]] * heads, axis=0)
        spots = lax.broadcasted_iota(jnp.int32, old.shape, 1).astype(jnp.float32)
        allowed = (spots < length) & ((spots < SINK) | (spots >= length - WINDOW))
        related = jnp.concatenate([closure_ref[place + r]] * heads, axis=0) > 0.5
        old = jnp.where(allowed, old * scale_factor, -1e30)
        new = jnp.where(related, new * scale_factor, -1e30)
        peak = jnp.maximum(
            jnp.max(old, axis=-1, keepdims=True), jnp.max(new, axis=-1, keepdims=True)
        )
        old = jnp.exp(old - peak)
        new = jnp.exp(new - peak)
        total = jnp.sum(old, axis=-1, keepdims=True) + jnp.sum(new, axis=-1, keepdims=True)
        old = (old / total).astype(bf16)
        new = (new / total).astype(bf16)
        mixed = transposed_dot(old, cache_ref[spot, :LAT, :]) + dot(new, content[part])
        for h in range(heads):
            outs[r].append(mixed[h * size : (h + 1) * size].astype(bf16))
    head_rows = [
        dot(jnp.concatenate([outs[0][h], outs[1][h]], axis=0), value_ref[h]).astype(bf16)
        for h in range(heads)
    ]
    head_rows = jnp.concatenate(head_rows, axis=1)
    partial = dot(head_rows, output_ref[...])
    keep_ref[...] = partial[:size]
    send_ref[...] = partial[size:].astype(bf16)


def attention_part(first, place, row_index, blocks, cache, tables, weights):
    size, width = blocks[0].shape
    out_shape = [
        jax.ShapeDtypeStruct((size, width), jnp.float32),
        jax.ShapeDtypeStruct((size, width), jnp.bfloat16),
    ]
    if first:
        out_shape.append(jax.ShapeDtypeStruct((1, size, LAT + ROPE), jnp.bfloat16))
    return pl.pallas_call(
        functools.partial(attention_kernel, first, place),
        out_shape=tuple(out_shape),
        in_specs=[SCALARS] + [WHOLE] * 13,
        out_specs=(WHOLE,) * len(out_shape),
        compiler_params=params(12),
        cost_estimate=SMALL,
        name="attention",
    )(row_index, *blocks, cache, *tables, *weights)


def join_kernel(
    row_ref,
    hidden_ref,
    keep_ref,
    arrived_ref,
    gain_ref,
    named_ref,
    residual_ref,
    block_ref,
    own_ref,
):
    total = keep_ref[...].astype(jnp.float32)
    for k in range(arrived_ref.shape[0]):
        total = total + arrived_ref[k].astype(jnp.float32)
    residual = hidden_ref[...].astype(jnp.float32) + total
    parts, _, part_width = residual_ref.shape
    normed = rms_scale(residual, gain_ref[...]).astype(jnp.bfloat16)
    for k in range(parts):
        part = slice(k * part_width, (k + 1) * part_width)
        residual_ref[k ^ row_ref[2]] = residual[:, part]
        block_ref[k ^ row_ref[2], :, :part_width] = normed[:, part]
        block_ref[k, :, part_width:] = named_ref[...]
    own_ref[...] = block_ref[:1]


def joined(indices, parts, hidden, keep, arrived, gain, named):
    rows, width = hidden.shape
    block_width = width // parts + EXTRA
    return pl.pallas_call(
        join_kernel,
        out_shape=(
            jax.ShapeDtypeStruct((parts, rows, width // parts), jnp.float32),
            jax.ShapeDtypeStruct((parts, rows, block_width), jnp.bfloat16),
            jax.ShapeDtypeStruct((1, rows, block_width), jnp.bfloat16),
        ),
        in_specs=[SCALARS] + [WHOLE] * 5,
        out_specs=(WHOLE, WHOLE, WHOLE),
        compiler_params=params(16),
        cost_estimate=LONGER,
        name="join",
    )(indices, hidden, keep, arrived, gain, named)


def finish_kernel(row_ref, own_ref, others_ref, out_ref):
    parts, _, width = others_ref.shape
    for k in range(parts + 1):
        values = own_ref[...] if k == 0 else others_ref[k - 1]
        start = pl.multiple_of((row_ref[2] ^ k) * width, 128)
        out_ref[:, pl.ds(start, width)] = values


def finished(indices, own, others):
    rows, width = own.shape
    return pl.pallas_call(
        finish_kernel,
        out_shape=jax.ShapeDtypeStruct((rows, width * (1 + others.shape[0])), own.dtype),
        in_specs=[SCALARS, WHOLE, WHOLE],
        out_specs=WHOLE,
        compiler_params=params(12),
        name="finish",
    )(indices, own, others)


def expert_kernel(shared, far_first, *refs):
    row_ref, blocks, refs = refs[0], refs[1:5], refs[5:]
    own_ref, router_ref, gate_up_ref, down_ref = refs[:4]
    refs = refs[4:]
    if shared:
        shared_gate_up_ref, shared_down_ref = refs[:2]
        refs = refs[2:]
    keep_ref, send_ref, rows_ref = refs
    experts, width = router_ref.shape
    parts, size, _ = blocks[0].shape
    part_width = width // parts
    for b, ref in enumerate(blocks):
        for k in range(parts):
            start = pl.multiple_of((k ^ row_ref[2]) * part_width, 128)
            rows_ref[b * size : (b + 1) * size, pl.ds(start, part_width)] = ref[k, :, :part_width]
    rows = rows_ref[...]
    named = jnp.concatenate([ref[0, :, part_width:] for ref in blocks], axis=0)[:, :experts]
    logits = transposed_dot(rows, router_ref[...])
    raised = jnp.exp(logits - jnp.max(logits, axis=-1, keepdims=True))
    router = raised / jnp.sum(raised, axis=-1, keepdims=True)
    share = jnp.sum(router * named.astype(jnp.float32) * own_ref[...], axis=-1, keepdims=True)

    def inner(weights_ref):
        gate = transposed_dot(rows, weights_ref[0])
        upper = transposed_dot(rows, weights_ref[1])
        return (jax.nn.silu(gate) * upper).astype(jnp.bfloat16)

    routed_inner = inner(gate_up_ref)
    if shared:
        shared_inner = inner(shared_gate_up_ref)
    tile = width // CHUNKS
    for k in range(CHUNKS):
        part = slice(k * tile, (k + 1) * tile)
        result = share * dot(routed_inner, down_ref[:, part])
        if shared:
            result = result + dot(shared_inner, shared_down_ref[:, part])
        place = (k * tile // part_width) ^ row_ref[2]
        inside = slice(k * tile % part_width, k * tile % part_width + tile)
        spot = (slice(None), place) if far_first else (place, slice(None))
        spot = (*spot, slice(None), inside)
        keep_ref[spot] = result[: 2 * size].reshape(2, size, tile)
        send_ref[spot] = result[2 * size :].astype(jnp.bfloat16).reshape(2, size, tile)


def expert_part(
    indices, parts, far_first, blocks, own_expert, router, routed_weights, shared_weights=()
):
    size = blocks[0].shape[1]
    width = router.shape[1]
    units = sum(each.shape[0] for each in (*routed_weights, *shared_weights) if each.ndim == 2)
    out_shape = (*((2, parts) if far_first else (parts, 2)), size, width // parts)
    operands = [indices, *blocks, own_expert, router, *routed_weights, *shared_weights]
    return pl.pallas_call(
        functools.partial(expert_kernel, bool(shared_weights), far_first),
        out_shape=(
            jax.ShapeDtypeStruct(out_shape, jnp.float32),
            jax.ShapeDtypeStruct(out_shape, jnp.bfloat16),
        ),
        in_specs=[SCALARS] + [WHOLE] * (len(operands) - 1),
        out_specs=(WHOLE, WHOLE),
        scratch_shapes=[pltpu.VMEM((4 * size, width), jnp.bfloat16)],
        compiler_params=params(12),
        cost_estimate=SMALL,
        name="experts",
    )(*operands)


def after(values, *others):
    return lax.optimization_barrier((values, *others))[0]


def swap(values, axis, size, bits):
    return lax.ppermute(values, axis, [(i, i ^ bits) for i in range(size)])


def body(
    sizes,
    hidden,
    latent_cache,
    lengths,
    parents,
    routes,
    accepted,
    input_gain,
    query_weight,
    latent_weight,
    latent_gain,
    key_absorb,
    value_absorb,
    output_weight,
    post_gain,
    router_weight,
    shared_gate_up,
    shared_down,
    expert_gate_up,
    expert_down,
):
    n_req, n_row, n_col = sizes
    req_index = lax.axis_index("req")
    row_index = lax.axis_index("row")
    bf16 = jnp.bfloat16

    far = swap(hidden, "row", n_row, 2)
    near = swap(hidden, "row", n_row, 1)

    experts = router_weight.shape[1]
    indices = jnp.stack([row_index, req_index * n_row + row_index, lax.axis_index("col")]).astype(jnp.int32)
    *tables, own_expert = tree_tables(indices, lengths, accepted, parents, experts)
    cache = jnp.swapaxes(latent_cache, 1, 2)
    weights = (
        input_gain[None],
        query_weight,
        latent_weight.T,
        latent_gain[None],
        key_absorb,
        value_absorb,
        output_weight,
    )
    own_keep, own_send, accepted_latents = attention_part(
        True, 0, indices, (hidden, near), cache, tables, weights
    )
    far = after(far, own_send)
    far_near = swap(far, "row", n_row, 1)
    far_keep, far_send = attention_part(
        False, 2, indices, (far, far_near), cache, tables, weights
    )

    def fold(keep, sent):
        return keep + swap(sent, "row", n_row, 1).astype(jnp.float32)

    from_far = swap(fold(far_keep, far_send).astype(bf16), "row", n_row, 2)
    partial = fold(own_keep, own_send) + from_far.astype(jnp.float32)
    partial, arrived = col_parts(partial, n_col)
    named = (routes[:, :, None] == jnp.arange(EXTRA, dtype=jnp.int32)).any(axis=1).astype(bf16)
    residual, block, own_part = joined(indices, n_col, hidden, partial, arrived, post_gain[None], named)

    router = router_weight.T
    routed_weights = (jnp.swapaxes(expert_gate_up[0], 1, 2), expert_down[0])
    shared_weights = (jnp.swapaxes(shared_gate_up, 1, 2), shared_down)
    distances = [0, 1, *range(n_req - 1, 1, -1)]
    blocks = [block, swap(block, "req", n_req, 1)]
    fars = [swap(each, "row", n_row, 2) for each in blocks]
    rest = [swap(own_part, "req", n_req, s) for s in distances[2:]]
    if rest:
        rest = after(jnp.concatenate(rest, axis=0)[None], fars[0], blocks[1])
        rest_far = swap(rest, "row", n_row, 2)
        rest, rest_far = col_gather(rest, n_col), col_gather(rest_far, n_col)
        blocks += [rest[:, k] for k in range(rest.shape[1])]
        fars += [rest_far[:, k] for k in range(rest.shape[1])]
    sends, folds, parts = [], [], []
    for k, s in enumerate(distances):
        near = swap(blocks[k], "row", n_row, 1)
        far = fars[k]
        if k > 1:
            far = after(far, *sends, *folds[: k - 1])
        elif k == 1:
            far = after(far, *sends)
        far_near = swap(far, "row", n_row, 1)
        keep, send = expert_part(
            indices,
            n_col,
            k < 3,
            (blocks[k], far, near, far_near),
            own_expert,
            router,
            routed_weights,
            () if s else shared_weights,
        )
        sends.append(send)
        near_sum = keep + swap(send, "row", n_row, 1).astype(jnp.float32)
        if k < 3:
            fold = near_sum[1].astype(bf16)
            part = near_sum[0] + swap(fold, "row", n_row, 2).astype(jnp.float32)
            part = col_scatter(part, n_col)[0]
        else:
            fold = near_sum[n_col // 2 :].astype(bf16)
            part = col_scatter(near_sum, n_col)[0]
            part = part[0] + swap(part[1].astype(bf16), "row", n_row, 2).astype(jnp.float32)
        folds.append(fold)
        parts.append(part.astype(bf16) if s else part)
    total = parts[0]
    for s, part in zip(distances[1:], parts[1:]):
        total = total + swap(part, "req", n_req, s).astype(jnp.float32)
    own = (residual[0] + total).astype(bf16)
    others = col_gather(own[None], n_col)
    layer_output = finished(indices, own, others[1:])
    return (layer_output, accepted_latents)


def col_gather(values, n_col):
    bits = 1
    while bits < n_col:
        values = jnp.concatenate([values, swap(values, "col", n_col, bits)], axis=0)
        bits *= 2
    return values


def col_scatter(values, n_col):
    bits = n_col // 2
    while bits:
        received = swap(values[bits:].astype(jnp.bfloat16), "col", n_col, bits)
        values = values[:bits] + received.astype(jnp.float32)
        bits //= 2
    return values


def col_parts(values, n_col):
    bits = 1
    while 2 * bits < n_col:
        sent = values.astype(jnp.bfloat16)
        values = sent.astype(jnp.float32) + swap(sent, "col", n_col, bits).astype(jnp.float32)
        bits *= 2
    sent = values.astype(jnp.bfloat16)
    return sent, swap(sent, "col", n_col, bits)[None]


def solution(mesh):
    placed = (
        P(("req", "row"), None),
        P("req", None, None),
        P("req"),
        P("req", None),
        P(("req", "row"), None),
        P(("req", "row")),
        P(),
        P(None, ("row", "col")),
        P(),
        P(),
        P(("row", "col"), None, None),
        P(("row", "col"), None, None),
        P(("row", "col"), None),
        P(),
        P(),
        P(None, None, ("row", "col")),
        P(("row", "col"), None),
        P(("req", "row"), None, None, "col"),
        P(("req", "row"), "col", None),
    )
    sizes = (mesh.shape["req"], mesh.shape["row"], mesh.shape["col"])
    return jax.shard_map(
        functools.partial(body, sizes),
        mesh=mesh,
        in_specs=placed,
        out_specs=(P(("req", "row"), None), P(("req", "row"), None, None)),
        check_vma=False,
    )
```

```python
import functools
import math

import jax
import jax.numpy as jnp
from jax import lax
from jax.experimental import pallas as pl
from jax.experimental.pallas import tpu as pltpu
from jax.sharding import PartitionSpec as P

NOPE = 128
ROPE = 64
LAT = 512
VDIM = 128
CACHE = 384
WINDOW = 160
SINK = 4


EPSILON = 1e-06
EXTRA = 128
CHUNKS = 4


def rms_scale(values, gain_row):
    mean_square = jnp.mean(values * values, axis=-1, keepdims=True)
    return values * lax.rsqrt(mean_square + EPSILON) * gain_row


def rotate(values, cosine, sine_part):
    half_width = values.shape[-1] // 2
    first_half = values[..., :half_width]
    second_half = values[..., half_width:]
    return jnp.concatenate(
        [
            first_half * cosine - second_half * sine_part,
            second_half * cosine + first_half * sine_part,
        ],
        axis=-1,
    )


def dot(values, weight):
    return jnp.dot(values, weight, preferred_element_type=jnp.float32)


def transposed_dot(values, weight):
    return lax.dot_general(
        values, weight, (((1,), (1,)), ((), ())), preferred_element_type=jnp.float32
    )


WHOLE = pl.BlockSpec(memory_space=pltpu.VMEM)
SCALARS = pl.BlockSpec(memory_space=pltpu.SMEM)


SMALL = pl.CostEstimate(flops=1, bytes_accessed=1, transcendentals=0)
LONG = pl.CostEstimate(flops=20000000000, bytes_accessed=1, transcendentals=0)
LONGER = pl.CostEstimate(flops=30000000000, bytes_accessed=1, transcendentals=0)


def params(megabytes):
    return pltpu.CompilerParams(vmem_limit_bytes=megabytes << 20)


def tree_kernel(
    row_ref, lengths_ref, accepted_ref, parents_ref, closure_ref, turns_ref, places_ref, expert_ref
):
    requests, size, _ = closure_ref.shape
    expert_ids = lax.broadcasted_iota(jnp.int32, expert_ref.shape, 1)
    expert_ref[...] = (expert_ids == row_ref[1]).astype(jnp.float32)
    down = lax.broadcasted_iota(jnp.int32, (size, size), 0)
    across = lax.broadcasted_iota(jnp.int32, (size, size), 1)
    eye = (down == across).astype(jnp.bfloat16)
    closures = []
    for k in range(requests):
        parent_row = parents_ref[pl.ds(row_ref[0] ^ k, 1), :]
        links = (parent_row == down).astype(jnp.bfloat16) + eye
        closures.append(
            lax.dot_general(
                links, eye, (((0,), (0,)), ((), ())), preferred_element_type=jnp.float32
            )
        )
    for repeat in range(max(1, (size - 1).bit_length())):
        narrow = [closure.astype(jnp.bfloat16) for closure in closures]
        closures = [jnp.minimum(dot(each, each), 1.0) for each in narrow]
    step = -2.0 * math.log(10000.0) / ROPE
    frequency = jnp.exp(
        lax.broadcasted_iota(jnp.int32, (size, ROPE // 2), 1).astype(jnp.float32) * step
    )
    for k in range(requests):
        closure_ref[k] = closures[k]
        depth = jnp.sum(closures[k], axis=-1, keepdims=True) - 1.0
        length = lengths_ref[row_ref[0] ^ k].astype(jnp.float32)
        angles = (length + depth) * frequency
        turns_ref[k, :, : ROPE // 2] = jnp.cos(angles)
        turns_ref[k, :, ROPE // 2 : ROPE] = jnp.sin(angles)
        turns_ref[k, :, ROPE : ROPE + 1] = jnp.full((size, 1), length)
    own = closures[0].astype(jnp.bfloat16)
    depth_row = transposed_dot(jnp.ones((8, size), jnp.bfloat16), own)[:1] - 1.0
    chosen = (lax.broadcasted_iota(jnp.int32, (size, 1), 0) == accepted_ref[0]).astype(jnp.float32)
    path_mask = jnp.sum(chosen * closures[0], axis=0, keepdims=True)
    places_ref[...] = jnp.where(
        depth_row == down.astype(jnp.float32), path_mask, 0.0
    ).astype(jnp.bfloat16)


def tree_tables(indices, lengths, accepted, parents, experts):
    requests, size = parents.shape
    return pl.pallas_call(
        tree_kernel,
        out_shape=(
            jax.ShapeDtypeStruct((requests, size, size), jnp.float32),
            jax.ShapeDtypeStruct((requests, size, ROPE + 1), jnp.float32),
            jax.ShapeDtypeStruct((size, size), jnp.bfloat16),
            jax.ShapeDtypeStruct((1, experts), jnp.float32),
        ),
        in_specs=[SCALARS, SCALARS, SCALARS, WHOLE],
        out_specs=(WHOLE, WHOLE, WHOLE, WHOLE),
        compiler_params=params(16),
        cost_estimate=LONG,
        name="trees",
    )(indices, lengths, accepted, parents)


def attention_kernel(first, place, row_ref, *refs):
    (
        first_ref,
        second_ref,
        cache_ref,
        closure_ref,
        turns_ref,
        places_ref,
        gain_ref,
        query_ref,
        latent_ref,
        latent_gain_ref,
        key_ref,
        value_ref,
        output_ref,
        keep_ref,
        send_ref,
    ) = refs[:15]
    size = first_ref.shape[0]
    heads = key_ref.shape[0]
    bf16 = jnp.bfloat16
    scale_factor = 1.0 / math.sqrt(NOPE + ROPE)
    rows = jnp.concatenate([first_ref[...], second_ref[...]], axis=0).astype(jnp.float32)
    rows = rms_scale(rows, gain_ref[...]).astype(bf16)
    turns = jnp.concatenate([turns_ref[place], turns_ref[place + 1]], axis=0)
    cosine, sine_part = turns[:, : ROPE // 2], turns[:, ROPE // 2 : ROPE]
    projected = transposed_dot(rows, latent_ref[...])
    content = rms_scale(projected[:, :LAT], latent_gain_ref[...]).astype(bf16)
    key_rope = rotate(projected[:, LAT:], cosine, sine_part).astype(bf16)
    if first:
        accepted_ref = refs[15]
        accepted_ref[0, :, :LAT] = dot(places_ref[...], content[:size]).astype(bf16)
        accepted_ref[0, :, LAT:] = dot(places_ref[...], key_rope[:size]).astype(bf16)
    queries = dot(rows, query_ref[...])
    query_latent, query_rope = [], []
    for h in range(heads):
        start = h * (NOPE + ROPE)
        query_latent.append(
            dot(queries[:, start : start + NOPE].astype(bf16), key_ref[h]).astype(bf16)
        )
        turned = queries[:, start + NOPE : start + NOPE + ROPE].astype(bf16).astype(jnp.float32)
        query_rope.append(rotate(turned, cosine, sine_part).astype(bf16))
    outs = [[], []]
    for r in range(2):
        spot = row_ref[0] ^ (place + r)
        part = slice(r * size, (r + 1) * size)
        latent_rows = jnp.concatenate([each[part] for each in query_latent], axis=0)
        rope_rows = jnp.concatenate([each[part] for each in query_rope], axis=0)
        old = dot(latent_rows, cache_ref[spot, :LAT, :]) + dot(rope_rows, cache_ref[spot, LAT:, :])
        new = transposed_dot(latent_rows, content[part]) + transposed_dot(rope_rows, key_rope[part])
        length = jnp.concatenate([turns_ref[place + r, :, ROPE : ROPE + 1]] * heads, axis=0)
        spots = lax.broadcasted_iota(jnp.int32, old.shape, 1).astype(jnp.float32)
        allowed = (spots < length) & ((spots < SINK) | (spots >= length - WINDOW))
        related = jnp.concatenate([closure_ref[place + r]] * heads, axis=0) > 0.5
        old = jnp.where(allowed, old * scale_factor, -1e30)
        new = jnp.where(related, new * scale_factor, -1e30)
        peak = jnp.maximum(
            jnp.max(old, axis=-1, keepdims=True), jnp.max(new, axis=-1, keepdims=True)
        )
        old = jnp.exp(old - peak)
        new = jnp.exp(new - peak)
        total = jnp.sum(old, axis=-1, keepdims=True) + jnp.sum(new, axis=-1, keepdims=True)
        old = (old / total).astype(bf16)
        new = (new / total).astype(bf16)
        mixed = transposed_dot(old, cache_ref[spot, :LAT, :]) + dot(new, content[part])
        for h in range(heads):
            outs[r].append(mixed[h * size : (h + 1) * size].astype(bf16))
    head_rows = [
        dot(jnp.concatenate([outs[0][h], outs[1][h]], axis=0), value_ref[h]).astype(bf16)
        for h in range(heads)
    ]
    head_rows = jnp.concatenate(head_rows, axis=1)
    partial = dot(head_rows, output_ref[...])
    keep_ref[...] = partial[:size]
    send_ref[...] = partial[size:].astype(bf16)


def attention_part(first, place, row_index, blocks, cache, tables, weights):
    size, width = blocks[0].shape
    out_shape = [
        jax.ShapeDtypeStruct((size, width), jnp.float32),
        jax.ShapeDtypeStruct((size, width), jnp.bfloat16),
    ]
    if first:
        out_shape.append(jax.ShapeDtypeStruct((1, size, LAT + ROPE), jnp.bfloat16))
    return pl.pallas_call(
        functools.partial(attention_kernel, first, place),
        out_shape=tuple(out_shape),
        in_specs=[SCALARS] + [WHOLE] * 13,
        out_specs=(WHOLE,) * len(out_shape),
        compiler_params=params(12),
        cost_estimate=SMALL,
        name="attention",
    )(row_index, *blocks, cache, *tables, *weights)


def join_kernel(
    row_ref,
    hidden_ref,
    keep_ref,
    arrived_ref,
    gain_ref,
    named_ref,
    residual_ref,
    block_ref,
    own_ref,
):
    total = keep_ref[...].astype(jnp.float32)
    for k in range(arrived_ref.shape[0]):
        total = total + arrived_ref[k].astype(jnp.float32)
    residual = hidden_ref[...].astype(jnp.float32) + total
    parts, _, part_width = residual_ref.shape
    normed = rms_scale(residual, gain_ref[...]).astype(jnp.bfloat16)
    for k in range(parts):
        part = slice(k * part_width, (k + 1) * part_width)
        residual_ref[k ^ row_ref[2]] = residual[:, part]
        block_ref[k ^ row_ref[2], :, :part_width] = normed[:, part]
        block_ref[k, :, part_width:] = named_ref[...]
    own_ref[...] = block_ref[:1]


def joined(indices, parts, hidden, keep, arrived, gain, named):
    rows, width = hidden.shape
    block_width = width // parts + EXTRA
    return pl.pallas_call(
        join_kernel,
        out_shape=(
            jax.ShapeDtypeStruct((parts, rows, width // parts), jnp.float32),
            jax.ShapeDtypeStruct((parts, rows, block_width), jnp.bfloat16),
            jax.ShapeDtypeStruct((1, rows, block_width), jnp.bfloat16),
        ),
        in_specs=[SCALARS] + [WHOLE] * 5,
        out_specs=(WHOLE, WHOLE, WHOLE),
        compiler_params=params(16),
        cost_estimate=LONGER,
        name="join",
    )(indices, hidden, keep, arrived, gain, named)


def finish_kernel(row_ref, own_ref, others_ref, out_ref):
    parts, _, width = others_ref.shape
    for k in range(parts + 1):
        values = own_ref[...] if k == 0 else others_ref[k - 1]
        start = pl.multiple_of((row_ref[2] ^ k) * width, 128)
        out_ref[:, pl.ds(start, width)] = values


def finished(indices, own, others):
    rows, width = own.shape
    return pl.pallas_call(
        finish_kernel,
        out_shape=jax.ShapeDtypeStruct((rows, width * (1 + others.shape[0])), own.dtype),
        in_specs=[SCALARS, WHOLE, WHOLE],
        out_specs=WHOLE,
        compiler_params=params(12),
        name="finish",
    )(indices, own, others)


def expert_kernel(shared, far_first, *refs):
    row_ref, blocks, refs = refs[0], refs[1:5], refs[5:]
    own_ref, router_ref, gate_up_ref, down_ref = refs[:4]
    refs = refs[4:]
    if shared:
        shared_gate_up_ref, shared_down_ref = refs[:2]
        refs = refs[2:]
    keep_ref, send_ref, rows_ref = refs
    experts, width = router_ref.shape
    parts, size, _ = blocks[0].shape
    part_width = width // parts
    for b, ref in enumerate(blocks):
        for k in range(parts):
            start = pl.multiple_of((k ^ row_ref[2]) * part_width, 128)
            rows_ref[b * size : (b + 1) * size, pl.ds(start, part_width)] = ref[k, :, :part_width]
    rows = rows_ref[...]
    named = jnp.concatenate([ref[0, :, part_width:] for ref in blocks], axis=0)[:, :experts]
    logits = transposed_dot(rows, router_ref[...])
    raised = jnp.exp(logits - jnp.max(logits, axis=-1, keepdims=True))
    router = raised / jnp.sum(raised, axis=-1, keepdims=True)
    share = jnp.sum(router * named.astype(jnp.float32) * own_ref[...], axis=-1, keepdims=True)

    def inner(weights_ref):
        gate = transposed_dot(rows, weights_ref[0])
        upper = transposed_dot(rows, weights_ref[1])
        return (jax.nn.silu(gate) * upper).astype(jnp.bfloat16)

    routed_inner = inner(gate_up_ref)
    if shared:
        shared_inner = inner(shared_gate_up_ref)
    tile = width // CHUNKS
    for k in range(CHUNKS):
        part = slice(k * tile, (k + 1) * tile)
        result = share * dot(routed_inner, down_ref[:, part])
        if shared:
            result = result + dot(shared_inner, shared_down_ref[:, part])
        place = (k * tile // part_width) ^ row_ref[2]
        inside = slice(k * tile % part_width, k * tile % part_width + tile)
        spot = (slice(None), place) if far_first else (place, slice(None))
        spot = (*spot, slice(None), inside)
        keep_ref[spot] = result[: 2 * size].reshape(2, size, tile)
        send_ref[spot] = result[2 * size :].astype(jnp.bfloat16).reshape(2, size, tile)


def expert_part(
    indices, parts, far_first, blocks, own_expert, router, routed_weights, shared_weights=()
):
    size = blocks[0].shape[1]
    width = router.shape[1]
    units = sum(each.shape[0] for each in (*routed_weights, *shared_weights) if each.ndim == 2)
    out_shape = (*((2, parts) if far_first else (parts, 2)), size, width // parts)
    operands = [indices, *blocks, own_expert, router, *routed_weights, *shared_weights]
    return pl.pallas_call(
        functools.partial(expert_kernel, bool(shared_weights), far_first),
        out_shape=(
            jax.ShapeDtypeStruct(out_shape, jnp.float32),
            jax.ShapeDtypeStruct(out_shape, jnp.bfloat16),
        ),
        in_specs=[SCALARS] + [WHOLE] * (len(operands) - 1),
        out_specs=(WHOLE, WHOLE),
        scratch_shapes=[pltpu.VMEM((4 * size, width), jnp.bfloat16)],
        compiler_params=params(12),
        cost_estimate=SMALL,
        name="experts",
    )(*operands)


def after(values, *others):
    return lax.optimization_barrier((values, *others))[0]


def swap(values, axis, size, bits):
    return lax.ppermute(values, axis, [(i, i ^ bits) for i in range(size)])


def body(
    sizes,
    hidden,
    latent_cache,
    lengths,
    parents,
    routes,
    accepted,
    input_gain,
    query_weight,
    latent_weight,
    latent_gain,
    key_absorb,
    value_absorb,
    output_weight,
    post_gain,
    router_weight,
    shared_gate_up,
    shared_down,
    expert_gate_up,
    expert_down,
):
    n_req, n_row, n_col = sizes
    req_index = lax.axis_index("req")
    row_index = lax.axis_index("row")
    bf16 = jnp.bfloat16

    far = swap(hidden, "row", n_row, 2)
    near = swap(hidden, "row", n_row, 1)

    experts = router_weight.shape[1]
    indices = jnp.stack([row_index, req_index * n_row + row_index, lax.axis_index("col")]).astype(jnp.int32)
    *tables, own_expert = tree_tables(indices, lengths, accepted, parents, experts)
    cache = jnp.swapaxes(latent_cache, 1, 2)
    weights = (
        input_gain[None],
        query_weight,
        latent_weight.T,
        latent_gain[None],
        key_absorb,
        value_absorb,
        output_weight,
    )
    own_keep, own_send, accepted_latents = attention_part(
        True, 0, indices, (hidden, near), cache, tables, weights
    )
    far = after(far, own_send)
    far_near = swap(far, "row", n_row, 1)
    far_keep, far_send = attention_part(
        False, 2, indices, (far, far_near), cache, tables, weights
    )

    def fold(keep, sent):
        return keep + swap(sent, "row", n_row, 1).astype(jnp.float32)

    from_far = swap(fold(far_keep, far_send).astype(bf16), "row", n_row, 2)
    partial = fold(own_keep, own_send) + from_far.astype(jnp.float32)
    partial, arrived = col_parts(partial, n_col)
    named = (routes[:, :, None] == jnp.arange(EXTRA, dtype=jnp.int32)).any(axis=1).astype(bf16)
    residual, block, own_part = joined(indices, n_col, hidden, partial, arrived, post_gain[None], named)

    router = router_weight.T
    routed_weights = (jnp.swapaxes(expert_gate_up[0], 1, 2), expert_down[0])
    shared_weights = (jnp.swapaxes(shared_gate_up, 1, 2), shared_down)
    distances = [0, 1, *range(n_req - 1, 1, -1)]
    fars = [swap(block, "row", n_row, 2)]
    blocks = [block, swap(after(block, fars[0]), "req", n_req, 1)]
    fars.append(swap(blocks[1], "row", n_row, 2))
    rest = [swap(own_part, "req", n_req, s) for s in distances[2:]]
    if rest:
        rest = after(jnp.concatenate(rest, axis=0)[None], fars[0])
        rest_far = swap(rest, "row", n_row, 2)
        rest, rest_far = col_gather(rest, n_col), col_gather(rest_far, n_col)
        blocks += [rest[:, k] for k in range(rest.shape[1])]
        fars += [rest_far[:, k] for k in range(rest.shape[1])]
    sends, folds, sums, returns = [], [], [], []
    for k, s in enumerate(distances):
        near = swap(blocks[k], "row", n_row, 1)
        far = fars[k]
        if k > 2:
            far = after(far, *sends, *folds, *returns[: k - 2])
        elif k:
            far = after(far, *sends, *folds[: k - 1])
        far_near = swap(far, "row", n_row, 1)
        keep, send = expert_part(
            indices,
            n_col,
            k < 3,
            (blocks[k], far, near, far_near),
            own_expert,
            router,
            routed_weights,
            () if s else shared_weights,
        )
        sends.append(send)
        near_sum = keep + swap(send, "row", n_row, 1).astype(jnp.float32)
        fold = near_sum[1] if k < 3 else near_sum[n_col // 2 :]
        folds.append(fold.astype(bf16))
        sums.append(near_sum)
        if k < 3:
            returns.append(swap(folds[k], "row", n_row, 2))
    parts = []
    last = col_scatter(sums[-1], n_col)[0] if n_req > 3 else None
    for k, near_sum in enumerate(sums):
        if k < 3:
            from_far = after(returns[k], *((), [last], folds[-1:])[k]) if n_req > 3 else returns[k]
            part = col_scatter(near_sum[0] + from_far.astype(jnp.float32), n_col)[0]
        else:
            part = last if k == n_req - 1 else col_scatter(near_sum, n_col)[0]
            part = part[0] + swap(part[1].astype(bf16), "row", n_row, 2).astype(jnp.float32)
        parts.append(part.astype(bf16) if k else part)
    total = parts[0]
    for s, part in zip(distances[1:], parts[1:]):
        total = total + swap(part, "req", n_req, s).astype(jnp.float32)
    own = (residual[0] + total).astype(bf16)
    others = col_gather(own[None], n_col)
    layer_output = finished(indices, own, others[1:])
    return (layer_output, accepted_latents)


def col_gather(values, n_col):
    bits = 1
    while bits < n_col:
        values = jnp.concatenate([values, swap(values, "col", n_col, bits)], axis=0)
        bits *= 2
    return values


def col_scatter(values, n_col):
    bits = n_col // 2
    while bits:
        received = swap(values[bits:].astype(jnp.bfloat16), "col", n_col, bits)
        values = values[:bits] + received.astype(jnp.float32)
        bits //= 2
    return values


def col_parts(values, n_col):
    bits = 1
    while 2 * bits < n_col:
        sent = values.astype(jnp.bfloat16)
        values = sent.astype(jnp.float32) + swap(sent, "col", n_col, bits).astype(jnp.float32)
        bits *= 2
    sent = values.astype(jnp.bfloat16)
    return sent, swap(sent, "col", n_col, bits)[None]


def solution(mesh):
    placed = (
        P(("req", "row"), None),
        P("req", None, None),
        P("req"),
        P("req", None),
        P(("req", "row"), None),
        P(("req", "row")),
        P(),
        P(None, ("row", "col")),
        P(),
        P(),
        P(("row", "col"), None, None),
        P(("row", "col"), None, None),
        P(("row", "col"), None),
        P(),
        P(),
        P(None, None, ("row", "col")),
        P(("row", "col"), None),
        P(("req", "row"), None, None, "col"),
        P(("req", "row"), "col", None),
    )
    sizes = (mesh.shape["req"], mesh.shape["row"], mesh.shape["col"])
    return jax.shard_map(
        functools.partial(body, sizes),
        mesh=mesh,
        in_specs=placed,
        out_specs=(P(("req", "row"), None), P(("req", "row"), None, None)),
        check_vma=False,
    )
```

```python
import functools
import math

import jax
import jax.numpy as jnp
from jax import lax
from jax.experimental import pallas as pl
from jax.experimental.pallas import tpu as pltpu
from jax.sharding import PartitionSpec as P

NOPE = 128
ROPE = 64
LAT = 512
VDIM = 128
CACHE = 384
WINDOW = 160
SINK = 4


EPSILON = 1e-06
EXTRA = 128
CHUNKS = 4


def rms_scale(values, gain_row):
    mean_square = jnp.mean(values * values, axis=-1, keepdims=True)
    return values * lax.rsqrt(mean_square + EPSILON) * gain_row


def rotate(values, cosine, sine_part):
    half_width = values.shape[-1] // 2
    first_half = values[..., :half_width]
    second_half = values[..., half_width:]
    return jnp.concatenate(
        [
            first_half * cosine - second_half * sine_part,
            second_half * cosine + first_half * sine_part,
        ],
        axis=-1,
    )


def dot(values, weight):
    return jnp.dot(values, weight, preferred_element_type=jnp.float32)


def transposed_dot(values, weight):
    return lax.dot_general(
        values, weight, (((1,), (1,)), ((), ())), preferred_element_type=jnp.float32
    )


WHOLE = pl.BlockSpec(memory_space=pltpu.VMEM)
SCALARS = pl.BlockSpec(memory_space=pltpu.SMEM)


SMALL = pl.CostEstimate(flops=1, bytes_accessed=1, transcendentals=0)
LONG = pl.CostEstimate(flops=20000000000, bytes_accessed=1, transcendentals=0)
LONGER = pl.CostEstimate(flops=30000000000, bytes_accessed=1, transcendentals=0)


def params(megabytes):
    return pltpu.CompilerParams(vmem_limit_bytes=megabytes << 20)


def tree_kernel(
    row_ref, lengths_ref, accepted_ref, parents_ref, closure_ref, turns_ref, places_ref, expert_ref
):
    requests, size, _ = closure_ref.shape
    expert_ids = lax.broadcasted_iota(jnp.int32, expert_ref.shape, 1)
    expert_ref[...] = (expert_ids == row_ref[1]).astype(jnp.float32)
    down = lax.broadcasted_iota(jnp.int32, (size, size), 0)
    across = lax.broadcasted_iota(jnp.int32, (size, size), 1)
    eye = (down == across).astype(jnp.bfloat16)
    closures = []
    for k in range(requests):
        parent_row = parents_ref[pl.ds(row_ref[0] ^ k, 1), :]
        links = (parent_row == down).astype(jnp.bfloat16) + eye
        closures.append(
            lax.dot_general(
                links, eye, (((0,), (0,)), ((), ())), preferred_element_type=jnp.float32
            )
        )
    for repeat in range(max(1, (size - 1).bit_length())):
        narrow = [closure.astype(jnp.bfloat16) for closure in closures]
        closures = [jnp.minimum(dot(each, each), 1.0) for each in narrow]
    step = -2.0 * math.log(10000.0) / ROPE
    frequency = jnp.exp(
        lax.broadcasted_iota(jnp.int32, (size, ROPE // 2), 1).astype(jnp.float32) * step
    )
    for k in range(requests):
        closure_ref[k] = closures[k]
        depth = jnp.sum(closures[k], axis=-1, keepdims=True) - 1.0
        length = lengths_ref[row_ref[0] ^ k].astype(jnp.float32)
        angles = (length + depth) * frequency
        turns_ref[k, :, : ROPE // 2] = jnp.cos(angles)
        turns_ref[k, :, ROPE // 2 : ROPE] = jnp.sin(angles)
        turns_ref[k, :, ROPE : ROPE + 1] = jnp.full((size, 1), length)
    own = closures[0].astype(jnp.bfloat16)
    depth_row = transposed_dot(jnp.ones((8, size), jnp.bfloat16), own)[:1] - 1.0
    chosen = (lax.broadcasted_iota(jnp.int32, (size, 1), 0) == accepted_ref[0]).astype(jnp.float32)
    path_mask = jnp.sum(chosen * closures[0], axis=0, keepdims=True)
    places_ref[...] = jnp.where(
        depth_row == down.astype(jnp.float32), path_mask, 0.0
    ).astype(jnp.bfloat16)


def tree_tables(indices, lengths, accepted, parents, experts):
    requests, size = parents.shape
    return pl.pallas_call(
        tree_kernel,
        out_shape=(
            jax.ShapeDtypeStruct((requests, size, size), jnp.float32),
            jax.ShapeDtypeStruct((requests, size, ROPE + 1), jnp.float32),
            jax.ShapeDtypeStruct((size, size), jnp.bfloat16),
            jax.ShapeDtypeStruct((1, experts), jnp.float32),
        ),
        in_specs=[SCALARS, SCALARS, SCALARS, WHOLE],
        out_specs=(WHOLE, WHOLE, WHOLE, WHOLE),
        compiler_params=params(16),
        cost_estimate=LONG,
        name="trees",
    )(indices, lengths, accepted, parents)


def attention_kernel(first, place, row_ref, *refs):
    (
        first_ref,
        second_ref,
        cache_ref,
        closure_ref,
        turns_ref,
        places_ref,
        gain_ref,
        query_ref,
        latent_ref,
        latent_gain_ref,
        key_ref,
        value_ref,
        output_ref,
        keep_ref,
        send_ref,
    ) = refs[:15]
    size = first_ref.shape[0]
    heads = key_ref.shape[0]
    bf16 = jnp.bfloat16
    scale_factor = 1.0 / math.sqrt(NOPE + ROPE)
    rows = jnp.concatenate([first_ref[...], second_ref[...]], axis=0).astype(jnp.float32)
    rows = rms_scale(rows, gain_ref[...]).astype(bf16)
    turns = jnp.concatenate([turns_ref[place], turns_ref[place + 1]], axis=0)
    cosine, sine_part = turns[:, : ROPE // 2], turns[:, ROPE // 2 : ROPE]
    projected = transposed_dot(rows, latent_ref[...])
    content = rms_scale(projected[:, :LAT], latent_gain_ref[...]).astype(bf16)
    key_rope = rotate(projected[:, LAT:], cosine, sine_part).astype(bf16)
    if first:
        accepted_ref = refs[15]
        accepted_ref[0, :, :LAT] = dot(places_ref[...], content[:size]).astype(bf16)
        accepted_ref[0, :, LAT:] = dot(places_ref[...], key_rope[:size]).astype(bf16)
    queries = dot(rows, query_ref[...])
    query_latent, query_rope = [], []
    for h in range(heads):
        start = h * (NOPE + ROPE)
        query_latent.append(
            dot(queries[:, start : start + NOPE].astype(bf16), key_ref[h]).astype(bf16)
        )
        turned = queries[:, start + NOPE : start + NOPE + ROPE].astype(bf16).astype(jnp.float32)
        query_rope.append(rotate(turned, cosine, sine_part).astype(bf16))
    outs = [[], []]
    for r in range(2):
        spot = row_ref[0] ^ (place + r)
        part = slice(r * size, (r + 1) * size)
        latent_rows = jnp.concatenate([each[part] for each in query_latent], axis=0)
        rope_rows = jnp.concatenate([each[part] for each in query_rope], axis=0)
        old = dot(latent_rows, cache_ref[spot, :LAT, :]) + dot(rope_rows, cache_ref[spot, LAT:, :])
        new = transposed_dot(latent_rows, content[part]) + transposed_dot(rope_rows, key_rope[part])
        length = jnp.concatenate([turns_ref[place + r, :, ROPE : ROPE + 1]] * heads, axis=0)
        spots = lax.broadcasted_iota(jnp.int32, old.shape, 1).astype(jnp.float32)
        allowed = (spots < length) & ((spots < SINK) | (spots >= length - WINDOW))
        related = jnp.concatenate([closure_ref[place + r]] * heads, axis=0) > 0.5
        old = jnp.where(allowed, old * scale_factor, -1e30)
        new = jnp.where(related, new * scale_factor, -1e30)
        peak = jnp.maximum(
            jnp.max(old, axis=-1, keepdims=True), jnp.max(new, axis=-1, keepdims=True)
        )
        old = jnp.exp(old - peak)
        new = jnp.exp(new - peak)
        total = jnp.sum(old, axis=-1, keepdims=True) + jnp.sum(new, axis=-1, keepdims=True)
        old = (old / total).astype(bf16)
        new = (new / total).astype(bf16)
        mixed = transposed_dot(old, cache_ref[spot, :LAT, :]) + dot(new, content[part])
        for h in range(heads):
            outs[r].append(mixed[h * size : (h + 1) * size].astype(bf16))
    head_rows = [
        dot(jnp.concatenate([outs[0][h], outs[1][h]], axis=0), value_ref[h]).astype(bf16)
        for h in range(heads)
    ]
    head_rows = jnp.concatenate(head_rows, axis=1)
    partial = dot(head_rows, output_ref[...])
    keep_ref[...] = partial[:size]
    send_ref[...] = partial[size:].astype(bf16)


def attention_part(first, place, row_index, blocks, cache, tables, weights):
    size, width = blocks[0].shape
    out_shape = [
        jax.ShapeDtypeStruct((size, width), jnp.float32),
        jax.ShapeDtypeStruct((size, width), jnp.bfloat16),
    ]
    if first:
        out_shape.append(jax.ShapeDtypeStruct((1, size, LAT + ROPE), jnp.bfloat16))
    return pl.pallas_call(
        functools.partial(attention_kernel, first, place),
        out_shape=tuple(out_shape),
        in_specs=[SCALARS] + [WHOLE] * 13,
        out_specs=(WHOLE,) * len(out_shape),
        compiler_params=params(12),
        cost_estimate=SMALL,
        name="attention",
    )(row_index, *blocks, cache, *tables, *weights)


def join_kernel(
    row_ref,
    hidden_ref,
    keep_ref,
    arrived_ref,
    gain_ref,
    named_ref,
    residual_ref,
    block_ref,
    own_ref,
):
    total = keep_ref[...].astype(jnp.float32)
    for k in range(arrived_ref.shape[0]):
        total = total + arrived_ref[k].astype(jnp.float32)
    residual = hidden_ref[...].astype(jnp.float32) + total
    parts, _, part_width = residual_ref.shape
    normed = rms_scale(residual, gain_ref[...]).astype(jnp.bfloat16)
    for k in range(parts):
        part = slice(k * part_width, (k + 1) * part_width)
        residual_ref[k ^ row_ref[2]] = residual[:, part]
        block_ref[k ^ row_ref[2], :, :part_width] = normed[:, part]
        block_ref[k, :, part_width:] = named_ref[...]
    own_ref[...] = block_ref[:1]


def joined(indices, parts, hidden, keep, arrived, gain, named):
    rows, width = hidden.shape
    block_width = width // parts + EXTRA
    return pl.pallas_call(
        join_kernel,
        out_shape=(
            jax.ShapeDtypeStruct((parts, rows, width // parts), jnp.float32),
            jax.ShapeDtypeStruct((parts, rows, block_width), jnp.bfloat16),
            jax.ShapeDtypeStruct((1, rows, block_width), jnp.bfloat16),
        ),
        in_specs=[SCALARS] + [WHOLE] * 5,
        out_specs=(WHOLE, WHOLE, WHOLE),
        compiler_params=params(16),
        cost_estimate=LONGER,
        name="join",
    )(indices, hidden, keep, arrived, gain, named)


def finish_kernel(row_ref, own_ref, others_ref, out_ref):
    parts, _, width = others_ref.shape
    for k in range(parts + 1):
        values = own_ref[...] if k == 0 else others_ref[k - 1]
        start = pl.multiple_of((row_ref[2] ^ k) * width, 128)
        out_ref[:, pl.ds(start, width)] = values


def finished(indices, own, others):
    rows, width = own.shape
    return pl.pallas_call(
        finish_kernel,
        out_shape=jax.ShapeDtypeStruct((rows, width * (1 + others.shape[0])), own.dtype),
        in_specs=[SCALARS, WHOLE, WHOLE],
        out_specs=WHOLE,
        compiler_params=params(12),
        name="finish",
    )(indices, own, others)


def expert_kernel(shared, far_first, *refs):
    row_ref, blocks, refs = refs[0], refs[1:5], refs[5:]
    own_ref, router_ref, gate_up_ref, down_ref = refs[:4]
    refs = refs[4:]
    if shared:
        shared_gate_up_ref, shared_down_ref = refs[:2]
        refs = refs[2:]
    keep_ref, send_ref, rows_ref = refs
    experts, width = router_ref.shape
    parts, size, _ = blocks[0].shape
    part_width = width // parts
    for b, ref in enumerate(blocks):
        for k in range(parts):
            start = pl.multiple_of((k ^ row_ref[2]) * part_width, 128)
            rows_ref[b * size : (b + 1) * size, pl.ds(start, part_width)] = ref[k, :, :part_width]
    rows = rows_ref[...]
    named = jnp.concatenate([ref[0, :, part_width:] for ref in blocks], axis=0)[:, :experts]
    logits = transposed_dot(rows, router_ref[...])
    raised = jnp.exp(logits - jnp.max(logits, axis=-1, keepdims=True))
    router = raised / jnp.sum(raised, axis=-1, keepdims=True)
    share = jnp.sum(router * named.astype(jnp.float32) * own_ref[...], axis=-1, keepdims=True)

    def inner(weights_ref):
        gate = transposed_dot(rows, weights_ref[0])
        upper = transposed_dot(rows, weights_ref[1])
        return (jax.nn.silu(gate) * upper).astype(jnp.bfloat16)

    routed_inner = inner(gate_up_ref)
    if shared:
        shared_inner = inner(shared_gate_up_ref)
    tile = width // CHUNKS
    for k in range(CHUNKS):
        part = slice(k * tile, (k + 1) * tile)
        result = share * dot(routed_inner, down_ref[:, part])
        if shared:
            result = result + dot(shared_inner, shared_down_ref[:, part])
        place = (k * tile // part_width) ^ row_ref[2]
        inside = slice(k * tile % part_width, k * tile % part_width + tile)
        spot = (slice(None), place) if far_first else (place, slice(None))
        spot = (*spot, slice(None), inside)
        keep_ref[spot] = result[: 2 * size].reshape(2, size, tile)
        send_ref[spot] = result[2 * size :].astype(jnp.bfloat16).reshape(2, size, tile)


def expert_part(
    indices, parts, far_first, blocks, own_expert, router, routed_weights, shared_weights=()
):
    size = blocks[0].shape[1]
    width = router.shape[1]
    units = sum(each.shape[0] for each in (*routed_weights, *shared_weights) if each.ndim == 2)
    out_shape = (*((2, parts) if far_first else (parts, 2)), size, width // parts)
    operands = [indices, *blocks, own_expert, router, *routed_weights, *shared_weights]
    return pl.pallas_call(
        functools.partial(expert_kernel, bool(shared_weights), far_first),
        out_shape=(
            jax.ShapeDtypeStruct(out_shape, jnp.float32),
            jax.ShapeDtypeStruct(out_shape, jnp.bfloat16),
        ),
        in_specs=[SCALARS] + [WHOLE] * (len(operands) - 1),
        out_specs=(WHOLE, WHOLE),
        scratch_shapes=[pltpu.VMEM((4 * size, width), jnp.bfloat16)],
        compiler_params=params(12),
        cost_estimate=SMALL,
        name="experts",
    )(*operands)


def after(values, *others):
    return lax.optimization_barrier((values, *others))[0]


def swap(values, axis, size, bits):
    return lax.ppermute(values, axis, [(i, i ^ bits) for i in range(size)])


def body(
    sizes,
    hidden,
    latent_cache,
    lengths,
    parents,
    routes,
    accepted,
    input_gain,
    query_weight,
    latent_weight,
    latent_gain,
    key_absorb,
    value_absorb,
    output_weight,
    post_gain,
    router_weight,
    shared_gate_up,
    shared_down,
    expert_gate_up,
    expert_down,
):
    n_req, n_row, n_col = sizes
    req_index = lax.axis_index("req")
    row_index = lax.axis_index("row")
    bf16 = jnp.bfloat16

    far = swap(hidden, "row", n_row, 2)
    near = swap(hidden, "row", n_row, 1)

    experts = router_weight.shape[1]
    indices = jnp.stack([row_index, req_index * n_row + row_index, lax.axis_index("col")]).astype(jnp.int32)
    *tables, own_expert = tree_tables(indices, lengths, accepted, parents, experts)
    cache = jnp.swapaxes(latent_cache, 1, 2)
    weights = (
        input_gain[None],
        query_weight,
        latent_weight.T,
        latent_gain[None],
        key_absorb,
        value_absorb,
        output_weight,
    )
    own_keep, own_send, accepted_latents = attention_part(
        True, 0, indices, (hidden, near), cache, tables, weights
    )
    far = after(far, own_send)
    far_near = swap(far, "row", n_row, 1)
    far_keep, far_send = attention_part(
        False, 2, indices, (far, far_near), cache, tables, weights
    )

    def fold(keep, sent):
        return keep + swap(sent, "row", n_row, 1).astype(jnp.float32)

    from_far = swap(fold(far_keep, far_send).astype(bf16), "row", n_row, 2)
    partial = fold(own_keep, own_send) + from_far.astype(jnp.float32)
    partial, arrived = col_parts(partial, n_col)
    named = (routes[:, :, None] == jnp.arange(EXTRA, dtype=jnp.int32)).any(axis=1).astype(bf16)
    residual, block, own_part = joined(indices, n_col, hidden, partial, arrived, post_gain[None], named)

    router = router_weight.T
    routed_weights = (jnp.swapaxes(expert_gate_up[0], 1, 2), expert_down[0])
    shared_weights = (jnp.swapaxes(shared_gate_up, 1, 2), shared_down)
    distances = [0, 1, *range(n_req - 1, 1, -1)]
    blocks = [block, swap(block, "req", n_req, 1)]
    fars = [swap(each, "row", n_row, 2) for each in blocks]
    rest = [swap(own_part, "req", n_req, s) for s in distances[2:]]
    if rest:
        rest = after(jnp.concatenate(rest, axis=0)[None], fars[0], blocks[1])
        rest_far = swap(rest, "row", n_row, 2)
        rest, rest_far = col_gather(rest, n_col), col_gather(rest_far, n_col)
        blocks += [rest[:, k] for k in range(rest.shape[1])]
        fars += [rest_far[:, k] for k in range(rest.shape[1])]
    sends, folds, sums, returns = [], [], [], []
    for k, s in enumerate(distances):
        near = swap(blocks[k], "row", n_row, 1)
        far = fars[k]
        far_near = swap(far, "row", n_row, 1)
        if k:
            far_near = after(far_near, *sends, *folds[: k - 1], *returns[: max(0, k - 2)])
        keep, send = expert_part(
            indices,
            n_col,
            k < 3,
            (blocks[k], far, near, far_near),
            own_expert,
            router,
            routed_weights,
            () if s else shared_weights,
        )
        sends.append(send)
        near_sum = keep + swap(send, "row", n_row, 1).astype(jnp.float32)
        fold = near_sum[1] if k < 3 else near_sum[n_col // 2 :]
        folds.append(fold.astype(bf16))
        sums.append(near_sum)
        if k < 3:
            returns.append(swap(folds[k], "row", n_row, 2))
    parts = []
    for k, near_sum in enumerate(sums):
        if k < 3:
            from_far = after(returns[k], *folds[-1:]) if k else returns[k]
            part = col_scatter(near_sum[0] + from_far.astype(jnp.float32), n_col)[0]
        else:
            part = col_scatter(near_sum, n_col)[0]
            part = part[0] + swap(part[1].astype(bf16), "row", n_row, 2).astype(jnp.float32)
        parts.append(part.astype(bf16) if k else part)
    total = parts[0]
    for s, part in zip(distances[1:], parts[1:]):
        total = total + swap(part, "req", n_req, s).astype(jnp.float32)
    own = (residual[0] + total).astype(bf16)
    others = col_gather(own[None], n_col)
    layer_output = finished(indices, own, others[1:])
    return (layer_output, accepted_latents)


def col_gather(values, n_col):
    bits = 1
    while bits < n_col:
        values = jnp.concatenate([values, swap(values, "col", n_col, bits)], axis=0)
        bits *= 2
    return values


def col_scatter(values, n_col):
    bits = n_col // 2
    while bits:
        received = swap(values[bits:].astype(jnp.bfloat16), "col", n_col, bits)
        values = values[:bits] + received.astype(jnp.float32)
        bits //= 2
    return values


def col_parts(values, n_col):
    bits = 1
    while 2 * bits < n_col:
        sent = values.astype(jnp.bfloat16)
        values = sent.astype(jnp.float32) + swap(sent, "col", n_col, bits).astype(jnp.float32)
        bits *= 2
    sent = values.astype(jnp.bfloat16)
    return sent, swap(sent, "col", n_col, bits)[None]


def solution(mesh):
    placed = (
        P(("req", "row"), None),
        P("req", None, None),
        P("req"),
        P("req", None),
        P(("req", "row"), None),
        P(("req", "row")),
        P(),
        P(None, ("row", "col")),
        P(),
        P(),
        P(("row", "col"), None, None),
        P(("row", "col"), None, None),
        P(("row", "col"), None),
        P(),
        P(),
        P(None, None, ("row", "col")),
        P(("row", "col"), None),
        P(("req", "row"), None, None, "col"),
        P(("req", "row"), "col", None),
    )
    sizes = (mesh.shape["req"], mesh.shape["row"], mesh.shape["col"])
    return jax.shard_map(
        functools.partial(body, sizes),
        mesh=mesh,
        in_specs=placed,
        out_specs=(P(("req", "row"), None), P(("req", "row"), None, None)),
        check_vma=False,
    )
```

```python
import functools
import math

import jax
import jax.numpy as jnp
from jax import lax
from jax.experimental import pallas as pl
from jax.experimental.pallas import tpu as pltpu
from jax.sharding import PartitionSpec as P

NOPE = 128
ROPE = 64
LAT = 512
VDIM = 128
CACHE = 384
WINDOW = 160
SINK = 4


EPSILON = 1e-06
EXTRA = 128
CHUNKS = 4


def rms_scale(values, gain_row):
    mean_square = jnp.mean(values * values, axis=-1, keepdims=True)
    return values * lax.rsqrt(mean_square + EPSILON) * gain_row


def rotate(values, cosine, sine_part):
    half_width = values.shape[-1] // 2
    first_half = values[..., :half_width]
    second_half = values[..., half_width:]
    return jnp.concatenate(
        [
            first_half * cosine - second_half * sine_part,
            second_half * cosine + first_half * sine_part,
        ],
        axis=-1,
    )


def dot(values, weight):
    return jnp.dot(values, weight, preferred_element_type=jnp.float32)


def transposed_dot(values, weight):
    return lax.dot_general(
        values, weight, (((1,), (1,)), ((), ())), preferred_element_type=jnp.float32
    )


WHOLE = pl.BlockSpec(memory_space=pltpu.VMEM)
SCALARS = pl.BlockSpec(memory_space=pltpu.SMEM)


SMALL = pl.CostEstimate(flops=1, bytes_accessed=1, transcendentals=0)
LONG = pl.CostEstimate(flops=20000000000, bytes_accessed=1, transcendentals=0)
LONGER = pl.CostEstimate(flops=30000000000, bytes_accessed=1, transcendentals=0)


def params(megabytes):
    return pltpu.CompilerParams(vmem_limit_bytes=megabytes << 20)


def tree_kernel(
    row_ref, lengths_ref, accepted_ref, parents_ref, closure_ref, turns_ref, places_ref, expert_ref
):
    requests, size, _ = closure_ref.shape
    expert_ids = lax.broadcasted_iota(jnp.int32, expert_ref.shape, 1)
    expert_ref[...] = (expert_ids == row_ref[1]).astype(jnp.float32)
    down = lax.broadcasted_iota(jnp.int32, (size, size), 0)
    across = lax.broadcasted_iota(jnp.int32, (size, size), 1)
    eye = (down == across).astype(jnp.bfloat16)
    closures = []
    for k in range(requests):
        parent_row = parents_ref[pl.ds(row_ref[0] ^ k, 1), :]
        links = (parent_row == down).astype(jnp.bfloat16) + eye
        closures.append(
            lax.dot_general(
                links, eye, (((0,), (0,)), ((), ())), preferred_element_type=jnp.float32
            )
        )
    for repeat in range(max(1, (size - 1).bit_length())):
        narrow = [closure.astype(jnp.bfloat16) for closure in closures]
        closures = [jnp.minimum(dot(each, each), 1.0) for each in narrow]
    step = -2.0 * math.log(10000.0) / ROPE
    frequency = jnp.exp(
        lax.broadcasted_iota(jnp.int32, (size, ROPE // 2), 1).astype(jnp.float32) * step
    )
    for k in range(requests):
        closure_ref[k] = closures[k]
        depth = jnp.sum(closures[k], axis=-1, keepdims=True) - 1.0
        length = lengths_ref[row_ref[0] ^ k].astype(jnp.float32)
        angles = (length + depth) * frequency
        turns_ref[k, :, : ROPE // 2] = jnp.cos(angles)
        turns_ref[k, :, ROPE // 2 : ROPE] = jnp.sin(angles)
        turns_ref[k, :, ROPE : ROPE + 1] = jnp.full((size, 1), length)
    own = closures[0].astype(jnp.bfloat16)
    depth_row = transposed_dot(jnp.ones((8, size), jnp.bfloat16), own)[:1] - 1.0
    chosen = (lax.broadcasted_iota(jnp.int32, (size, 1), 0) == accepted_ref[0]).astype(jnp.float32)
    path_mask = jnp.sum(chosen * closures[0], axis=0, keepdims=True)
    places_ref[...] = jnp.where(
        depth_row == down.astype(jnp.float32), path_mask, 0.0
    ).astype(jnp.bfloat16)


def tree_tables(indices, lengths, accepted, parents, experts):
    requests, size = parents.shape
    return pl.pallas_call(
        tree_kernel,
        out_shape=(
            jax.ShapeDtypeStruct((requests, size, size), jnp.float32),
            jax.ShapeDtypeStruct((requests, size, ROPE + 1), jnp.float32),
            jax.ShapeDtypeStruct((size, size), jnp.bfloat16),
            jax.ShapeDtypeStruct((1, experts), jnp.float32),
        ),
        in_specs=[SCALARS, SCALARS, SCALARS, WHOLE],
        out_specs=(WHOLE, WHOLE, WHOLE, WHOLE),
        compiler_params=params(16),
        cost_estimate=LONG,
        name="trees",
    )(indices, lengths, accepted, parents)


def attention_kernel(first, place, row_ref, *refs):
    (
        first_ref,
        second_ref,
        cache_ref,
        closure_ref,
        turns_ref,
        places_ref,
        gain_ref,
        query_ref,
        latent_ref,
        latent_gain_ref,
        key_ref,
        value_ref,
        output_ref,
        keep_ref,
        send_ref,
    ) = refs[:15]
    size = first_ref.shape[0]
    heads = key_ref.shape[0]
    bf16 = jnp.bfloat16
    scale_factor = 1.0 / math.sqrt(NOPE + ROPE)
    rows = jnp.concatenate([first_ref[...], second_ref[...]], axis=0).astype(jnp.float32)
    rows = rms_scale(rows, gain_ref[...]).astype(bf16)
    turns = jnp.concatenate([turns_ref[place], turns_ref[place + 1]], axis=0)
    cosine, sine_part = turns[:, : ROPE // 2], turns[:, ROPE // 2 : ROPE]
    projected = transposed_dot(rows, latent_ref[...])
    content = rms_scale(projected[:, :LAT], latent_gain_ref[...]).astype(bf16)
    key_rope = rotate(projected[:, LAT:], cosine, sine_part).astype(bf16)
    if first:
        accepted_ref = refs[15]
        accepted_ref[0, :, :LAT] = dot(places_ref[...], content[:size]).astype(bf16)
        accepted_ref[0, :, LAT:] = dot(places_ref[...], key_rope[:size]).astype(bf16)
    queries = dot(rows, query_ref[...])
    query_latent, query_rope = [], []
    for h in range(heads):
        start = h * (NOPE + ROPE)
        query_latent.append(
            dot(queries[:, start : start + NOPE].astype(bf16), key_ref[h]).astype(bf16)
        )
        turned = queries[:, start + NOPE : start + NOPE + ROPE].astype(bf16).astype(jnp.float32)
        query_rope.append(rotate(turned, cosine, sine_part).astype(bf16))
    outs = [[], []]
    for r in range(2):
        spot = row_ref[0] ^ (place + r)
        part = slice(r * size, (r + 1) * size)
        latent_rows = jnp.concatenate([each[part] for each in query_latent], axis=0)
        rope_rows = jnp.concatenate([each[part] for each in query_rope], axis=0)
        old = dot(latent_rows, cache_ref[spot, :LAT, :]) + dot(rope_rows, cache_ref[spot, LAT:, :])
        new = transposed_dot(latent_rows, content[part]) + transposed_dot(rope_rows, key_rope[part])
        length = jnp.concatenate([turns_ref[place + r, :, ROPE : ROPE + 1]] * heads, axis=0)
        spots = lax.broadcasted_iota(jnp.int32, old.shape, 1).astype(jnp.float32)
        allowed = (spots < length) & ((spots < SINK) | (spots >= length - WINDOW))
        related = jnp.concatenate([closure_ref[place + r]] * heads, axis=0) > 0.5
        old = jnp.where(allowed, old * scale_factor, -1e30)
        new = jnp.where(related, new * scale_factor, -1e30)
        peak = jnp.maximum(
            jnp.max(old, axis=-1, keepdims=True), jnp.max(new, axis=-1, keepdims=True)
        )
        old = jnp.exp(old - peak)
        new = jnp.exp(new - peak)
        total = jnp.sum(old, axis=-1, keepdims=True) + jnp.sum(new, axis=-1, keepdims=True)
        old = (old / total).astype(bf16)
        new = (new / total).astype(bf16)
        mixed = transposed_dot(old, cache_ref[spot, :LAT, :]) + dot(new, content[part])
        for h in range(heads):
            outs[r].append(mixed[h * size : (h + 1) * size].astype(bf16))
    head_rows = [
        dot(jnp.concatenate([outs[0][h], outs[1][h]], axis=0), value_ref[h]).astype(bf16)
        for h in range(heads)
    ]
    head_rows = jnp.concatenate(head_rows, axis=1)
    partial = dot(head_rows, output_ref[...])
    keep_ref[...] = partial[:size]
    send_ref[...] = partial[size:].astype(bf16)


def attention_part(first, place, row_index, blocks, cache, tables, weights):
    size, width = blocks[0].shape
    out_shape = [
        jax.ShapeDtypeStruct((size, width), jnp.float32),
        jax.ShapeDtypeStruct((size, width), jnp.bfloat16),
    ]
    if first:
        out_shape.append(jax.ShapeDtypeStruct((1, size, LAT + ROPE), jnp.bfloat16))
    return pl.pallas_call(
        functools.partial(attention_kernel, first, place),
        out_shape=tuple(out_shape),
        in_specs=[SCALARS] + [WHOLE] * 13,
        out_specs=(WHOLE,) * len(out_shape),
        compiler_params=params(12),
        cost_estimate=SMALL,
        name="attention",
    )(row_index, *blocks, cache, *tables, *weights)


def join_kernel(
    row_ref,
    hidden_ref,
    keep_ref,
    arrived_ref,
    gain_ref,
    named_ref,
    residual_ref,
    block_ref,
    own_ref,
):
    total = keep_ref[...].astype(jnp.float32)
    for k in range(arrived_ref.shape[0]):
        total = total + arrived_ref[k].astype(jnp.float32)
    residual = hidden_ref[...].astype(jnp.float32) + total
    parts, _, part_width = residual_ref.shape
    normed = rms_scale(residual, gain_ref[...]).astype(jnp.bfloat16)
    for k in range(parts):
        part = slice(k * part_width, (k + 1) * part_width)
        residual_ref[k ^ row_ref[2]] = residual[:, part]
        block_ref[k ^ row_ref[2], :, :part_width] = normed[:, part]
        block_ref[k, :, part_width:] = named_ref[...]
    own_ref[...] = block_ref[:1]


def joined(indices, parts, hidden, keep, arrived, gain, named):
    rows, width = hidden.shape
    block_width = width // parts + EXTRA
    return pl.pallas_call(
        join_kernel,
        out_shape=(
            jax.ShapeDtypeStruct((parts, rows, width // parts), jnp.float32),
            jax.ShapeDtypeStruct((parts, rows, block_width), jnp.bfloat16),
            jax.ShapeDtypeStruct((1, rows, block_width), jnp.bfloat16),
        ),
        in_specs=[SCALARS] + [WHOLE] * 5,
        out_specs=(WHOLE, WHOLE, WHOLE),
        compiler_params=params(16),
        cost_estimate=LONGER,
        name="join",
    )(indices, hidden, keep, arrived, gain, named)


def finish_kernel(row_ref, own_ref, others_ref, out_ref):
    parts, _, width = others_ref.shape
    for k in range(parts + 1):
        values = own_ref[...] if k == 0 else others_ref[k - 1]
        start = pl.multiple_of((row_ref[2] ^ k) * width, 128)
        out_ref[:, pl.ds(start, width)] = values


def finished(indices, own, others):
    rows, width = own.shape
    return pl.pallas_call(
        finish_kernel,
        out_shape=jax.ShapeDtypeStruct((rows, width * (1 + others.shape[0])), own.dtype),
        in_specs=[SCALARS, WHOLE, WHOLE],
        out_specs=WHOLE,
        compiler_params=params(12),
        name="finish",
    )(indices, own, others)


def expert_kernel(shared, far_first, *refs):
    row_ref, blocks, refs = refs[0], refs[1:5], refs[5:]
    own_ref, router_ref, gate_up_ref, down_ref = refs[:4]
    refs = refs[4:]
    if shared:
        shared_gate_up_ref, shared_down_ref = refs[:2]
        refs = refs[2:]
    keep_ref, send_ref, rows_ref = refs
    experts, width = router_ref.shape
    parts, size, _ = blocks[0].shape
    part_width = width // parts
    for b, ref in enumerate(blocks):
        for k in range(parts):
            start = pl.multiple_of((k ^ row_ref[2]) * part_width, 128)
            rows_ref[b * size : (b + 1) * size, pl.ds(start, part_width)] = ref[k, :, :part_width]
    rows = rows_ref[...]
    named = jnp.concatenate([ref[0, :, part_width:] for ref in blocks], axis=0)[:, :experts]
    logits = transposed_dot(rows, router_ref[...])
    raised = jnp.exp(logits - jnp.max(logits, axis=-1, keepdims=True))
    router = raised / jnp.sum(raised, axis=-1, keepdims=True)
    share = jnp.sum(router * named.astype(jnp.float32) * own_ref[...], axis=-1, keepdims=True)

    def inner(weights_ref):
        gate = transposed_dot(rows, weights_ref[0])
        upper = transposed_dot(rows, weights_ref[1])
        return (jax.nn.silu(gate) * upper).astype(jnp.bfloat16)

    routed_inner = inner(gate_up_ref)
    if shared:
        shared_inner = inner(shared_gate_up_ref)
    tile = width // CHUNKS
    for k in range(CHUNKS):
        part = slice(k * tile, (k + 1) * tile)
        result = share * dot(routed_inner, down_ref[:, part])
        if shared:
            result = result + dot(shared_inner, shared_down_ref[:, part])
        place = (k * tile // part_width) ^ row_ref[2]
        inside = slice(k * tile % part_width, k * tile % part_width + tile)
        spot = (slice(None), place) if far_first else (place, slice(None))
        spot = (*spot, slice(None), inside)
        keep_ref[spot] = result[: 2 * size].reshape(2, size, tile)
        send_ref[spot] = result[2 * size :].astype(jnp.bfloat16).reshape(2, size, tile)


def expert_part(
    indices, parts, far_first, blocks, own_expert, router, routed_weights, shared_weights=()
):
    size = blocks[0].shape[1]
    width = router.shape[1]
    units = sum(each.shape[0] for each in (*routed_weights, *shared_weights) if each.ndim == 2)
    out_shape = (*((2, parts) if far_first else (parts, 2)), size, width // parts)
    operands = [indices, *blocks, own_expert, router, *routed_weights, *shared_weights]
    return pl.pallas_call(
        functools.partial(expert_kernel, bool(shared_weights), far_first),
        out_shape=(
            jax.ShapeDtypeStruct(out_shape, jnp.float32),
            jax.ShapeDtypeStruct(out_shape, jnp.bfloat16),
        ),
        in_specs=[SCALARS] + [WHOLE] * (len(operands) - 1),
        out_specs=(WHOLE, WHOLE),
        scratch_shapes=[pltpu.VMEM((4 * size, width), jnp.bfloat16)],
        compiler_params=params(12),
        cost_estimate=SMALL,
        name="experts",
    )(*operands)


def after(values, *others):
    return lax.optimization_barrier((values, *others))[0]


def swap(values, axis, size, bits):
    return lax.ppermute(values, axis, [(i, i ^ bits) for i in range(size)])


def body(
    sizes,
    hidden,
    latent_cache,
    lengths,
    parents,
    routes,
    accepted,
    input_gain,
    query_weight,
    latent_weight,
    latent_gain,
    key_absorb,
    value_absorb,
    output_weight,
    post_gain,
    router_weight,
    shared_gate_up,
    shared_down,
    expert_gate_up,
    expert_down,
):
    n_req, n_row, n_col = sizes
    req_index = lax.axis_index("req")
    row_index = lax.axis_index("row")
    bf16 = jnp.bfloat16

    far = swap(hidden, "row", n_row, 2)
    near = swap(hidden, "row", n_row, 1)

    experts = router_weight.shape[1]
    indices = jnp.stack([row_index, req_index * n_row + row_index, lax.axis_index("col")]).astype(jnp.int32)
    *tables, own_expert = tree_tables(indices, lengths, accepted, parents, experts)
    cache = jnp.swapaxes(latent_cache, 1, 2)
    weights = (
        input_gain[None],
        query_weight,
        latent_weight.T,
        latent_gain[None],
        key_absorb,
        value_absorb,
        output_weight,
    )
    far_near = swap(after(far, tables[0]), "row", n_row, 1)
    far_keep, far_send = attention_part(False, 2, indices, (far, far_near), cache, tables, weights)
    own_keep, own_send, accepted_latents = attention_part(
        True, 0, indices, (hidden, after(near, far_send)), cache, tables, weights
    )

    def fold(keep, sent):
        return keep + swap(sent, "row", n_row, 1).astype(jnp.float32)

    from_far = swap(fold(far_keep, far_send).astype(bf16), "row", n_row, 2)
    partial = fold(own_keep, own_send) + from_far.astype(jnp.float32)
    partial, arrived = col_parts(partial, n_col)
    named = (routes[:, :, None] == jnp.arange(EXTRA, dtype=jnp.int32)).any(axis=1).astype(bf16)
    residual, block, own_part = joined(indices, n_col, hidden, partial, arrived, post_gain[None], named)

    router = router_weight.T
    routed_weights = (jnp.swapaxes(expert_gate_up[0], 1, 2), expert_down[0])
    shared_weights = (jnp.swapaxes(shared_gate_up, 1, 2), shared_down)
    distances = [0, 1, *range(n_req - 1, 1, -1)]
    blocks = [block, swap(block, "req", n_req, 1)]
    fars = [swap(each, "row", n_row, 2) for each in blocks]
    rest = [swap(own_part, "req", n_req, s) for s in distances[2:]]
    if rest:
        rest = after(jnp.concatenate(rest, axis=0)[None], fars[0], blocks[1])
        rest_far = swap(rest, "row", n_row, 2)
        rest, rest_far = col_gather(rest, n_col), col_gather(rest_far, n_col)
        blocks += [rest[:, k] for k in range(rest.shape[1])]
        fars += [rest_far[:, k] for k in range(rest.shape[1])]
    sends, cores, sums = [], [], []
    for k, s in enumerate(distances):
        near = swap(blocks[k], "row", n_row, 1)
        far_near = swap(fars[k], "row", n_row, 1)
        if k:
            far_near = after(far_near, *sends, *cores[: k - 1])
        keep, send = expert_part(
            indices,
            n_col,
            k < 3,
            (blocks[k], fars[k], near, far_near),
            own_expert,
            router,
            routed_weights,
            () if s else shared_weights,
        )
        sends.append(send)
        cores.append(swap(send, "row", n_row, 1))
        sums.append(keep + cores[k].astype(jnp.float32))
    parts = []
    arrivals = []
    for k in reversed(range(n_req)):
        if k < 3:
            from_far = swap(sums[k][1].astype(bf16), "row", n_row, 2)
            from_far = after(from_far, *(cores[-1:] if k == 2 else arrivals))
            part = sums[k][0] + from_far.astype(jnp.float32)
            part, _ = col_scatter(part, n_col, arrivals if k == 2 else ())
            part = part[0]
        else:
            part, arrivals = col_scatter(sums[k], n_col)
            part = part[0]
            part = part[0] + swap(part[1].astype(bf16), "row", n_row, 2).astype(jnp.float32)
        parts.append(part.astype(bf16) if k else part)
    parts.reverse()
    total = parts[0]
    for s, part in zip(distances[1:], parts[1:]):
        total = total + swap(part, "req", n_req, s).astype(jnp.float32)
    own = (residual[0] + total).astype(bf16)
    others = col_gather(own[None], n_col)
    layer_output = finished(indices, own, others[1:])
    return (layer_output, accepted_latents)


def col_gather(values, n_col):
    bits = 1
    while bits < n_col:
        values = jnp.concatenate([values, swap(values, "col", n_col, bits)], axis=0)
        bits *= 2
    return values


def col_scatter(values, n_col, first=()):
    bits = n_col // 2
    arrived = []
    while bits:
        received = swap(values[bits:].astype(jnp.bfloat16), "col", n_col, bits)
        arrived.append(after(received, *first))
        values = values[:bits] + arrived[-1].astype(jnp.float32)
        bits //= 2
    return values, arrived


def col_parts(values, n_col):
    bits = 1
    while 2 * bits < n_col:
        sent = values.astype(jnp.bfloat16)
        values = sent.astype(jnp.float32) + swap(sent, "col", n_col, bits).astype(jnp.float32)
        bits *= 2
    sent = values.astype(jnp.bfloat16)
    return sent, swap(sent, "col", n_col, bits)[None]


def solution(mesh):
    placed = (
        P(("req", "row"), None),
        P("req", None, None),
        P("req"),
        P("req", None),
        P(("req", "row"), None),
        P(("req", "row")),
        P(),
        P(None, ("row", "col")),
        P(),
        P(),
        P(("row", "col"), None, None),
        P(("row", "col"), None, None),
        P(("row", "col"), None),
        P(),
        P(),
        P(None, None, ("row", "col")),
        P(("row", "col"), None),
        P(("req", "row"), None, None, "col"),
        P(("req", "row"), "col", None),
    )
    sizes = (mesh.shape["req"], mesh.shape["row"], mesh.shape["col"])
    return jax.shard_map(
        functools.partial(body, sizes),
        mesh=mesh,
        in_specs=placed,
        out_specs=(P(("req", "row"), None), P(("req", "row"), None, None)),
        check_vma=False,
    )
```

```python
import functools
import math

import jax
import jax.numpy as jnp
from jax import lax
from jax.experimental import pallas as pl
from jax.experimental.pallas import tpu as pltpu
from jax.sharding import PartitionSpec as P

NOPE = 128
ROPE = 64
LAT = 512
VDIM = 128
CACHE = 384
WINDOW = 160
SINK = 4


EPSILON = 1e-06
EXTRA = 128
CHUNKS = 4


def rms_scale(values, gain_row):
    mean_square = jnp.mean(values * values, axis=-1, keepdims=True)
    return values * lax.rsqrt(mean_square + EPSILON) * gain_row


def rotate(values, cosine, sine_part):
    half_width = values.shape[-1] // 2
    first_half = values[..., :half_width]
    second_half = values[..., half_width:]
    return jnp.concatenate(
        [
            first_half * cosine - second_half * sine_part,
            second_half * cosine + first_half * sine_part,
        ],
        axis=-1,
    )


def dot(values, weight):
    return jnp.dot(values, weight, preferred_element_type=jnp.float32)


def transposed_dot(values, weight):
    return lax.dot_general(
        values, weight, (((1,), (1,)), ((), ())), preferred_element_type=jnp.float32
    )


WHOLE = pl.BlockSpec(memory_space=pltpu.VMEM)
SCALARS = pl.BlockSpec(memory_space=pltpu.SMEM)


SMALL = pl.CostEstimate(flops=1, bytes_accessed=1, transcendentals=0)
LONG = pl.CostEstimate(flops=20000000000, bytes_accessed=1, transcendentals=0)
LONGER = pl.CostEstimate(flops=30000000000, bytes_accessed=1, transcendentals=0)


def params(megabytes):
    return pltpu.CompilerParams(vmem_limit_bytes=megabytes << 20)


def tree_kernel(
    row_ref, lengths_ref, accepted_ref, parents_ref, closure_ref, turns_ref, places_ref, expert_ref
):
    requests, size, _ = closure_ref.shape
    expert_ids = lax.broadcasted_iota(jnp.int32, expert_ref.shape, 1)
    expert_ref[...] = (expert_ids == row_ref[1]).astype(jnp.float32)
    down = lax.broadcasted_iota(jnp.int32, (size, size), 0)
    across = lax.broadcasted_iota(jnp.int32, (size, size), 1)
    eye = (down == across).astype(jnp.bfloat16)
    closures = []
    for k in range(requests):
        parent_row = parents_ref[pl.ds(row_ref[0] ^ k, 1), :]
        links = (parent_row == down).astype(jnp.bfloat16) + eye
        closures.append(
            lax.dot_general(
                links, eye, (((0,), (0,)), ((), ())), preferred_element_type=jnp.float32
            )
        )
    for repeat in range(max(1, (size - 1).bit_length())):
        narrow = [closure.astype(jnp.bfloat16) for closure in closures]
        closures = [jnp.minimum(dot(each, each), 1.0) for each in narrow]
    step = -2.0 * math.log(10000.0) / ROPE
    frequency = jnp.exp(
        lax.broadcasted_iota(jnp.int32, (size, ROPE // 2), 1).astype(jnp.float32) * step
    )
    for k in range(requests):
        closure_ref[k] = closures[k]
        depth = jnp.sum(closures[k], axis=-1, keepdims=True) - 1.0
        length = lengths_ref[row_ref[0] ^ k].astype(jnp.float32)
        angles = (length + depth) * frequency
        turns_ref[k, :, : ROPE // 2] = jnp.cos(angles)
        turns_ref[k, :, ROPE // 2 : ROPE] = jnp.sin(angles)
        turns_ref[k, :, ROPE : ROPE + 1] = jnp.full((size, 1), length)
    own = closures[0].astype(jnp.bfloat16)
    depth_row = transposed_dot(jnp.ones((8, size), jnp.bfloat16), own)[:1] - 1.0
    chosen = (lax.broadcasted_iota(jnp.int32, (size, 1), 0) == accepted_ref[0]).astype(jnp.float32)
    path_mask = jnp.sum(chosen * closures[0], axis=0, keepdims=True)
    places_ref[...] = jnp.where(
        depth_row == down.astype(jnp.float32), path_mask, 0.0
    ).astype(jnp.bfloat16)


def tree_tables(indices, lengths, accepted, parents, experts):
    requests, size = parents.shape
    return pl.pallas_call(
        tree_kernel,
        out_shape=(
            jax.ShapeDtypeStruct((requests, size, size), jnp.float32),
            jax.ShapeDtypeStruct((requests, size, ROPE + 1), jnp.float32),
            jax.ShapeDtypeStruct((size, size), jnp.bfloat16),
            jax.ShapeDtypeStruct((1, experts), jnp.float32),
        ),
        in_specs=[SCALARS, SCALARS, SCALARS, WHOLE],
        out_specs=(WHOLE, WHOLE, WHOLE, WHOLE),
        compiler_params=params(16),
        cost_estimate=LONG,
        name="trees",
    )(indices, lengths, accepted, parents)


def attention_kernel(first, place, row_ref, *refs):
    (
        first_ref,
        second_ref,
        cache_ref,
        closure_ref,
        turns_ref,
        places_ref,
        gain_ref,
        query_ref,
        latent_ref,
        latent_gain_ref,
        key_ref,
        value_ref,
        output_ref,
        keep_ref,
        send_ref,
    ) = refs[:15]
    size = first_ref.shape[0]
    heads = key_ref.shape[0]
    bf16 = jnp.bfloat16
    scale_factor = 1.0 / math.sqrt(NOPE + ROPE)
    rows = jnp.concatenate([first_ref[...], second_ref[...]], axis=0).astype(jnp.float32)
    rows = rms_scale(rows, gain_ref[...]).astype(bf16)
    turns = jnp.concatenate([turns_ref[place], turns_ref[place + 1]], axis=0)
    cosine, sine_part = turns[:, : ROPE // 2], turns[:, ROPE // 2 : ROPE]
    projected = transposed_dot(rows, latent_ref[...])
    content = rms_scale(projected[:, :LAT], latent_gain_ref[...]).astype(bf16)
    key_rope = rotate(projected[:, LAT:], cosine, sine_part).astype(bf16)
    if first:
        accepted_ref = refs[15]
        accepted_ref[0, :, :LAT] = dot(places_ref[...], content[:size]).astype(bf16)
        accepted_ref[0, :, LAT:] = dot(places_ref[...], key_rope[:size]).astype(bf16)
    queries = dot(rows, query_ref[...])
    query_latent, query_rope = [], []
    for h in range(heads):
        start = h * (NOPE + ROPE)
        query_latent.append(
            dot(queries[:, start : start + NOPE].astype(bf16), key_ref[h]).astype(bf16)
        )
        turned = queries[:, start + NOPE : start + NOPE + ROPE].astype(bf16).astype(jnp.float32)
        query_rope.append(rotate(turned, cosine, sine_part).astype(bf16))
    outs = [[], []]
    for r in range(2):
        spot = row_ref[0] ^ (place + r)
        part = slice(r * size, (r + 1) * size)
        latent_rows = jnp.concatenate([each[part] for each in query_latent], axis=0)
        rope_rows = jnp.concatenate([each[part] for each in query_rope], axis=0)
        old = dot(latent_rows, cache_ref[spot, :LAT, :]) + dot(rope_rows, cache_ref[spot, LAT:, :])
        new = transposed_dot(latent_rows, content[part]) + transposed_dot(rope_rows, key_rope[part])
        length = jnp.concatenate([turns_ref[place + r, :, ROPE : ROPE + 1]] * heads, axis=0)
        spots = lax.broadcasted_iota(jnp.int32, old.shape, 1).astype(jnp.float32)
        allowed = (spots < length) & ((spots < SINK) | (spots >= length - WINDOW))
        related = jnp.concatenate([closure_ref[place + r]] * heads, axis=0) > 0.5
        old = jnp.where(allowed, old * scale_factor, -1e30)
        new = jnp.where(related, new * scale_factor, -1e30)
        peak = jnp.maximum(
            jnp.max(old, axis=-1, keepdims=True), jnp.max(new, axis=-1, keepdims=True)
        )
        old = jnp.exp(old - peak)
        new = jnp.exp(new - peak)
        total = jnp.sum(old, axis=-1, keepdims=True) + jnp.sum(new, axis=-1, keepdims=True)
        old = (old / total).astype(bf16)
        new = (new / total).astype(bf16)
        mixed = transposed_dot(old, cache_ref[spot, :LAT, :]) + dot(new, content[part])
        for h in range(heads):
            outs[r].append(mixed[h * size : (h + 1) * size].astype(bf16))
    head_rows = [
        dot(jnp.concatenate([outs[0][h], outs[1][h]], axis=0), value_ref[h]).astype(bf16)
        for h in range(heads)
    ]
    head_rows = jnp.concatenate(head_rows, axis=1)
    partial = dot(head_rows, output_ref[...])
    keep_ref[...] = partial[:size]
    send_ref[...] = partial[size:].astype(bf16)


def attention_part(first, place, row_index, blocks, cache, tables, weights):
    size, width = blocks[0].shape
    out_shape = [
        jax.ShapeDtypeStruct((size, width), jnp.float32),
        jax.ShapeDtypeStruct((size, width), jnp.bfloat16),
    ]
    if first:
        out_shape.append(jax.ShapeDtypeStruct((1, size, LAT + ROPE), jnp.bfloat16))
    return pl.pallas_call(
        functools.partial(attention_kernel, first, place),
        out_shape=tuple(out_shape),
        in_specs=[SCALARS] + [WHOLE] * 13,
        out_specs=(WHOLE,) * len(out_shape),
        compiler_params=params(12),
        cost_estimate=SMALL,
        name="attention",
    )(row_index, *blocks, cache, *tables, *weights)


def join_kernel(
    row_ref,
    hidden_ref,
    keep_ref,
    arrived_ref,
    gain_ref,
    named_ref,
    residual_ref,
    block_ref,
    own_ref,
):
    total = keep_ref[...].astype(jnp.float32)
    for k in range(arrived_ref.shape[0]):
        total = total + arrived_ref[k].astype(jnp.float32)
    residual = hidden_ref[...].astype(jnp.float32) + total
    parts, _, part_width = residual_ref.shape
    normed = rms_scale(residual, gain_ref[...]).astype(jnp.bfloat16)
    for k in range(parts):
        part = slice(k * part_width, (k + 1) * part_width)
        residual_ref[k ^ row_ref[2]] = residual[:, part]
        block_ref[k ^ row_ref[2], :, :part_width] = normed[:, part]
        block_ref[k, :, part_width:] = named_ref[...]
    own_ref[...] = block_ref[:1]


def joined(indices, parts, hidden, keep, arrived, gain, named):
    rows, width = hidden.shape
    block_width = width // parts + EXTRA
    return pl.pallas_call(
        join_kernel,
        out_shape=(
            jax.ShapeDtypeStruct((parts, rows, width // parts), jnp.float32),
            jax.ShapeDtypeStruct((parts, rows, block_width), jnp.bfloat16),
            jax.ShapeDtypeStruct((1, rows, block_width), jnp.bfloat16),
        ),
        in_specs=[SCALARS] + [WHOLE] * 5,
        out_specs=(WHOLE, WHOLE, WHOLE),
        compiler_params=params(16),
        cost_estimate=LONGER,
        name="join",
    )(indices, hidden, keep, arrived, gain, named)


def finish_kernel(row_ref, own_ref, others_ref, out_ref):
    parts, _, width = others_ref.shape
    for k in range(parts + 1):
        values = own_ref[...] if k == 0 else others_ref[k - 1]
        start = pl.multiple_of((row_ref[2] ^ k) * width, 128)
        out_ref[:, pl.ds(start, width)] = values


def finished(indices, own, others):
    rows, width = own.shape
    return pl.pallas_call(
        finish_kernel,
        out_shape=jax.ShapeDtypeStruct((rows, width * (1 + others.shape[0])), own.dtype),
        in_specs=[SCALARS, WHOLE, WHOLE],
        out_specs=WHOLE,
        compiler_params=params(12),
        name="finish",
    )(indices, own, others)


def expert_kernel(shared, far_first, *refs):
    row_ref, blocks, refs = refs[0], refs[1:5], refs[5:]
    own_ref, router_ref, gate_up_ref, down_ref = refs[:4]
    refs = refs[4:]
    if shared:
        shared_gate_up_ref, shared_down_ref = refs[:2]
        refs = refs[2:]
    keep_ref, send_ref, rows_ref = refs
    experts, width = router_ref.shape
    parts, size, _ = blocks[0].shape
    part_width = width // parts
    for b, ref in enumerate(blocks):
        for k in range(parts):
            start = pl.multiple_of((k ^ row_ref[2]) * part_width, 128)
            rows_ref[b * size : (b + 1) * size, pl.ds(start, part_width)] = ref[k, :, :part_width]
    rows = rows_ref[...]
    named = jnp.concatenate([ref[0, :, part_width:] for ref in blocks], axis=0)[:, :experts]
    logits = transposed_dot(rows, router_ref[...])
    raised = jnp.exp(logits - jnp.max(logits, axis=-1, keepdims=True))
    router = raised / jnp.sum(raised, axis=-1, keepdims=True)
    share = jnp.sum(router * named.astype(jnp.float32) * own_ref[...], axis=-1, keepdims=True)

    def inner(weights_ref):
        gate = transposed_dot(rows, weights_ref[0])
        upper = transposed_dot(rows, weights_ref[1])
        return (jax.nn.silu(gate) * upper).astype(jnp.bfloat16)

    routed_inner = inner(gate_up_ref)
    if shared:
        shared_inner = inner(shared_gate_up_ref)
    tile = width // CHUNKS
    for k in range(CHUNKS):
        part = slice(k * tile, (k + 1) * tile)
        result = share * dot(routed_inner, down_ref[:, part])
        if shared:
            result = result + dot(shared_inner, shared_down_ref[:, part])
        place = (k * tile // part_width) ^ row_ref[2]
        inside = slice(k * tile % part_width, k * tile % part_width + tile)
        spot = (slice(None), place) if far_first else (place, slice(None))
        spot = (*spot, slice(None), inside)
        keep_ref[spot] = result[: 2 * size].reshape(2, size, tile)
        send_ref[spot] = result[2 * size :].astype(jnp.bfloat16).reshape(2, size, tile)


def expert_part(
    indices, parts, far_first, blocks, own_expert, router, routed_weights, shared_weights=()
):
    size = blocks[0].shape[1]
    width = router.shape[1]
    units = sum(each.shape[0] for each in (*routed_weights, *shared_weights) if each.ndim == 2)
    out_shape = (*((2, parts) if far_first else (parts, 2)), size, width // parts)
    operands = [indices, *blocks, own_expert, router, *routed_weights, *shared_weights]
    return pl.pallas_call(
        functools.partial(expert_kernel, bool(shared_weights), far_first),
        out_shape=(
            jax.ShapeDtypeStruct(out_shape, jnp.float32),
            jax.ShapeDtypeStruct(out_shape, jnp.bfloat16),
        ),
        in_specs=[SCALARS] + [WHOLE] * (len(operands) - 1),
        out_specs=(WHOLE, WHOLE),
        scratch_shapes=[pltpu.VMEM((4 * size, width), jnp.bfloat16)],
        compiler_params=params(12),
        cost_estimate=SMALL,
        name="experts",
    )(*operands)


def after(values, *others):
    return lax.optimization_barrier((values, *others))[0]


def swap(values, axis, size, bits):
    return lax.ppermute(values, axis, [(i, i ^ bits) for i in range(size)])


def body(
    sizes,
    hidden,
    latent_cache,
    lengths,
    parents,
    routes,
    accepted,
    input_gain,
    query_weight,
    latent_weight,
    latent_gain,
    key_absorb,
    value_absorb,
    output_weight,
    post_gain,
    router_weight,
    shared_gate_up,
    shared_down,
    expert_gate_up,
    expert_down,
):
    n_req, n_row, n_col = sizes
    req_index = lax.axis_index("req")
    row_index = lax.axis_index("row")
    bf16 = jnp.bfloat16

    far = swap(hidden, "row", n_row, 2)
    near = swap(hidden, "row", n_row, 1)

    experts = router_weight.shape[1]
    indices = jnp.stack([row_index, req_index * n_row + row_index, lax.axis_index("col")]).astype(jnp.int32)
    *tables, own_expert = tree_tables(indices, lengths, accepted, parents, experts)
    cache = jnp.swapaxes(latent_cache, 1, 2)
    weights = (
        input_gain[None],
        query_weight,
        latent_weight.T,
        latent_gain[None],
        key_absorb,
        value_absorb,
        output_weight,
    )
    far_near = swap(after(far, tables[0]), "row", n_row, 1)
    far_keep, far_send = attention_part(False, 2, indices, (far, far_near), cache, tables, weights)
    far_core = swap(far_send, "row", n_row, 1)
    own_keep, own_send, accepted_latents = attention_part(
        True, 0, indices, (hidden, after(near, far_core)), cache, tables, weights
    )

    from_far = swap((far_keep + far_core.astype(jnp.float32)).astype(bf16), "row", n_row, 2)
    own_core = swap(own_send, "row", n_row, 1)
    partial = own_keep + own_core.astype(jnp.float32) + from_far.astype(jnp.float32)
    partial, arrived = col_parts(partial, n_col)
    named = (routes[:, :, None] == jnp.arange(EXTRA, dtype=jnp.int32)).any(axis=1).astype(bf16)
    residual, block, own_part = joined(indices, n_col, hidden, partial, arrived, post_gain[None], named)

    router = router_weight.T
    routed_weights = (jnp.swapaxes(expert_gate_up[0], 1, 2), expert_down[0])
    shared_weights = (jnp.swapaxes(shared_gate_up, 1, 2), shared_down)
    distances = [0, *range(n_req - 1, 0, -1)]
    nearest = swap(block, "req", n_req, 1)
    blocks, fars = [block], [swap(block, "row", n_row, 2)]
    rest = [swap(own_part, "req", n_req, s) for s in distances[1:-1]]
    nearest_far = nearest
    if rest:
        rest = after(jnp.concatenate(rest, axis=0)[None], fars[0], nearest)
        rest_far = swap(rest, "row", n_row, 2)
        nearest_far = after(nearest, rest_far)
        rest, rest_far = col_gather(rest, n_col), col_gather(rest_far, n_col)
        blocks += [rest[:, k] for k in range(rest.shape[1])]
        fars += [rest_far[:, k] for k in range(rest.shape[1])]
    blocks.append(nearest)
    fars.append(swap(nearest_far, "row", n_row, 2))
    sends, cores, sums = [], [], []
    for k, s in enumerate(distances):
        near = swap(blocks[k], "row", n_row, 1)
        if k == n_req - 1 and k > 1:
            fars[k] = after(fars[k], sends[k - 1])
        far_near = swap(fars[k], "row", n_row, 1)
        if k:
            far_near = after(far_near, *sends, *cores[: k - 1])
        keep, send = expert_part(
            indices,
            n_col,
            k != 2,
            (blocks[k], fars[k], near, far_near),
            own_expert,
            router,
            routed_weights,
            () if s else shared_weights,
        )
        sends.append(send)
        cores.append(swap(send, "row", n_row, 1))
        sums.append(keep + cores[k].astype(jnp.float32))
    arrivals = ()
    if n_req > 2:
        third, arrivals = col_scatter(sums[2], n_col)
        third = third[0, 0] + swap(third[0, 1].astype(bf16), "row", n_row, 2).astype(jnp.float32)
    parts = []
    for k, near_sum in enumerate(sums):
        if k == 2:
            part = third
        else:
            from_far = swap(near_sum[1].astype(bf16), "row", n_row, 2)
            from_far = after(from_far, *(cores[2:] if k == 1 else arrivals))
            part = near_sum[0] + from_far.astype(jnp.float32)
            part = col_scatter(part, n_col, arrivals if k == 1 else ())[0][0]
        parts.append(part.astype(bf16) if k else part)
    total = parts[0]
    for s, part in zip(distances[1:], parts[1:]):
        total = total + swap(part, "req", n_req, s).astype(jnp.float32)
    own = (residual[0] + total).astype(bf16)
    others = col_gather(own[None], n_col)
    layer_output = finished(indices, own, others[1:])
    return (layer_output, accepted_latents)


def col_gather(values, n_col):
    bits = 1
    while bits < n_col:
        values = jnp.concatenate([values, swap(values, "col", n_col, bits)], axis=0)
        bits *= 2
    return values


def col_scatter(values, n_col, first=()):
    bits = n_col // 2
    arrived = []
    while bits:
        received = swap(values[bits:].astype(jnp.bfloat16), "col", n_col, bits)
        arrived.append(after(received, *first))
        values = values[:bits] + arrived[-1].astype(jnp.float32)
        bits //= 2
    return values, arrived


def col_parts(values, n_col):
    bits = 1
    while 2 * bits < n_col:
        sent = values.astype(jnp.bfloat16)
        values = sent.astype(jnp.float32) + swap(sent, "col", n_col, bits).astype(jnp.float32)
        bits *= 2
    sent = values.astype(jnp.bfloat16)
    return sent, swap(sent, "col", n_col, bits)[None]


def solution(mesh):
    placed = (
        P(("req", "row"), None),
        P("req", None, None),
        P("req"),
        P("req", None),
        P(("req", "row"), None),
        P(("req", "row")),
        P(),
        P(None, ("row", "col")),
        P(),
        P(),
        P(("row", "col"), None, None),
        P(("row", "col"), None, None),
        P(("row", "col"), None),
        P(),
        P(),
        P(None, None, ("row", "col")),
        P(("row", "col"), None),
        P(("req", "row"), None, None, "col"),
        P(("req", "row"), "col", None),
    )
    sizes = (mesh.shape["req"], mesh.shape["row"], mesh.shape["col"])
    return jax.shard_map(
        functools.partial(body, sizes),
        mesh=mesh,
        in_specs=placed,
        out_specs=(P(("req", "row"), None), P(("req", "row"), None, None)),
        check_vma=False,
    )
```

```python
import functools
import math

import jax
import jax.numpy as jnp
from jax import lax
from jax.experimental import pallas as pl
from jax.experimental.pallas import tpu as pltpu
from jax.sharding import PartitionSpec as P

NOPE = 128
ROPE = 64
LAT = 512
VDIM = 128
CACHE = 384
WINDOW = 160
SINK = 4


EPSILON = 1e-06
EXTRA = 128
CHUNKS = 4


def rms_scale(values, gain_row):
    mean_square = jnp.mean(values * values, axis=-1, keepdims=True)
    return values * lax.rsqrt(mean_square + EPSILON) * gain_row


def rotate(values, cosine, sine_part):
    half_width = values.shape[-1] // 2
    first_half = values[..., :half_width]
    second_half = values[..., half_width:]
    return jnp.concatenate(
        [
            first_half * cosine - second_half * sine_part,
            second_half * cosine + first_half * sine_part,
        ],
        axis=-1,
    )


def dot(values, weight):
    return jnp.dot(values, weight, preferred_element_type=jnp.float32)


def transposed_dot(values, weight):
    return lax.dot_general(
        values, weight, (((1,), (1,)), ((), ())), preferred_element_type=jnp.float32
    )


WHOLE = pl.BlockSpec(memory_space=pltpu.VMEM)
SCALARS = pl.BlockSpec(memory_space=pltpu.SMEM)


SMALL = pl.CostEstimate(flops=1, bytes_accessed=1, transcendentals=0)
LONG = pl.CostEstimate(flops=20000000000, bytes_accessed=1, transcendentals=0)
LONGER = pl.CostEstimate(flops=30000000000, bytes_accessed=1, transcendentals=0)


def params(megabytes):
    return pltpu.CompilerParams(vmem_limit_bytes=megabytes << 20)


def tree_kernel(
    row_ref, lengths_ref, accepted_ref, parents_ref, closure_ref, turns_ref, places_ref, expert_ref
):
    requests, size, _ = closure_ref.shape
    expert_ids = lax.broadcasted_iota(jnp.int32, expert_ref.shape, 1)
    expert_ref[...] = (expert_ids == row_ref[1]).astype(jnp.float32)
    down = lax.broadcasted_iota(jnp.int32, (size, size), 0)
    across = lax.broadcasted_iota(jnp.int32, (size, size), 1)
    eye = (down == across).astype(jnp.bfloat16)
    closures = []
    for k in range(requests):
        parent_row = parents_ref[pl.ds(row_ref[0] ^ k, 1), :]
        links = (parent_row == down).astype(jnp.bfloat16) + eye
        closures.append(
            lax.dot_general(
                links, eye, (((0,), (0,)), ((), ())), preferred_element_type=jnp.float32
            )
        )
    for repeat in range(max(1, (size - 1).bit_length())):
        narrow = [closure.astype(jnp.bfloat16) for closure in closures]
        closures = [jnp.minimum(dot(each, each), 1.0) for each in narrow]
    step = -2.0 * math.log(10000.0) / ROPE
    frequency = jnp.exp(
        lax.broadcasted_iota(jnp.int32, (size, ROPE // 2), 1).astype(jnp.float32) * step
    )
    for k in range(requests):
        closure_ref[k] = closures[k]
        depth = jnp.sum(closures[k], axis=-1, keepdims=True) - 1.0
        length = lengths_ref[row_ref[0] ^ k].astype(jnp.float32)
        angles = (length + depth) * frequency
        turns_ref[k, :, : ROPE // 2] = jnp.cos(angles)
        turns_ref[k, :, ROPE // 2 : ROPE] = jnp.sin(angles)
        turns_ref[k, :, ROPE : ROPE + 1] = jnp.full((size, 1), length)
    own = closures[0].astype(jnp.bfloat16)
    depth_row = transposed_dot(jnp.ones((8, size), jnp.bfloat16), own)[:1] - 1.0
    chosen = (lax.broadcasted_iota(jnp.int32, (size, 1), 0) == accepted_ref[0]).astype(jnp.float32)
    path_mask = jnp.sum(chosen * closures[0], axis=0, keepdims=True)
    places_ref[...] = jnp.where(
        depth_row == down.astype(jnp.float32), path_mask, 0.0
    ).astype(jnp.bfloat16)


def tree_tables(indices, lengths, accepted, parents, experts):
    requests, size = parents.shape
    return pl.pallas_call(
        tree_kernel,
        out_shape=(
            jax.ShapeDtypeStruct((requests, size, size), jnp.float32),
            jax.ShapeDtypeStruct((requests, size, ROPE + 1), jnp.float32),
            jax.ShapeDtypeStruct((size, size), jnp.bfloat16),
            jax.ShapeDtypeStruct((1, experts), jnp.float32),
        ),
        in_specs=[SCALARS, SCALARS, SCALARS, WHOLE],
        out_specs=(WHOLE, WHOLE, WHOLE, WHOLE),
        compiler_params=params(16),
        cost_estimate=LONG,
        name="trees",
    )(indices, lengths, accepted, parents)


def attention_kernel(first, place, row_ref, *refs):
    (
        first_ref,
        second_ref,
        cache_ref,
        closure_ref,
        turns_ref,
        places_ref,
        gain_ref,
        query_ref,
        latent_ref,
        latent_gain_ref,
        key_ref,
        value_ref,
        output_ref,
        keep_ref,
        send_ref,
    ) = refs[:15]
    size = first_ref.shape[0]
    heads = key_ref.shape[0]
    bf16 = jnp.bfloat16
    scale_factor = 1.0 / math.sqrt(NOPE + ROPE)
    rows = jnp.concatenate([first_ref[...], second_ref[...]], axis=0).astype(jnp.float32)
    rows = rms_scale(rows, gain_ref[...]).astype(bf16)
    turns = jnp.concatenate([turns_ref[place], turns_ref[place + 1]], axis=0)
    cosine, sine_part = turns[:, : ROPE // 2], turns[:, ROPE // 2 : ROPE]
    projected = transposed_dot(rows, latent_ref[...])
    content = rms_scale(projected[:, :LAT], latent_gain_ref[...]).astype(bf16)
    key_rope = rotate(projected[:, LAT:], cosine, sine_part).astype(bf16)
    if first:
        accepted_ref = refs[15]
        accepted_ref[0, :, :LAT] = dot(places_ref[...], content[:size]).astype(bf16)
        accepted_ref[0, :, LAT:] = dot(places_ref[...], key_rope[:size]).astype(bf16)
    queries = dot(rows, query_ref[...])
    query_latent, query_rope = [], []
    for h in range(heads):
        start = h * (NOPE + ROPE)
        query_latent.append(
            dot(queries[:, start : start + NOPE].astype(bf16), key_ref[h]).astype(bf16)
        )
        turned = queries[:, start + NOPE : start + NOPE + ROPE].astype(bf16).astype(jnp.float32)
        query_rope.append(rotate(turned, cosine, sine_part).astype(bf16))
    outs = [[], []]
    for r in range(2):
        spot = row_ref[0] ^ (place + r)
        part = slice(r * size, (r + 1) * size)
        latent_rows = jnp.concatenate([each[part] for each in query_latent], axis=0)
        rope_rows = jnp.concatenate([each[part] for each in query_rope], axis=0)
        old = dot(latent_rows, cache_ref[spot, :LAT, :]) + dot(rope_rows, cache_ref[spot, LAT:, :])
        new = transposed_dot(latent_rows, content[part]) + transposed_dot(rope_rows, key_rope[part])
        length = jnp.concatenate([turns_ref[place + r, :, ROPE : ROPE + 1]] * heads, axis=0)
        spots = lax.broadcasted_iota(jnp.int32, old.shape, 1).astype(jnp.float32)
        allowed = (spots < length) & ((spots < SINK) | (spots >= length - WINDOW))
        related = jnp.concatenate([closure_ref[place + r]] * heads, axis=0) > 0.5
        old = jnp.where(allowed, old * scale_factor, -1e30)
        new = jnp.where(related, new * scale_factor, -1e30)
        peak = jnp.maximum(
            jnp.max(old, axis=-1, keepdims=True), jnp.max(new, axis=-1, keepdims=True)
        )
        old = jnp.exp(old - peak)
        new = jnp.exp(new - peak)
        total = jnp.sum(old, axis=-1, keepdims=True) + jnp.sum(new, axis=-1, keepdims=True)
        old = (old / total).astype(bf16)
        new = (new / total).astype(bf16)
        mixed = transposed_dot(old, cache_ref[spot, :LAT, :]) + dot(new, content[part])
        for h in range(heads):
            outs[r].append(mixed[h * size : (h + 1) * size].astype(bf16))
    head_rows = [
        dot(jnp.concatenate([outs[0][h], outs[1][h]], axis=0), value_ref[h]).astype(bf16)
        for h in range(heads)
    ]
    head_rows = jnp.concatenate(head_rows, axis=1)
    partial = dot(head_rows, output_ref[...])
    keep_ref[...] = partial[:size]
    send_ref[...] = partial[size:].astype(bf16)


def attention_part(first, place, row_index, blocks, cache, tables, weights):
    size, width = blocks[0].shape
    out_shape = [
        jax.ShapeDtypeStruct((size, width), jnp.float32),
        jax.ShapeDtypeStruct((size, width), jnp.bfloat16),
    ]
    if first:
        out_shape.append(jax.ShapeDtypeStruct((1, size, LAT + ROPE), jnp.bfloat16))
    return pl.pallas_call(
        functools.partial(attention_kernel, first, place),
        out_shape=tuple(out_shape),
        in_specs=[SCALARS] + [WHOLE] * 13,
        out_specs=(WHOLE,) * len(out_shape),
        compiler_params=params(12),
        cost_estimate=SMALL,
        name="attention",
    )(row_index, *blocks, cache, *tables, *weights)


def join_kernel(
    row_ref,
    hidden_ref,
    keep_ref,
    arrived_ref,
    gain_ref,
    named_ref,
    residual_ref,
    block_ref,
    own_ref,
):
    total = keep_ref[...].astype(jnp.float32)
    for k in range(arrived_ref.shape[0]):
        total = total + arrived_ref[k].astype(jnp.float32)
    residual = hidden_ref[...].astype(jnp.float32) + total
    parts, _, part_width = residual_ref.shape
    normed = rms_scale(residual, gain_ref[...]).astype(jnp.bfloat16)
    for k in range(parts):
        part = slice(k * part_width, (k + 1) * part_width)
        residual_ref[k ^ row_ref[2]] = residual[:, part]
        block_ref[k ^ row_ref[2], :, :part_width] = normed[:, part]
        block_ref[k, :, part_width:] = named_ref[...]
    own_ref[...] = block_ref[:1]


def joined(indices, parts, hidden, keep, arrived, gain, named):
    rows, width = hidden.shape
    block_width = width // parts + EXTRA
    return pl.pallas_call(
        join_kernel,
        out_shape=(
            jax.ShapeDtypeStruct((parts, rows, width // parts), jnp.float32),
            jax.ShapeDtypeStruct((parts, rows, block_width), jnp.bfloat16),
            jax.ShapeDtypeStruct((1, rows, block_width), jnp.bfloat16),
        ),
        in_specs=[SCALARS] + [WHOLE] * 5,
        out_specs=(WHOLE, WHOLE, WHOLE),
        compiler_params=params(16),
        cost_estimate=LONGER,
        name="join",
    )(indices, hidden, keep, arrived, gain, named)


def finish_kernel(row_ref, own_ref, others_ref, out_ref):
    parts, _, width = others_ref.shape
    for k in range(parts + 1):
        values = own_ref[...] if k == 0 else others_ref[k - 1]
        start = pl.multiple_of((row_ref[2] ^ k) * width, 128)
        out_ref[:, pl.ds(start, width)] = values


def finished(indices, own, others):
    rows, width = own.shape
    return pl.pallas_call(
        finish_kernel,
        out_shape=jax.ShapeDtypeStruct((rows, width * (1 + others.shape[0])), own.dtype),
        in_specs=[SCALARS, WHOLE, WHOLE],
        out_specs=WHOLE,
        compiler_params=params(12),
        name="finish",
    )(indices, own, others)


def expert_kernel(shared, far_first, *refs):
    row_ref, blocks, refs = refs[0], refs[1:5], refs[5:]
    own_ref, router_ref, gate_up_ref, down_ref = refs[:4]
    refs = refs[4:]
    if shared:
        shared_gate_up_ref, shared_down_ref = refs[:2]
        refs = refs[2:]
    keep_ref, send_ref, rows_ref = refs
    experts, width = router_ref.shape
    parts, size, _ = blocks[0].shape
    part_width = width // parts
    for b, ref in enumerate(blocks):
        for k in range(parts):
            start = pl.multiple_of((k ^ row_ref[2]) * part_width, 128)
            rows_ref[b * size : (b + 1) * size, pl.ds(start, part_width)] = ref[k, :, :part_width]
    rows = rows_ref[...]
    named = jnp.concatenate([ref[0, :, part_width:] for ref in blocks], axis=0)[:, :experts]
    logits = transposed_dot(rows, router_ref[...])
    raised = jnp.exp(logits - jnp.max(logits, axis=-1, keepdims=True))
    router = raised / jnp.sum(raised, axis=-1, keepdims=True)
    share = jnp.sum(router * named.astype(jnp.float32) * own_ref[...], axis=-1, keepdims=True)

    def inner(weights_ref):
        gate = transposed_dot(rows, weights_ref[0])
        upper = transposed_dot(rows, weights_ref[1])
        return (jax.nn.silu(gate) * upper).astype(jnp.bfloat16)

    routed_inner = inner(gate_up_ref)
    if shared:
        shared_inner = inner(shared_gate_up_ref)
    tile = width // CHUNKS
    for k in range(CHUNKS):
        part = slice(k * tile, (k + 1) * tile)
        result = share * dot(routed_inner, down_ref[:, part])
        if shared:
            result = result + dot(shared_inner, shared_down_ref[:, part])
        place = (k * tile // part_width) ^ row_ref[2]
        inside = slice(k * tile % part_width, k * tile % part_width + tile)
        spot = (slice(None), place) if far_first else (place, slice(None))
        spot = (*spot, slice(None), inside)
        keep_ref[spot] = result[: 2 * size].reshape(2, size, tile)
        send_ref[spot] = result[2 * size :].astype(jnp.bfloat16).reshape(2, size, tile)


def expert_part(
    indices, parts, far_first, blocks, own_expert, router, routed_weights, shared_weights=()
):
    size = blocks[0].shape[1]
    width = router.shape[1]
    units = sum(each.shape[0] for each in (*routed_weights, *shared_weights) if each.ndim == 2)
    out_shape = (*((2, parts) if far_first else (parts, 2)), size, width // parts)
    operands = [indices, *blocks, own_expert, router, *routed_weights, *shared_weights]
    return pl.pallas_call(
        functools.partial(expert_kernel, bool(shared_weights), far_first),
        out_shape=(
            jax.ShapeDtypeStruct(out_shape, jnp.float32),
            jax.ShapeDtypeStruct(out_shape, jnp.bfloat16),
        ),
        in_specs=[SCALARS] + [WHOLE] * (len(operands) - 1),
        out_specs=(WHOLE, WHOLE),
        scratch_shapes=[pltpu.VMEM((4 * size, width), jnp.bfloat16)],
        compiler_params=params(12),
        cost_estimate=SMALL,
        name="experts",
    )(*operands)


def after(values, *others):
    return lax.optimization_barrier((values, *others))[0]


def swap(values, axis, size, bits):
    return lax.ppermute(values, axis, [(i, i ^ bits) for i in range(size)])


def body(
    sizes,
    hidden,
    latent_cache,
    lengths,
    parents,
    routes,
    accepted,
    input_gain,
    query_weight,
    latent_weight,
    latent_gain,
    key_absorb,
    value_absorb,
    output_weight,
    post_gain,
    router_weight,
    shared_gate_up,
    shared_down,
    expert_gate_up,
    expert_down,
):
    n_req, n_row, n_col = sizes
    req_index = lax.axis_index("req")
    row_index = lax.axis_index("row")
    bf16 = jnp.bfloat16

    far = swap(hidden, "row", n_row, 2)
    near = swap(hidden, "row", n_row, 1)

    experts = router_weight.shape[1]
    indices = jnp.stack([row_index, req_index * n_row + row_index, lax.axis_index("col")]).astype(jnp.int32)
    *tables, own_expert = tree_tables(indices, lengths, accepted, parents, experts)
    cache = jnp.swapaxes(latent_cache, 1, 2)
    weights = (
        input_gain[None],
        query_weight,
        latent_weight.T,
        latent_gain[None],
        key_absorb,
        value_absorb,
        output_weight,
    )
    far_near = swap(after(far, tables[0]), "row", n_row, 1)
    far_keep, far_send = attention_part(False, 2, indices, (far, far_near), cache, tables, weights)
    far_core = swap(far_send, "row", n_row, 1)
    own_keep, own_send, accepted_latents = attention_part(
        True, 0, indices, (hidden, after(near, far_core)), cache, tables, weights
    )

    from_far = swap((far_keep + far_core.astype(jnp.float32)).astype(bf16), "row", n_row, 2)
    own_core = swap(own_send, "row", n_row, 1)
    partial = own_keep + own_core.astype(jnp.float32) + from_far.astype(jnp.float32)
    partial, arrived = col_parts(partial, n_col)
    named = (routes[:, :, None] == jnp.arange(EXTRA, dtype=jnp.int32)).any(axis=1).astype(bf16)
    residual, block, own_part = joined(indices, n_col, hidden, partial, arrived, post_gain[None], named)

    router = router_weight.T
    routed_weights = (jnp.swapaxes(expert_gate_up[0], 1, 2), expert_down[0])
    shared_weights = (jnp.swapaxes(shared_gate_up, 1, 2), shared_down)
    distances = [0, *range(n_req - 1, 0, -1)]
    nearest = swap(block, "req", n_req, 1)
    blocks, fars = [block], [swap(block, "row", n_row, 2)]
    rest = [swap(own_part, "req", n_req, s) for s in distances[1:-1]]
    nearest_far = nearest
    if rest:
        rest = after(jnp.concatenate(rest, axis=0)[None], fars[0], nearest)
        rest_far = swap(rest, "row", n_row, 2)
        nearest_far = after(nearest, rest_far)
        rest, rest_far = col_gather(rest, n_col), col_gather(rest_far, n_col)
        blocks += [rest[:, k] for k in range(rest.shape[1])]
        fars += [rest_far[:, k] for k in range(rest.shape[1])]
    blocks.append(nearest)
    fars.append(swap(nearest_far, "row", n_row, 2))
    sends, cores, sums = [], [], []
    for k, s in enumerate(distances):
        near = swap(blocks[k], "row", n_row, 1)
        if k == n_req - 1 and k > 1:
            fars[k] = after(fars[k], sends[k - 1])
        far_near = swap(fars[k], "row", n_row, 1)
        if k:
            far_near = after(far_near, *sends, *cores[: k - 1])
        keep, send = expert_part(
            indices,
            n_col,
            k != 2,
            (blocks[k], fars[k], near, far_near),
            own_expert,
            router,
            routed_weights,
            () if s else shared_weights,
        )
        sends.append(send)
        cores.append(swap(send, "row", n_row, 1))
        sums.append(keep + cores[k].astype(jnp.float32))
    arrivals = ()
    if n_req > 2:
        third, arrivals = col_scatter(sums[2], n_col)
        third = third[0, 0] + swap(third[0, 1].astype(bf16), "row", n_row, 2).astype(jnp.float32)
    parts = []
    for k, near_sum in enumerate(sums):
        if k == 2:
            part = third
        else:
            from_far = swap(near_sum[1].astype(bf16), "row", n_row, 2)
            from_far = after(from_far, *(arrivals if k == 0 else () if k == n_req - 1 else ()))
            part = near_sum[0] + from_far.astype(jnp.float32)
            part = col_scatter(part, n_col, arrivals if k == 1 else ())[0][0]
        parts.append(part.astype(bf16) if k else part)
    total = parts[0]
    for s, part in zip(distances[1:], parts[1:]):
        total = total + swap(part, "req", n_req, s).astype(jnp.float32)
    own = (residual[0] + total).astype(bf16)
    others = col_gather(own[None], n_col)
    layer_output = finished(indices, own, others[1:])
    return (layer_output, accepted_latents)


def col_gather(values, n_col):
    bits = 1
    while bits < n_col:
        values = jnp.concatenate([values, swap(values, "col", n_col, bits)], axis=0)
        bits *= 2
    return values


def col_scatter(values, n_col, first=()):
    bits = n_col // 2
    arrived = []
    while bits:
        received = swap(values[bits:].astype(jnp.bfloat16), "col", n_col, bits)
        arrived.append(after(received, *first))
        values = values[:bits] + arrived[-1].astype(jnp.float32)
        bits //= 2
    return values, arrived


def col_parts(values, n_col):
    bits = 1
    while 2 * bits < n_col:
        sent = values.astype(jnp.bfloat16)
        values = sent.astype(jnp.float32) + swap(sent, "col", n_col, bits).astype(jnp.float32)
        bits *= 2
    sent = values.astype(jnp.bfloat16)
    return sent, swap(sent, "col", n_col, bits)[None]


def solution(mesh):
    placed = (
        P(("req", "row"), None),
        P("req", None, None),
        P("req"),
        P("req", None),
        P(("req", "row"), None),
        P(("req", "row")),
        P(),
        P(None, ("row", "col")),
        P(),
        P(),
        P(("row", "col"), None, None),
        P(("row", "col"), None, None),
        P(("row", "col"), None),
        P(),
        P(),
        P(None, None, ("row", "col")),
        P(("row", "col"), None),
        P(("req", "row"), None, None, "col"),
        P(("req", "row"), "col", None),
    )
    sizes = (mesh.shape["req"], mesh.shape["row"], mesh.shape["col"])
    return jax.shard_map(
        functools.partial(body, sizes),
        mesh=mesh,
        in_specs=placed,
        out_specs=(P(("req", "row"), None), P(("req", "row"), None, None)),
        check_vma=False,
    )
```
